128 devices in a mesh: curve: 32 (over y, z, core), split: 4 (over x).
Axes of the slice: x: 4, y: 4, z: 4, core: 2. Of those that a mesh axis runs over, the one named last changes fastest.
Arguments:
- velocity: float32 [3, 1015808], P(None, ('curve', 'split')), may hold values from -6 to 6
- energy: float32 [27, 32768], P(None, ('curve', 'split')), may hold values from 0.1 to 1
- point_mass: float32 [216, 32768], P(None, ('curve', 'split')), may hold values from 0.5 to 2
- inv_jacobian: float32 [1944, 32768], P(None, ('curve', 'split')), may hold values from -6 to 6
- energy_mass_inv: float32 [729, 32768], P(None, ('curve', 'split')), may hold values from -0.2 to 6
- send_rows: int32 [128, 36], P(('curve', 'split')), may hold values from 0 to 255, as said below
- arrive_rows: int32 [128, 36], P(('curve', 'split')), may hold values from 0 to 255, as said below
- zone_nodes: int32 [64, 32768], P(None, ('curve', 'split')), may hold values from 0 to 7935, as said below
- shared_nodes: int32 [128, 4, 256], P(('curve', 'split')), may hold values from 0 to 7935, as said below
Outputs:
- velocity_next: float32 [3, 1015808], P(None, ('curve', 'split'))
- energy_next: float32 [27, 32768], P(None, ('curve', 'split'))
The draws below stay inside these ranges and needn't reach their ends.
Inputs may be any that keep to these rules, and one draw needn't show every extreme that they name: `send_rows`: entry p * 9 + m of a device's row is the local zone row leaving for peer p in slot m; a row's entries are distinct. `arrive_rows`: A device's row holds the same local rows as its row of send_rows, in another order; entry p * 9 + m is where the zone from peer p, slot m, lands. `zone_nodes`: every local node of a device belongs to some zone of that device. `shared_nodes`: the four lists of a device are disjoint with distinct entries; entry m of list 0 of device (c, s) and entry m of list 1 of device (c + 1, s) are one node, likewise list 2 and list 3 of the next device along split.
All inputs are finite; a program needn't handle non-finite values.
Results may differ from the reference program's by a relative error of at most 0.00011.
Values sent between devices are 32-bit elements; how exact they have to be, the bound alone decides.
No kernel may reach another device: no remote copies, remote signals or barrier semaphores. Data moves between devices by JAX's collectives and lax.ppermute only.
A program may use at most 128 MiB of HBM per device.

```python
import math
import jax
import jax.numpy as jnp
import numpy as np
from jax import lax

H1D = 4
Q1D = 6
L1D = 3
SWEEPS = 3
ZONES_DEV = 256
CAP = 9
NPZ = 64
QP = 216
LD = 27
SHARE = 256
NODES_DEV = 7936
ZONES = 32768
NODES = 1015808
N_CURVE = 32
N_SPLIT = 4
DEVICES = 128


def pick_rows(key, extent, needed):
    shuffled = jax.random.permutation(key, extent)
    top_at = jnp.argmax(shuffled == extent - 1)
    shuffled = shuffled.at[top_at].set(shuffled[0]).at[0].set(extent - 1)
    low_at = jnp.argmax(shuffled == 0)
    shuffled = shuffled.at[low_at].set(shuffled[1]).at[1].set(0)
    chosen = shuffled[:needed]
    return chosen[jax.random.permutation(jax.random.fold_in(key, 7), needed)].astype(jnp.int32)


def migration_rows(key):

    def one_device(device_index):
        device_key = jax.random.fold_in(key, device_index)
        leaving = pick_rows(jax.random.fold_in(device_key, 1), ZONES_DEV, 4 * CAP)
        landing = leaving[jax.random.permutation(jax.random.fold_in(device_key, 2), 4 * CAP)]
        return (leaving, landing)
    return jax.vmap(one_device)(jnp.arange(DEVICES))


def draw_send_rows(key, part):
    return migration_rows(jax.random.fold_in(key, 11))[0]


def draw_arrive_rows(key, part):
    return migration_rows(jax.random.fold_in(key, 11))[1]


def draw_zone_nodes(key, part):

    def one_device(device_index):
        device_key = jax.random.fold_in(key, device_index)
        covered = jax.random.permutation(jax.random.fold_in(device_key, 1), NODES_DEV).astype(jnp.int32)
        repeats = jax.random.randint(jax.random.fold_in(device_key, 2), (NPZ * ZONES_DEV - NODES_DEV,), 0, NODES_DEV)
        joined = jnp.concatenate([covered, repeats.astype(jnp.int32)])
        joined = joined[jax.random.permutation(jax.random.fold_in(device_key, 3), NPZ * ZONES_DEV)]
        return joined.reshape(NPZ, ZONES_DEV)
    blocks = jax.vmap(one_device)(jnp.arange(DEVICES))
    return jnp.transpose(blocks, (1, 0, 2)).reshape(NPZ, DEVICES * ZONES_DEV)


def draw_shared_nodes(key, part):

    def one_device(device_index):
        device_key = jax.random.fold_in(jax.random.fold_in(key, 23), device_index)
        return pick_rows(device_key, NODES_DEV, 4 * SHARE).reshape(4, SHARE)
    return jax.vmap(one_device)(jnp.arange(DEVICES))


def draw_energy_mass_inv(key, part):
    shape_all = (LD * LD, ZONES)
    row_index = jnp.arange(LD * LD)
    on_diagonal = row_index // LD == row_index % LD
    diagonal = jax.random.uniform(jax.random.fold_in(key, 1), shape_all, jnp.float32, 2.0, 6.0)
    beside = jnp.clip(0.08 * jax.random.normal(jax.random.fold_in(key, 2), shape_all, jnp.float32), -0.2, 0.2)
    return jnp.where(on_diagonal[:, None], diagonal, beside)


def level_of(rng, shape, cuts, least, high):
    def one(dim, blocks):
        steps = jax.random.uniform(jax.random.fold_in(jax.random.fold_in(rng, 6), dim), (blocks,), jnp.float32, least / len(cuts), high / len(cuts))
        return jnp.repeat(jnp.exp(steps), shape[dim] // blocks).reshape((-1,) + (1,) * (len(shape) - dim - 1))

    gain = one(*cuts[0])
    for cut in cuts[1:]:
        gain = gain * one(*cut)
    return gain


def noise(own_key, shape, spread, limit, shards=(), kind=jnp.bfloat16):
    result = spread * jax.random.normal(own_key, shape, jnp.float32)
    if shards:
        result = result * level_of(own_key, shape, shards, -0.22, 0.18)
    return jnp.clip(result, -limit, limit).astype(kind)


def setup_inputs(seed: int = 0) -> dict:
    splits = jax.random.split(jax.random.key(seed), 10)
    velocity = noise(splits[0], (3, NODES), 1.0, 6.0, ((1, 128),), jnp.float32)
    energy = jnp.clip(jnp.exp(math.log(1.0) - 2.3025851 * jax.random.uniform(splits[1], (LD, ZONES), jnp.float32) ** level_of(splits[1], (LD, ZONES), ((1, 128),), -0.2, 0.2)), 0.1, 1.0)
    point_mass = jnp.clip(jnp.exp(math.log(2.0) - 1.3862944 * jax.random.uniform(splits[2], (QP, ZONES), jnp.float32) ** level_of(splits[2], (QP, ZONES), ((1, 128),), -0.2, 0.2)), 0.5, 2.0)
    inv_jacobian = noise(splits[3], (9 * QP, ZONES), 1.0, 6.0, ((1, 128),), jnp.float32)
    energy_mass_inv = draw_energy_mass_inv(jax.random.fold_in(splits[9], 71), 0)
    send_rows = draw_send_rows(jax.random.fold_in(splits[9], 71), 0)
    arrive_rows = draw_arrive_rows(jax.random.fold_in(splits[9], 71), 0)
    zone_nodes = draw_zone_nodes(jax.random.fold_in(splits[9], 71), 0)
    shared_nodes = draw_shared_nodes(jax.random.fold_in(splits[9], 71), 0)
    return dict(velocity=velocity, energy=energy, point_mass=point_mass, inv_jacobian=inv_jacobian, energy_mass_inv=energy_mass_inv, send_rows=send_rows, arrive_rows=arrive_rows, zone_nodes=zone_nodes, shared_nodes=shared_nodes)


GAMMA_LESS = 0.4
STEP_SIZE = 0.25
LOWER_BOUND = 0.15
UPPER_BOUND = 1.0
HIGH = lax.Precision.HIGHEST


def gauss_points(point_count):
    if point_count == 2:
        on_line = [-0.5773502691896257, 0.5773502691896257]
    elif point_count == 3:
        on_line = [-0.7745966692414834, 0.0, 0.7745966692414834]
    elif point_count == 4:
        on_line = [-0.8611363115940526, -0.3399810435848563, 0.3399810435848563, 0.8611363115940526]
    elif point_count == 5:
        on_line = [-0.9061798459386640, -0.5384693101056831, 0.0, 0.5384693101056831, 0.9061798459386640]
    else:
        on_line = [-0.9324695142031521, -0.6612093864662645, -0.2386191860831909,
                   0.2386191860831909, 0.6612093864662645, 0.9324695142031521]
    return [0.5 * (v + 1.0) for v in on_line]


def lobatto_points(node_count):
    if node_count == 2:
        on_line = [-1.0, 1.0]
    elif node_count == 3:
        on_line = [-1.0, 0.0, 1.0]
    elif node_count == 4:
        on_line = [-1.0, -0.4472135954999579, 0.4472135954999579, 1.0]
    elif node_count == 5:
        on_line = [-1.0, -0.6546536707079771, 0.0, 0.6546536707079771, 1.0]
    else:
        on_line = [-1.0, -0.7650553239294647, -0.2852315164806451,
                   0.2852315164806451, 0.7650553239294647, 1.0]
    return [0.5 * (v + 1.0) for v in on_line]


def basis_tables(nodes_line, points_line, energy_line):
    points = gauss_points(points_line)
    lobatto = lobatto_points(nodes_line)
    value_table = np.zeros((points_line, nodes_line))
    slope_table = np.zeros((points_line, nodes_line))
    for i in range(nodes_line):
        others = [lobatto[j] for j in range(nodes_line) if j != i]
        scaling = np.prod([lobatto[i] - o for o in others])
        for q in range(points_line):
            t = points[q]
            value_table[q, i] = np.prod([t - o for o in others]) / scaling
            summed = 0.0
            for m in range(len(others)):
                summed += np.prod([t - others[n] for n in range(len(others)) if n != m])
            slope_table[q, i] = summed / scaling
    degree = energy_line - 1
    bern_table = np.zeros((points_line, energy_line))
    for q in range(points_line):
        t = points[q]
        for j in range(energy_line):
            bern_table[q, j] = math.comb(degree, j) * t ** j * (1.0 - t) ** (degree - j)
    return value_table, slope_table, bern_table


def tables():
    value_table, slope_table, bern_table = basis_tables(H1D, Q1D, L1D)
    return (jnp.asarray(value_table, jnp.float32), jnp.asarray(slope_table, jnp.float32),
            jnp.asarray(bern_table, jnp.float32))


def apply_along(matrix, tensor, which_axis):
    einsum_forms = ("ai,cijkz->cajkz", "aj,cijkz->ciakz", "ak,cijkz->cijaz")
    return jnp.einsum(einsum_forms[which_axis], matrix, tensor, precision=HIGH)


def through(tensor, matrices):
    return apply_along(matrices[2], apply_along(matrices[1], apply_along(matrices[0], tensor, 0), 1), 2)


def scatter_nodes(terms, connect, node_count):
    return jnp.zeros((terms.shape[0], node_count), jnp.float32).at[:, connect].add(terms)


def zone_force(velocity_nodes, connect, energy_dofs, mass, jacobian):
    value_table, slope_table, bern_table = tables()
    zone_count = connect.shape[1]
    vel_zone = velocity_nodes[:, connect].reshape(3, H1D, H1D, H1D, zone_count)
    energy_points = through(energy_dofs.reshape(1, L1D, L1D, L1D, zone_count), (bern_table, bern_table, bern_table))[0]
    pressure_weight = GAMMA_LESS * energy_points * mass.reshape(Q1D, Q1D, Q1D, zone_count)
    stress_flux = jacobian.reshape(3, 3, Q1D, Q1D, Q1D, zone_count) * pressure_weight
    value_t = value_table.T
    slope_t = slope_table.T
    rhs_zone = (through(stress_flux[0], (slope_t, value_t, value_t))
                + through(stress_flux[1], (value_t, slope_t, value_t))
                + through(stress_flux[2], (value_t, value_t, slope_t)))
    first_b = apply_along(value_table, vel_zone, 0)
    first_g = apply_along(slope_table, vel_zone, 0)
    grad_x = apply_along(value_table, apply_along(value_table, first_g, 1), 2)
    grad_y = apply_along(value_table, apply_along(slope_table, first_b, 1), 2)
    grad_z = apply_along(slope_table, apply_along(value_table, first_b, 1), 2)
    work_density = jnp.sum(stress_flux[0] * grad_x + stress_flux[1] * grad_y + stress_flux[2] * grad_z, axis=0)
    bern_t = bern_table.T
    rhs_energy = -through(work_density[None], (bern_t, bern_t, bern_t)).reshape(L1D ** 3, zone_count)
    rhs_nodes = scatter_nodes(rhs_zone.reshape(3, H1D ** 3, zone_count), connect, velocity_nodes.shape[1])
    return rhs_nodes, rhs_energy


def zone_mass(direction_nodes, connect, mass):
    value_table, slope_table, bern_table = tables()
    zone_count = connect.shape[1]
    dir_zone = direction_nodes[:, connect].reshape(3, H1D, H1D, H1D, zone_count)
    at_points = through(dir_zone, (value_table, value_table, value_table))
    weighted = at_points * mass.reshape(Q1D, Q1D, Q1D, zone_count)
    value_t = value_table.T
    back = through(weighted, (value_t, value_t, value_t))
    return scatter_nodes(back.reshape(3, H1D ** 3, zone_count), connect, direction_nodes.shape[1])


def bound_term(connect, mass, node_count):
    value_table, slope_table, bern_table = tables()
    zone_count = connect.shape[1]
    abs_table = jnp.abs(value_table)
    row_total = jnp.sum(abs_table, axis=1)
    point_weight = row_total[:, None, None] * row_total[None, :, None] * row_total[None, None, :]
    weighted = (mass.reshape(Q1D, Q1D, Q1D, zone_count) * point_weight[:, :, :, None])[None]
    abs_t = abs_table.T
    term = through(weighted, (abs_t, abs_t, abs_t))
    return scatter_nodes(term.reshape(1, H1D ** 3, zone_count), connect, node_count)


def apply_inverse(inverse, rhs_energy):
    return jnp.einsum("jlz,lz->jz", inverse.reshape(L1D ** 3, L1D ** 3, inverse.shape[1]), rhs_energy, precision=HIGH)


def chebyshev(rhs_nodes, bound, apply_mass):
    theta = 0.5 * (UPPER_BOUND + LOWER_BOUND)
    delta = 0.5 * (UPPER_BOUND - LOWER_BOUND)
    sigma = theta / delta
    rho_now = 1.0 / sigma
    residual = rhs_nodes
    direction = residual / bound / theta
    solution = jnp.zeros_like(rhs_nodes)
    for sweep in range(SWEEPS):
        solution = solution + direction
        residual = residual - apply_mass(direction)
        rho_new = 1.0 / (2.0 * sigma - rho_now)
        direction = rho_new * rho_now * direction + (2.0 * rho_new / delta) * (residual / bound)
        rho_now = rho_new
    return solution + direction


def reference(velocity, energy, point_mass, inv_jacobian, energy_mass_inv, send_rows, arrive_rows, zone_nodes, shared_nodes):
    devices = N_CURVE * N_SPLIT
    zone_count = point_mass.shape[1] // devices
    node_count = velocity.shape[1] // devices
    slots = 4 * CAP
    column = jnp.arange(slots, dtype=jnp.int32)
    offsets = jnp.array([1, -1, 2, -2], dtype=jnp.int32)
    peer_offset = offsets[(column // CAP).astype(jnp.int32)]
    target = jnp.arange(devices, dtype=jnp.int32)
    source = (target[:, None] - peer_offset[None, :]).astype(jnp.int32)
    valid = (source >= 0) & (source < devices)
    source_safe = jnp.clip(source, 0, devices - 1).astype(jnp.int32)
    from_rows = send_rows[source_safe, jnp.broadcast_to(column[None, :], source_safe.shape)]

    def migrate(field_rows):
        blocks = field_rows.reshape(field_rows.shape[0], devices, zone_count)
        parcels = blocks[:, source_safe, from_rows]
        current = blocks[:, jnp.broadcast_to(target[:, None], arrive_rows.shape), arrive_rows]
        placed = jnp.where(valid[None], parcels, current)
        blocks = blocks.at[:, jnp.broadcast_to(target[:, None], arrive_rows.shape), arrive_rows].set(placed)
        return jnp.transpose(blocks, (1, 0, 2))

    mass = migrate(point_mass)
    jacobian = migrate(inv_jacobian)
    inverse = migrate(energy_mass_inv)
    energy_now = migrate(energy)
    vel = jnp.transpose(velocity.reshape(3, devices, node_count), (1, 0, 2))
    connect = jnp.transpose(zone_nodes.reshape(zone_nodes.shape[0], devices, zone_count), (1, 0, 2))
    lists = shared_nodes

    def assemble(values):
        picked = jax.vmap(lambda y, l: y[:, l])(values, lists)
        grid = picked.reshape((N_CURVE, N_SPLIT) + picked.shape[1:])
        blank_curve = jnp.zeros_like(grid[:1])
        blank_split = jnp.zeros_like(grid[:, :1])
        prev_curve = jnp.concatenate([blank_curve, grid[:-1]], 0)
        next_curve = jnp.concatenate([grid[1:], blank_curve], 0)
        prev_split = jnp.concatenate([blank_split, grid[:, :-1]], 1)
        next_split = jnp.concatenate([grid[:, 1:], blank_split], 1)
        incoming = jnp.stack([next_curve[:, :, :, 1], prev_curve[:, :, :, 0],
                              next_split[:, :, :, 3], prev_split[:, :, :, 2]], 3)
        incoming = incoming.reshape((devices,) + incoming.shape[2:])
        return jax.vmap(lambda y, l, v: y.at[:, l].add(v))(values, lists, incoming)

    bound = assemble(lax.map(lambda a: bound_term(a[0], a[1], node_count), (connect, mass)))

    def apply_mass(direction):
        return assemble(lax.map(lambda a: zone_mass(a[0], a[1], a[2]), (direction, connect, mass)))

    def evaluate(vel_now, energy_in):
        rhs_nodes, rhs_energy = lax.map(lambda a: zone_force(a[0], a[1], a[2], a[3], a[4]),
                                        (vel_now, connect, energy_in, mass, jacobian))
        accel = chebyshev(assemble(rhs_nodes), bound, apply_mass)
        change = jax.vmap(apply_inverse)(inverse, rhs_energy)
        return accel, change

    accel_one, change_one = evaluate(vel, energy_now)
    vel_half = vel + 0.5 * STEP_SIZE * accel_one
    energy_half = energy_now + 0.5 * STEP_SIZE * change_one
    accel_two, change_two = evaluate(vel_half, energy_half)
    vel_next = vel + STEP_SIZE * accel_two
    energy_next = energy_now + STEP_SIZE * change_two
    velocity_next = jnp.transpose(vel_next, (1, 0, 2)).reshape(3, devices * node_count)
    energy_out = jnp.transpose(energy_next, (1, 0, 2)).reshape(energy_next.shape[1], devices * zone_count)
    return velocity_next, energy_out
```

```python
import functools
import math

import jax
import jax.numpy as jnp
import numpy as np
from jax import lax
from jax.experimental import pallas as pl
from jax.experimental.pallas import tpu as pltpu
from jax.sharding import PartitionSpec as P

H1D, Q1D, L1D, SWEEPS = 4, 6, 3, 3
NPZ, QP, LD = 64, 216, 27
GAMMA_LESS = 0.4
STEP_SIZE = 0.25
THETA, DELTA = 0.575, 0.425
SIGMA = THETA / DELTA
AXES = ("curve", "split")
CAP = 9
HALF = 128
WIDE = 256
ROWS = 32
AT_JAC, AT_MASS, AT_INV, AT_EN, AT_FLAG, MSG = 0, 2048, 2304, 3072, 3100, 3200
TAIL = 512
BF, F32 = jnp.bfloat16, jnp.float32
NT = (((1,), (1,)), ((), ()))
TN = (((0,), (0,)), ((), ()))


def line_tables():
    on_line = [-0.9324695142031521, -0.6612093864662645, -0.2386191860831909]
    on_line = on_line + [-v for v in reversed(on_line)]
    points = [0.5 * (v + 1.0) for v in on_line]
    lobatto = [0.5 * (v + 1.0) for v in [-1.0, -0.4472135954999579, 0.4472135954999579, 1.0]]
    value, slope, bern = np.zeros((Q1D, H1D)), np.zeros((Q1D, H1D)), np.zeros((Q1D, L1D))
    for i in range(H1D):
        others = [lobatto[j] for j in range(H1D) if j != i]
        scaling = np.prod([lobatto[i] - o for o in others])
        for q, t in enumerate(points):
            value[q, i] = np.prod([t - o for o in others]) / scaling
            slope[q, i] = sum(
                np.prod([t - others[n] for n in range(3) if n != m]) for m in range(3)
            ) / scaling
    for q, t in enumerate(points):
        for j in range(L1D):
            bern[q, j] = math.comb(2, j) * t**j * (1.0 - t) ** (2 - j)
    return [np.float32(t).astype(np.float64) for t in (value, slope, bern)]


def halves(table):
    high = table.astype(np.float32).astype(BF)
    low = (table - high.astype(np.float64)).astype(np.float32).astype(BF)
    return high, low


def beside(table):
    high, low = halves(table)
    return np.concatenate([high, high, low], 1)


def above(table):
    return np.concatenate(halves(table), 0)


def constants():
    b, g, p = line_tables()
    kron = lambda x, y, z: np.kron(np.kron(x, y), z)
    bbb, ppp = kron(b, b, b), kron(p, p, p)
    grads = [kron(g, b, b), kron(b, g, b), kron(b, b, g)]
    r = np.abs(b).sum(1, keepdims=True)
    limit = kron(np.abs(b), np.abs(b), np.abs(b)) * kron(r, r, r)
    spread = np.kron(np.ones((LD, 1)), np.eye(LD))
    gather = np.kron(np.eye(LD), np.ones((1, LD)))
    return dict(
        mass_up=beside(bbb),
        mass_down=above(bbb.T),
        grad_up=np.concatenate([beside(t) for t in grads], 0),
        grad_down=np.stack([above(t.T) for t in grads], 0),
        limit=above(limit.T),
        bern_up=np.stack(halves(ppp), 0),
        bern_down=np.stack(halves(ppp.T), 0),
        spread=spread.astype(BF),
        gather=gather.astype(BF),
    )


def split2(x):
    high = x.astype(BF)
    return high, (x - high.astype(F32)).astype(BF)


def split3(x):
    high = x.astype(BF)
    rest = x - high.astype(F32)
    mid = rest.astype(BF)
    return high, mid, (rest - mid.astype(F32)).astype(BF)


def dot(a, b, dims=None):
    if dims is None:
        return jnp.dot(a, b, preferred_element_type=F32)
    return lax.dot_general(a, b, dims, preferred_element_type=F32)


def up(table, x):
    high, low = split2(x)
    return dot(table[...], jnp.concatenate([high, low, high], 0))


def down(table, x):
    high, low = split2(x)
    table = table[...]
    half = table.shape[0] // 2
    both = dot(table, high)
    return both[:half] + both[half:] + dot(table[:half], low)


def pick(tables, chunk_of, lane_of, shape):
    acc = [jnp.zeros(shape, F32) for _ in tables]
    for k in range(62):
        here = chunk_of == k
        for c, row in enumerate(tables):
            got = jnp.take_along_axis(jnp.broadcast_to(row(k), shape), lane_of, axis=1)
            acc[c] = jnp.where(here, got, acc[c])
    return acc


def table_rows(ref, count):
    def row(c, k):
        return ref[c * ROWS + k // 2 : c * ROWS + k // 2 + 1, (k % 2) * HALF : (k % 2 + 1) * HALF]

    return [functools.partial(row, c) for c in range(count)]


def gather_zones(idx_ref, tab_ref, out_ref):
    @pl.loop(0, 8)
    def _(t):
        r0 = pl.multiple_of(t * 8, 8)
        for h in range(2):
            lanes = slice(h * HALF, (h + 1) * HALF)
            idx = idx_ref[pl.ds(r0, 8), lanes]
            got = pick(table_rows(tab_ref, 3), idx >> 7, idx & 127, (8, HALF))
            for c in range(3):
                out_ref[c, pl.ds(r0, 8), lanes] = got[c]


def scatter_tile(acc, idx, rows):
    lane = jnp.where(
        lax.broadcasted_iota(jnp.int32, (WIDE, WIDE), 0) == (idx & 255), 1.0, 0.0
    ).astype(BF)
    here = lax.broadcasted_iota(jnp.int32, (ROWS, WIDE), 0) == (idx >> 8)
    parts = []
    for x in rows:
        high = x.astype(BF).astype(F32)
        for part in (high, x - high):
            parts.append(jnp.where(here, part, 0.0).astype(BF))
    return acc + dot(jnp.concatenate(parts, 0), lane, NT)


def joined(acc):
    acc = acc.reshape(acc.shape[0] // (2 * ROWS), 2, ROWS, WIDE)
    return (acc[:, 0] + acc[:, 1]).reshape(-1, WIDE)


def scatter_zones(idx_ref, term_ref, count):
    def eight(t, acc):
        r0 = pl.multiple_of(t * 8, 8)
        idx = idx_ref[pl.ds(r0, 8), :]
        terms = [term_ref[c, pl.ds(r0, 8), :] for c in range(count)]
        for a in range(8):
            acc = scatter_tile(acc, idx[a : a + 1], [x[a : a + 1] for x in terms])
        return acc

    return joined(lax.fori_loop(0, 8, eight, jnp.zeros((2 * ROWS * count, WIDE), F32)))


def flat_row(ref, first):
    return jnp.concatenate([ref[first : first + 1, :], ref[first + 1 : first + 2, :]], 1)


def received(lists_ref, got_refs, count):
    acc = jnp.zeros((2 * ROWS * count, WIDE), F32)
    for k, got in enumerate(got_refs):
        acc = scatter_tile(acc, flat_row(lists_ref, 2 * k), [flat_row(got, 2 * c) for c in range(count)])
    return joined(acc)


def send_shared(lists_ref, tab_ref, send_refs, count):
    idx = lists_ref[...]
    got = pick(table_rows(tab_ref, count), idx >> 7, idx & 127, (8, HALF))
    for k, send in enumerate(send_refs):
        send[...] = jnp.concatenate(
            [got[min(c, count - 1)][2 * k : 2 * k + 2] for c in range(4)], 0
        )


def force(v_ref, en, jac_ref, mass, t_ref, work_ref, cst):
    bu = cst["bern_up"]
    eh, el = split2(en)
    e_q = dot(bu[0], eh) + dot(bu[0], el) + dot(bu[1], eh)
    pressure = GAMMA_LESS * e_q * mass
    for c in range(3):
        high, low = split2(v_ref[c])
        vc = jnp.concatenate([high, low, high], 0)
        term = jnp.zeros((NPZ, WIDE), F32)
        for k in range(3):
            w = jac_ref[(3 * k + c) * QP : (3 * k + c + 1) * QP, :] * pressure
            dv = dot(cst["grad_up"][k * QP : (k + 1) * QP, :], vc)
            if c == 0 and k == 0:
                work_ref[...] = w * dv
            else:
                work_ref[...] += w * dv
            term = term + down(cst["grad_down"][k], w)
        t_ref[c] = term
    wh, wl = split2(work_ref[...])
    bd = cst["bern_down"]
    return -(dot(bd[0], wh) + dot(bd[0], wl) + dot(bd[1], wh))


def energy_change(rhs_e, inv, cst):
    rh, rl = split2(rhs_e)
    prod = inv * (dot(cst["spread"][...], rh) + dot(cst["spread"][...], rl))
    ph, pl_ = split2(prod)
    return dot(cst["gather"][...], ph) + dot(cst["gather"][...], pl_)


def nodes_in(vel_ref, tab_ref):
    for c in range(3):
        for r in range(31):
            tab_ref[c * ROWS + r : c * ROWS + r + 1, :] = vel_ref[c : c + 1, r * WIDE : (r + 1) * WIDE]
        tab_ref[c * ROWS + 31 : (c + 1) * ROWS, :] = jnp.zeros((1, WIDE), F32)


def pack_kernel(send_ref, jac_ref, mass_ref, inv_ref, en_ref, *refs):
    msgs, (oh,) = refs[:4], refs[4:]
    lane = lax.broadcasted_iota(jnp.int32, (1, WIDE), 1)
    for m in range(4 * CAP):
        p, j = divmod(m, CAP)
        at = p * 8 + j if j < 8 else 32 + p
        oh[at : at + 1, :] = jnp.where(lane == send_ref[0, m], 1.0, 0.0)
    oh[36:40, :] = jnp.zeros((4, WIDE), F32)
    hot = oh[...].astype(BF)

    def put(at, n, block):
        for p in range(4):
            msgs[p][:, at : at + n] = block[p * 8 : (p + 1) * 8]
            done = 0
            while done < n:
                piece, off = divmod(at + done, TAIL)
                step = min(n - done, TAIL - off)
                msgs[p][piece : piece + 1, MSG + off : MSG + off + step] = block[
                    32 + p : 33 + p, done : done + step
                ]
                done += step

    for ref, at in ((jac_ref, AT_JAC), (mass_ref, AT_MASS), (inv_ref, AT_INV), (en_ref, AT_EN)):
        total = ref.shape[0]
        for i in range(0, total, WIDE):
            n = min(WIDE, total - i)
            parts = split3(ref[i : i + n, :])
            put(at + i, n, sum(dot(hot, part, NT) for part in parts))
    for p in range(4):
        msgs[p][:, AT_FLAG:MSG] = jnp.ones((8, MSG - AT_FLAG), F32)


def first_kernel(
    arrive_ref, m0, m1, m2, m3, jac_ref, mass_ref, inv_ref, en_ref, vel_ref, zn_ref, lists_ref,
    limit, grad_up, grad_down, bern_up, bern_down, spread, gather,
    jac_out, mass_out, inv_out, en_out, vel_out, ehalf_out, y_out, s0, s1, s2, s3,
    oh, arr, vz, terms, work,
):
    cst = dict(grad_up=grad_up, grad_down=grad_down, bern_up=bern_up, bern_down=bern_down,
               spread=spread, gather=gather)
    msgs = (m0, m1, m2, m3)
    lane = lax.broadcasted_iota(jnp.int32, (1, WIDE), 1)
    oh[...] = jnp.zeros(oh.shape, F32)
    for m in range(4 * CAP):
        p, j = divmod(m, CAP)
        at = p * 8 + j if j < 8 else 32 + p
        flag = msgs[p][0:1, AT_FLAG : AT_FLAG + 1]
        oh[at : at + 1, :] = jnp.where(lane == arrive_ref[0, m], 1.0, 0.0) * flag
    lands = jnp.sum(oh[...], axis=0, keepdims=True) > 0.5
    hot = oh[...].astype(BF)
    hot3 = jnp.concatenate([hot, hot, hot], 0)
    for p in range(4):
        arr[p * 8 : (p + 1) * 8, :] = msgs[p][:, :MSG]
        for piece in range(7):
            n = min(TAIL, MSG - piece * TAIL)
            arr[32 + p : 33 + p, piece * TAIL : piece * TAIL + n] = msgs[p][
                piece : piece + 1, MSG : MSG + n
            ]
    arr[36:48, :] = jnp.zeros((12, MSG), F32)
    for ref, out, at in (
        (jac_ref, jac_out, AT_JAC), (mass_ref, mass_out, AT_MASS),
        (inv_ref, inv_out, AT_INV), (en_ref, en_out, AT_EN),
    ):
        total = ref.shape[0]
        for i in range(0, total, WIDE):
            n = min(WIDE, total - i)
            wide = min(WIDE, -(-n // HALF) * HALF)
            came = jnp.concatenate(split3(arr[:, at + i : at + i + wide]), 0)
            out[i : i + n, :] = jnp.where(lands, dot(came, hot3, TN)[:n], ref[i : i + n, :])
    nodes_in(vel_ref, vel_out)
    gather_zones(zn_ref, vel_out, vz)
    mass = mass_out[...]
    rhs_e = force(vz, en_out[...], jac_out, mass, terms, work, cst)
    terms[3] = down(limit, mass)
    ehalf_out[...] = en_out[...] + 0.5 * STEP_SIZE * energy_change(rhs_e, inv_out[...], cst)
    y_out[...] = scatter_zones(zn_ref, terms, 4)
    send_shared(lists_ref, y_out, (s0, s1, s2, s3), 4)


def rhos():
    rho, out = 1.0 / SIGMA, []
    for _ in range(SWEEPS):
        new = 1.0 / (2.0 * SIGMA - rho)
        out.append((new * rho, 2.0 * new / DELTA))
        rho = new
    return out


def three(x):
    return jnp.concatenate([x, x, x], 0)


def update(y, r_ref, d_ref, a_ref, ib_ref, step):
    keep, add = rhos()[step]
    r = r_ref[...] - y
    d = keep * d_ref[...] + add * (r * three(ib_ref[...]))
    return r, d, a_ref[...] + d


def apply_mass(zn_ref, mass_ref, mass_up, mass_down, d_ref, y_out, zone, terms):
    gather_zones(zn_ref, d_ref, zone)
    mass = mass_ref[...]
    for c in range(3):
        terms[c] = down(mass_down, up(mass_up[...], zone[c]) * mass)
    y_out[...] = scatter_zones(zn_ref, terms, 3)


def start_kernel(
    g0, g1, g2, g3, y_ref, *refs, first
):
    if first:
        lists, zn, mass, up_ref, down_ref = refs[:5]
        ib, r_out, d_out, y_out, s0, s1, s2, s3, zone, terms = refs[5:]
        y = y_ref[...] + received(lists, (g0, g1, g2, g3), 4)
        pad = lax.broadcasted_iota(jnp.int32, (ROWS, WIDE), 0) == 31
        inv_bound = 1.0 / jnp.where(pad, 1.0, y[96:])
        ib[...] = inv_bound
        r = y[:96]
    else:
        ib, lists, zn, mass, up_ref, down_ref = refs[:6]
        r_out, d_out, y_out, s0, s1, s2, s3, zone, terms = refs[6:]
        r = y_ref[...] + received(lists, (g0, g1, g2, g3), 3)
        inv_bound = ib[...]
    r_out[...] = r
    d_out[...] = r * three(inv_bound) * (1.0 / THETA)
    apply_mass(zn, mass, up_ref, down_ref, d_out, y_out, zone, terms)
    send_shared(lists, y_out, (s0, s1, s2, s3), 3)


def sweep_kernel(
    g0, g1, g2, g3, y_ref, r_ref, d_ref, a_ref, ib_ref, lists, zn, mass, mass_up, mass_down,
    r_out, d_out, a_out, y_out, s0, s1, s2, s3, zone, terms, *, step,
):
    y = y_ref[...] + received(lists, (g0, g1, g2, g3), 3)
    r, d, a = update(y, r_ref, d_ref, a_ref, ib_ref, step)
    r_out[...] = r
    d_out[...] = d
    a_out[...] = a
    apply_mass(zn, mass, mass_up, mass_down, d_out, y_out, zone, terms)
    send_shared(lists, y_out, (s0, s1, s2, s3), 3)


def second_kernel(
    g0, g1, g2, g3, y_ref, r_ref, d_ref, a_ref, ib_ref, lists, zn, mass, jac, inv, en, ehalf, vel,
    grad_up, grad_down, bern_up, bern_down, spread, gather,
    en_out, y_out, s0, s1, s2, s3, vhalf, vz, terms, work,
):
    cst = dict(grad_up=grad_up, grad_down=grad_down, bern_up=bern_up, bern_down=bern_down,
               spread=spread, gather=gather)
    y = y_ref[...] + received(lists, (g0, g1, g2, g3), 3)
    _, _, a = update(y, r_ref, d_ref, a_ref, ib_ref, SWEEPS - 1)
    vhalf[...] = vel[...] + 0.5 * STEP_SIZE * a
    gather_zones(zn, vhalf, vz)
    rhs_e = force(vz, ehalf[...], jac, mass[...], terms, work, cst)
    y_out[...] = scatter_zones(zn, terms, 3)
    send_shared(lists, y_out, (s0, s1, s2, s3), 3)
    en_out[...] = en[...] + STEP_SIZE * energy_change(rhs_e, inv[...], cst)


def last_kernel(g0, g1, g2, g3, y_ref, r_ref, d_ref, a_ref, ib_ref, lists, vel, out):
    y = y_ref[...] + received(lists, (g0, g1, g2, g3), 3)
    _, _, a = update(y, r_ref, d_ref, a_ref, ib_ref, SWEEPS - 1)
    v = vel[...] + STEP_SIZE * a
    for c in range(3):
        for r in range(31):
            out[c : c + 1, r * WIDE : (r + 1) * WIDE] = v[c * ROWS + r : c * ROWS + r + 1]


VM = pl.BlockSpec(memory_space=pltpu.VMEM)
SM = pl.BlockSpec(memory_space=pltpu.SMEM)


def call(kernel, args, outs, scratch=(), scalars=0, limit=24, name=None):
    shapes = [jax.ShapeDtypeStruct(s, F32) for s in outs]
    return pl.pallas_call(
        kernel,
        out_shape=shapes,
        in_specs=[SM] * scalars + [VM] * (len(args) - scalars),
        out_specs=[VM] * len(outs),
        scratch_shapes=[pltpu.VMEM(s, F32) for s in scratch],
        compiler_params=pltpu.CompilerParams(vmem_limit_bytes=limit * 1024 * 1024),
        name=name,
    )(*args)


def paired(first, size):
    return [p for i in range(first, size - 1, 2) for p in ((i, i + 1), (i + 1, i))]


def exchange(sends):
    n_curve, n_split = lax.axis_size("curve"), lax.axis_size("split")
    return [
        lax.ppermute(sends[0], "curve", paired(0, n_curve)),
        lax.ppermute(sends[1], "curve", paired(1, n_curve)),
        lax.ppermute(sends[2], "split", paired(0, n_split)),
        lax.ppermute(sends[3], "split", paired(1, n_split)),
    ]


def per_device(velocity, energy, mass, jac, inv, send_rows, arrive_rows, zone_nodes, shared_nodes):
    cst = {k: jnp.asarray(v) for k, v in constants().items()}
    n_curve, n_split = lax.axis_size("curve"), lax.axis_size("split")
    devices = n_curve * n_split
    lists = shared_nodes[0].reshape(4, 2, HALF)
    odd_c, odd_s = lax.axis_index("curve") % 2 == 1, lax.axis_index("split") % 2 == 1
    swap = lambda odd, x: jnp.where(odd, x[::-1], x)
    lists = jnp.concatenate([swap(odd_c, lists[:2]), swap(odd_s, lists[2:])], 0).reshape(8, HALF)

    zones, node, msg = (WIDE,), (96, WIDE), (8, MSG + TAIL)
    send = [(8, HALF)] * 4
    zscr = [(3, NPZ, WIDE), (3, NPZ, WIDE)]
    msgs = call(pack_kernel, (send_rows, jac, mass, inv, energy), [msg] * 4, [(40, WIDE)], 1, name="pack")
    came = []
    for p, off in enumerate((1, -1, 2, -2)):
        pairs = [(i, i + off) for i in range(devices) if 0 <= i + off < devices]
        came.append(lax.ppermute(msgs[p], AXES, pairs))
    fc = [cst[k] for k in ("grad_up", "grad_down", "bern_up", "bern_down", "spread", "gather")]
    mc = [cst["mass_up"], cst["mass_down"]]
    jac, mass, inv, en, vel, ehalf, y, *sends = call(
        first_kernel,
        (arrive_rows, *came, jac, mass, inv, energy, velocity, zone_nodes, lists,
         cst["limit"], *fc),
        [(9 * QP,) + zones, (QP,) + zones, (LD * LD,) + zones, (LD,) + zones, node, (LD,) + zones,
         (128, WIDE)] + send,
        [(48, WIDE), (48, MSG), (3, NPZ, WIDE), (4, NPZ, WIDE), (QP, WIDE)],
        1, limit=32, name="force_one",
    )
    ib = None
    for section in range(2):
        got = exchange(sends)
        outs = [node, node, node] + send
        tail = (lists, zone_nodes, mass, *mc)
        if section == 0:
            ib, r, d, y, *sends = call(
                functools.partial(start_kernel, first=True), (*got, y, *tail),
                [(ROWS, WIDE)] + outs, zscr, name="mass_start",
            )
        else:
            r, d, y, *sends = call(
                functools.partial(start_kernel, first=False), (*got, y, ib, *tail), outs, zscr,
                name="mass_start_two",
            )
        a = d
        for step in range(SWEEPS - 1):
            got = exchange(sends)
            r, d, a, y, *sends = call(
                functools.partial(sweep_kernel, step=step), (*got, y, r, d, a, ib, *tail),
                [node] + outs, zscr, name="mass_sweep",
            )
        got = exchange(sends)
        if section == 0:
            energy_next, y, *sends = call(
                second_kernel,
                (*got, y, r, d, a, ib, lists, zone_nodes, mass, jac, inv, en, ehalf, vel, *fc),
                [(LD,) + zones, node] + send,
                [node, (3, NPZ, WIDE), (3, NPZ, WIDE), (QP, WIDE)], limit=32, name="force_two",
            )
        else:
            (velocity_next,) = call(
                last_kernel, (*got, y, r, d, a, ib, lists, vel), [velocity.shape], name="finish"
            )
    return velocity_next, energy_next


def solution(mesh):
    both = P(None, AXES)
    rows = P(AXES, None)
    return jax.shard_map(
        per_device,
        mesh=mesh,
        in_specs=(both, both, both, both, both, rows, rows, both, P(AXES, None, None)),
        out_specs=(both, both),
        check_vma=False,
    )
```

```python
import functools
import math

import jax
import jax.numpy as jnp
import numpy as np
from jax import lax
from jax.experimental import pallas as pl
from jax.experimental.pallas import tpu as pltpu
from jax.sharding import PartitionSpec as P

H1D, Q1D, L1D, SWEEPS = 4, 6, 3, 3
NPZ, QP, LD = 64, 216, 27
GAMMA_LESS = 0.4
STEP_SIZE = 0.25
THETA, DELTA = 0.575, 0.425
SIGMA = THETA / DELTA
AXES = ("curve", "split")
CAP = 9
HALF = 128
WIDE = 256
ROWS = 32
AT_JAC, AT_MASS, AT_INV, AT_EN, AT_FLAG, MSG = 0, 2048, 2304, 3072, 3100, 3200
TAIL = 512
BF, F32 = jnp.bfloat16, jnp.float32
NT = (((1,), (1,)), ((), ()))
TN = (((0,), (0,)), ((), ()))


def line_tables():
    on_line = [-0.9324695142031521, -0.6612093864662645, -0.2386191860831909]
    on_line = on_line + [-v for v in reversed(on_line)]
    points = [0.5 * (v + 1.0) for v in on_line]
    lobatto = [0.5 * (v + 1.0) for v in [-1.0, -0.4472135954999579, 0.4472135954999579, 1.0]]
    value, slope, bern = np.zeros((Q1D, H1D)), np.zeros((Q1D, H1D)), np.zeros((Q1D, L1D))
    for i in range(H1D):
        others = [lobatto[j] for j in range(H1D) if j != i]
        scaling = np.prod([lobatto[i] - o for o in others])
        for q, t in enumerate(points):
            value[q, i] = np.prod([t - o for o in others]) / scaling
            slope[q, i] = sum(
                np.prod([t - others[n] for n in range(3) if n != m]) for m in range(3)
            ) / scaling
    for q, t in enumerate(points):
        for j in range(L1D):
            bern[q, j] = math.comb(2, j) * t**j * (1.0 - t) ** (2 - j)
    return [np.float32(t).astype(np.float64) for t in (value, slope, bern)]


def halves(table):
    high = table.astype(np.float32).astype(BF)
    low = (table - high.astype(np.float64)).astype(np.float32).astype(BF)
    return high, low


def beside(table):
    high, low = halves(table)
    return np.concatenate([high, high, low], 1)


def above(table):
    return np.concatenate(halves(table), 0)


def stacked(tables):
    places, blocks, at = {}, [], 0
    for name, table in tables.items():
        rows, columns = table.shape
        places[name] = (at, rows, columns)
        room = -(-rows // 16) * 16
        block = np.zeros((room, WIDE), BF)
        block[:rows, :columns] = table
        blocks.append(block)
        at += room
    return np.concatenate(blocks, 0), places


def constants():
    b, g, p = line_tables()
    kron = lambda x, y, z: np.kron(np.kron(x, y), z)
    bbb, ppp = kron(b, b, b), kron(p, p, p)
    grads = [kron(g, b, b), kron(b, g, b), kron(b, b, g)]
    r = np.abs(b).sum(1, keepdims=True)
    limit = kron(np.abs(b), np.abs(b), np.abs(b)) * kron(r, r, r)
    spread = np.kron(np.ones((LD, 1)), np.eye(LD)).astype(BF)
    collect = np.kron(np.eye(LD), np.ones((1, LD))).astype(BF)
    force = dict(
        bern_up_high=halves(ppp)[0],
        bern_up_low=halves(ppp)[1],
        bern_down_high=halves(ppp.T)[0],
        bern_down_low=halves(ppp.T)[1],
        spread=spread,
        limit=above(limit.T),
    )
    for k, t in enumerate(grads):
        force["up%d" % k] = beside(t)
        force["down%d" % k] = above(t.T)
    for k in range(0, LD * LD, 243):
        force["collect%d" % k] = collect[:, k : k + 243]
    return stacked(force), stacked(dict(up=beside(bbb), down=above(bbb.T)))


(FORCE_TABLES, FORCE_AT), (MASS_TABLES, MASS_AT) = constants()


def entry(ref, places, name):
    at, rows, columns = places[name]
    return ref[at : at + rows, :columns]


def split2(x):
    high = x.astype(BF)
    return high, (x - high.astype(F32)).astype(BF)


def split3(x):
    high = x.astype(BF)
    rest = x - high.astype(F32)
    mid = rest.astype(BF)
    return high, mid, (rest - mid.astype(F32)).astype(BF)


def dot(a, b, dims=None):
    if dims is None:
        return jnp.dot(a, b, preferred_element_type=F32)
    return lax.dot_general(a, b, dims, preferred_element_type=F32)


def up(table, x):
    high, low = split2(x)
    return dot(table, jnp.concatenate([high, low, high], 0))


def down(table, x):
    high, low = split2(x)
    half = table.shape[0] // 2
    both = dot(table, high)
    return both[:half] + both[half:] + dot(table[:half], low)


def pick(tables, chunk_of, lane_of, shape, kind=F32):
    acc = [jnp.zeros(shape, kind) for _ in tables]
    for k in range(62):
        here = chunk_of == k
        for c, row in enumerate(tables):
            got = jnp.take_along_axis(jnp.broadcast_to(row(k), shape), lane_of, axis=1)
            acc[c] = jnp.where(here, got, acc[c])
    return acc


def table_rows(ref, count):
    def row(c, k):
        return ref[c * ROWS + k // 2 : c * ROWS + k // 2 + 1, (k % 2) * HALF : (k % 2 + 1) * HALF]

    return [functools.partial(row, c) for c in range(count)]


def gather_zones(idx_ref, tab_ref, word_ref, out_ref):
    x = tab_ref[...]
    scale = jnp.max(jnp.abs(x), keepdims=True)
    per_unit = 1000000.0 / jnp.maximum(scale, 1e-30)
    step = jnp.maximum(scale, 1e-30) * 1e-6
    q = jnp.round(x * per_unit).astype(jnp.int32) + (1 << 20)
    word_ref[:ROWS] = (q[:ROWS] << 11) | (q[2 * ROWS :] >> 10)
    word_ref[ROWS:] = (q[ROWS : 2 * ROWS] << 11) | (q[2 * ROWS :] & 1023)

    @pl.loop(0, 8)
    def _(t):
        r0 = pl.multiple_of(t * 8, 8)
        for h in range(2):
            lanes = slice(h * HALF, (h + 1) * HALF)
            idx = idx_ref[pl.ds(r0, 8), lanes]
            w0, w1 = pick(table_rows(word_ref, 2), idx >> 7, idx & 127, (8, HALF), jnp.int32)
            back = (
                lax.shift_right_logical(w0, 11),
                lax.shift_right_logical(w1, 11),
                ((w0 & 2047) << 10) | (w1 & 1023),
            )
            for c in range(3):
                out_ref[c, pl.ds(r0, 8), lanes] = (back[c] - (1 << 20)).astype(F32) * step


def scatter_tile(acc, idx, rows):
    lane = jnp.where(
        lax.broadcasted_iota(jnp.int32, (WIDE, WIDE), 0) == (idx & 255), 1.0, 0.0
    ).astype(BF)
    here = lax.broadcasted_iota(jnp.int32, (ROWS, WIDE), 0) == (idx >> 8)
    parts = []
    for x in rows:
        high = x.astype(BF).astype(F32)
        for part in (high, x - high):
            parts.append(jnp.where(here, part, 0.0).astype(BF))
    return acc + dot(jnp.concatenate(parts, 0), lane, NT)


def joined(acc):
    acc = acc.reshape(acc.shape[0] // (2 * ROWS), 2, ROWS, WIDE)
    return (acc[:, 0] + acc[:, 1]).reshape(-1, WIDE)


def scatter_zones(idx_ref, term_ref, count):
    def eight(t, acc):
        r0 = pl.multiple_of(t * 8, 8)
        idx = idx_ref[pl.ds(r0, 8), :]
        terms = [term_ref[c, pl.ds(r0, 8), :] for c in range(count)]
        for a in range(8):
            acc = scatter_tile(acc, idx[a : a + 1], [x[a : a + 1] for x in terms])
        return acc

    return joined(lax.fori_loop(0, 8, eight, jnp.zeros((2 * ROWS * count, WIDE), F32)))


def flat_row(ref, first):
    return jnp.concatenate([ref[first : first + 1, :], ref[first + 1 : first + 2, :]], 1)


def received(lists_ref, got_refs, count):
    acc = jnp.zeros((2 * ROWS * count, WIDE), F32)
    for k, got in enumerate(got_refs):
        acc = scatter_tile(acc, flat_row(lists_ref, 2 * k), [flat_row(got, 2 * c) for c in range(count)])
    return joined(acc)


def send_shared(lists_ref, tab_ref, send_refs, count):
    idx = lists_ref[...]
    got = pick(table_rows(tab_ref, count), idx >> 7, idx & 127, (8, HALF))
    for k, send in enumerate(send_refs):
        send[...] = jnp.concatenate(
            [got[min(c, count - 1)][2 * k : 2 * k + 2] for c in range(4)], 0
        )


def force(v_ref, en, jac_ref, mass, t_ref, work_ref, tables):
    get = functools.partial(entry, tables, FORCE_AT)
    eh, el = split2(en)
    e_q = dot(get("bern_up_high"), eh) + dot(get("bern_up_high"), el) + dot(get("bern_up_low"), eh)
    pressure = GAMMA_LESS * e_q * mass
    for c in range(3):
        high, low = split2(v_ref[c])
        vc = jnp.concatenate([high, low, high], 0)
        term = jnp.zeros((NPZ, WIDE), F32)
        for k in range(3):
            w = jac_ref[(3 * k + c) * QP : (3 * k + c + 1) * QP, :] * pressure
            dv = dot(get("up%d" % k), vc)
            if c == 0 and k == 0:
                work_ref[...] = w * dv
            else:
                work_ref[...] += w * dv
            term = term + down(get("down%d" % k), w)
        t_ref[c] = term
    wh, wl = split2(work_ref[...])
    high, low = get("bern_down_high"), get("bern_down_low")
    return -(dot(high, wh) + dot(high, wl) + dot(low, wh))


def energy_change(rhs_e, inv_ref, tables):
    get = functools.partial(entry, tables, FORCE_AT)
    rh, rl = split2(rhs_e)
    prod = inv_ref[...] * (dot(get("spread"), rh) + dot(get("spread"), rl))
    total = jnp.zeros((LD, WIDE), F32)
    for k in range(0, LD * LD, 243):
        for part in split2(prod[k : k + 243]):
            total = total + dot(get("collect%d" % k), part)
    return total


def nodes_in(vel_ref, tab_ref):
    for c in range(3):
        for r in range(31):
            tab_ref[c * ROWS + r : c * ROWS + r + 1, :] = vel_ref[c : c + 1, r * WIDE : (r + 1) * WIDE]
        tab_ref[c * ROWS + 31 : (c + 1) * ROWS, :] = jnp.zeros((1, WIDE), F32)


def fetch(pairs, sems):
    copies = [pltpu.make_async_copy(a, b, sems.at[i]) for i, (a, b) in enumerate(pairs)]
    for copy in copies:
        copy.start()
    return copies


def split_side():
    return lax.axis_index("split")


def sent_block(k):
    s = split_side()
    return (s % 2, 1 - s % 2, 2 + s // 2, 3 - s // 2)[k]


def landing_block(k):
    s = split_side()
    return (1 - s % 2, s % 2, 3 - s // 2, 2 + s // 2)[k]


def pack_kernel(send_ref, shared_ref, jac_hbm, mass_hbm, inv_hbm, en_hbm, *refs):
    msgs, (lists, oh, jac_ref, mass_ref, inv_ref, en_ref, sems) = refs[:4], refs[4:]
    copies = fetch(
        ((mass_hbm, mass_ref), (inv_hbm, inv_ref), (en_hbm, en_ref), (jac_hbm, jac_ref)), sems
    )
    lane = lax.broadcasted_iota(jnp.int32, (1, WIDE), 1)
    for k in range(4):
        first = sent_block(k) * CAP
        for j in range(CAP):
            at = k * 8 + j if j < 8 else 32 + k
            oh[at : at + 1, :] = jnp.where(lane == send_ref[0, first + j], 1.0, 0.0)
    oh[36:40, :] = jnp.zeros((4, WIDE), F32)
    hot = oh[...].astype(BF)
    odds = (lax.axis_index("curve") % 2, split_side() % 2)
    for k in range(4):
        other = k ^ 1
        row = jnp.where(odds[k // 2] == 1, shared_ref[0, other : other + 1, :], shared_ref[0, k : k + 1, :])
        lists[2 * k : 2 * k + 1, :] = row[:, :HALF]
        lists[2 * k + 1 : 2 * k + 2, :] = row[:, HALF:]

    def put(at, n, block):
        for p in range(4):
            msgs[p][:, at : at + n] = block[p * 8 : (p + 1) * 8]
            done = 0
            while done < n:
                piece, off = divmod(at + done, TAIL)
                step = min(n - done, TAIL - off)
                msgs[p][piece : piece + 1, MSG + off : MSG + off + step] = block[
                    32 + p : 33 + p, done : done + step
                ]
                done += step

    places = ((mass_ref, AT_MASS), (inv_ref, AT_INV), (en_ref, AT_EN), (jac_ref, AT_JAC))
    for copy, (ref, at) in zip(copies, places):
        copy.wait()
        total = ref.shape[0]
        for i in range(0, total, WIDE):
            n = min(WIDE, total - i)
            parts = split3(ref[i : i + n, :])
            put(at + i, n, sum(dot(hot, part, NT) for part in parts))
    for p in range(4):
        msgs[p][:, AT_FLAG:MSG] = jnp.ones((8, MSG - AT_FLAG), F32)


def first_kernel(
    arrive_ref, m0, m1, m2, m3, lists_ref, jac_hbm, mass_hbm, inv_hbm, en_hbm, vel_hbm, zn_hbm, tables_hbm,
    jac_out, mass_out, inv_out, en_out, vel_out, ehalf_out, y_out, s0, s1, s2, s3,
    oh, arr, vz, terms, work, words, jac_ref, mass_ref, inv_ref, en_ref, vel_ref, zn_ref, tables, sems,
):
    copies = fetch(
        ((vel_hbm, vel_ref), (zn_hbm, zn_ref), (jac_hbm, jac_ref), (mass_hbm, mass_ref),
         (inv_hbm, inv_ref), (en_hbm, en_ref), (tables_hbm, tables)), sems,
    )
    msgs = (m0, m1, m2, m3)
    lane = lax.broadcasted_iota(jnp.int32, (1, WIDE), 1)
    oh[...] = jnp.zeros(oh.shape, F32)
    for k in range(4):
        first = landing_block(k) * CAP
        flag = msgs[k][0:1, AT_FLAG : AT_FLAG + 1]
        for j in range(CAP):
            at = k * 8 + j if j < 8 else 32 + k
            oh[at : at + 1, :] = jnp.where(lane == arrive_ref[0, first + j], 1.0, 0.0) * flag
    lands = jnp.sum(oh[...], axis=0, keepdims=True) > 0.5
    hot = oh[...].astype(BF)
    hot3 = jnp.concatenate([hot, hot, hot], 0)
    for p in range(4):
        arr[p * 8 : (p + 1) * 8, :] = msgs[p][:, :MSG]
        for piece in range(7):
            n = min(TAIL, MSG - piece * TAIL)
            arr[32 + p : 33 + p, piece * TAIL : piece * TAIL + n] = msgs[p][
                piece : piece + 1, MSG : MSG + n
            ]
    arr[36:48, :] = jnp.zeros((12, MSG), F32)
    copies[0].wait()
    nodes_in(vel_ref, vel_out)
    copies[1].wait()
    gather_zones(zn_ref, vel_out, words, vz)
    for copy in copies[2:]:
        copy.wait()
    for ref, out, at in (
        (jac_ref, jac_out, AT_JAC), (mass_ref, mass_out, AT_MASS),
        (inv_ref, inv_out, AT_INV), (en_ref, en_out, AT_EN),
    ):
        total = ref.shape[0]
        for i in range(0, total, WIDE):
            n = min(WIDE, total - i)
            wide = min(WIDE, -(-n // HALF) * HALF)
            came = jnp.concatenate(split3(arr[:, at + i : at + i + wide]), 0)
            out[i : i + n, :] = jnp.where(lands, dot(came, hot3, TN)[:n], ref[i : i + n, :])
    mass = mass_out[...]
    rhs_e = force(vz, en_out[...], jac_out, mass, terms, work, tables)
    terms[3] = down(entry(tables, FORCE_AT, "limit"), mass)
    ehalf_out[...] = en_out[...] + 0.5 * STEP_SIZE * energy_change(rhs_e, inv_out, tables)
    y_out[...] = scatter_zones(zn_ref, terms, 4)
    send_shared(lists_ref, y_out, (s0, s1, s2, s3), 4)


def rhos():
    rho, out = 1.0 / SIGMA, []
    for _ in range(SWEEPS):
        new = 1.0 / (2.0 * SIGMA - rho)
        out.append((new * rho, 2.0 * new / DELTA))
        rho = new
    return out


def three(x):
    return jnp.concatenate([x, x, x], 0)


def update(y, r_ref, d_ref, a_ref, ib_ref, step):
    keep, add = rhos()[step]
    r = r_ref[...] - y
    d = keep * d_ref[...] + add * (r * three(ib_ref[...]))
    return r, d, a_ref[...] + d


def apply_mass(zn_ref, mass_ref, tables, d_ref, y_out, zone, terms, words):
    gather_zones(zn_ref, d_ref, words, zone)
    mass = mass_ref[...]
    for c in range(3):
        at_points = up(entry(tables, MASS_AT, "up"), zone[c])
        terms[c] = down(entry(tables, MASS_AT, "down"), at_points * mass)
    y_out[...] = scatter_zones(zn_ref, terms, 3)


def start_kernel(g0, g1, g2, g3, y_ref, *refs, first):
    if first:
        lists, zn, mass, tables = refs[:4]
        ib, r_out, d_out, y_out, s0, s1, s2, s3, *scratch = refs[4:]
        y = y_ref[...] + received(lists, (g0, g1, g2, g3), 4)
        pad = lax.broadcasted_iota(jnp.int32, (ROWS, WIDE), 0) == 31
        inv_bound = 1.0 / jnp.where(pad, 1.0, y[96:])
        ib[...] = inv_bound
        r = y[:96]
    else:
        ib, lists, zn, mass, tables = refs[:5]
        r_out, d_out, y_out, s0, s1, s2, s3, *scratch = refs[5:]
        r = y_ref[...] + received(lists, (g0, g1, g2, g3), 3)
        inv_bound = ib[...]
    r_out[...] = r
    d_out[...] = r * three(inv_bound) * (1.0 / THETA)
    apply_mass(zn, mass, tables, d_out, y_out, *scratch)
    send_shared(lists, y_out, (s0, s1, s2, s3), 3)


def sweep_kernel(
    g0, g1, g2, g3, y_ref, r_ref, d_ref, a_ref, ib_ref, lists, zn, mass, tables,
    r_out, d_out, a_out, y_out, s0, s1, s2, s3, *scratch, step,
):
    y = y_ref[...] + received(lists, (g0, g1, g2, g3), 3)
    r, d, a = update(y, r_ref, d_ref, a_ref, ib_ref, step)
    r_out[...] = r
    d_out[...] = d
    a_out[...] = a
    apply_mass(zn, mass, tables, d_out, y_out, *scratch)
    send_shared(lists, y_out, (s0, s1, s2, s3), 3)


def second_kernel(
    g0, g1, g2, g3, y_ref, r_ref, d_ref, a_ref, ib_ref, lists, zn, mass, jac, inv, en, ehalf, vel, tables,
    en_out, y_out, s0, s1, s2, s3, vhalf, vz, terms, work, words,
):
    y = y_ref[...] + received(lists, (g0, g1, g2, g3), 3)
    _, _, a = update(y, r_ref, d_ref, a_ref, ib_ref, SWEEPS - 1)
    vhalf[...] = vel[...] + 0.5 * STEP_SIZE * a
    gather_zones(zn, vhalf, words, vz)
    rhs_e = force(vz, ehalf[...], jac, mass[...], terms, work, tables)
    y_out[...] = scatter_zones(zn, terms, 3)
    send_shared(lists, y_out, (s0, s1, s2, s3), 3)
    en_out[...] = en[...] + STEP_SIZE * energy_change(rhs_e, inv, tables)


def last_kernel(g0, g1, g2, g3, y_ref, r_ref, d_ref, a_ref, ib_ref, lists, vel, out):
    y = y_ref[...] + received(lists, (g0, g1, g2, g3), 3)
    _, _, a = update(y, r_ref, d_ref, a_ref, ib_ref, SWEEPS - 1)
    v = vel[...] + STEP_SIZE * a
    for c in range(3):
        for r in range(31):
            out[c : c + 1, r * WIDE : (r + 1) * WIDE] = v[c * ROWS + r : c * ROWS + r + 1]


VM = pl.BlockSpec(memory_space=pltpu.VMEM)
SM = pl.BlockSpec(memory_space=pltpu.SMEM)
HB = pl.BlockSpec(memory_space=pl.ANY)


def shape_of(s):
    return s if isinstance(s, jax.ShapeDtypeStruct) else jax.ShapeDtypeStruct(s, F32)


def call(kernel, args, outs, scratch=(), specs=None, limit=16, copies=0, name=None):
    scratch = [pltpu.VMEM(shape_of(s).shape, shape_of(s).dtype) for s in scratch]
    return pl.pallas_call(
        kernel,
        out_shape=[shape_of(s) for s in outs],
        in_specs=specs or [VM] * len(args),
        out_specs=[VM] * len(outs),
        scratch_shapes=scratch + ([pltpu.SemaphoreType.DMA((copies,))] if copies else []),
        compiler_params=pltpu.CompilerParams(vmem_limit_bytes=limit * 1024 * 1024),
        name=name,
    )(*args)


def paired(first, size, hop=1):
    low = [i for i in range(size - hop) if (i // hop) % 2 == first]
    return [p for i in low for p in ((i, i + hop), (i + hop, i))]


def exchange(sends):
    n_curve, n_split = lax.axis_size("curve"), lax.axis_size("split")
    return [
        lax.ppermute(sends[0], "curve", paired(0, n_curve)),
        lax.ppermute(sends[1], "curve", paired(1, n_curve)),
        lax.ppermute(sends[2], "split", paired(0, n_split)),
        lax.ppermute(sends[3], "split", paired(1, n_split)),
    ]


def per_device(velocity, energy, mass, jac, inv, send_rows, arrive_rows, zone_nodes, shared_nodes):
    force_tables, mass_tables = jnp.asarray(FORCE_TABLES), jnp.asarray(MASS_TABLES)
    devices = lax.axis_size("curve") * lax.axis_size("split")
    ints = lambda *s: jax.ShapeDtypeStruct(s, jnp.int32)
    half = lambda *s: jax.ShapeDtypeStruct(s, BF)
    node, msg = (96, WIDE), (8, MSG + TAIL)
    fields = [(9 * QP, WIDE), (QP, WIDE), (LD * LD, WIDE), (LD, WIDE)]
    send = [(8, HALF)] * 4
    zone = (3, NPZ, WIDE)
    words = ints(2 * ROWS, WIDE)
    *msgs, lists = call(
        pack_kernel, (send_rows, shared_nodes, jac, mass, inv, energy), [msg] * 4 + [ints(8, HALF)],
        [(40, WIDE)] + fields, [SM, VM] + [HB] * 4, copies=4, name="pack",
    )
    came = []
    for k, m in enumerate(msgs):
        came.append(lax.ppermute(m, AXES, paired(k % 2, devices, 1 + k // 2)))
    jac, mass, inv, en, vel, ehalf, y, *sends = call(
        first_kernel,
        (arrive_rows, *came, lists, jac, mass, inv, energy, velocity, zone_nodes, force_tables),
        fields + [node, (LD, WIDE), (128, WIDE)] + send,
        [(48, WIDE), (48, MSG), zone, (4, NPZ, WIDE), (QP, WIDE), words] + fields
        + [velocity.shape, ints(NPZ, WIDE), half(*FORCE_TABLES.shape)],
        [SM] + [VM] * 5 + [HB] * 7, limit=24, copies=7, name="force_one",
    )
    scratch = [zone, zone, words]
    for section in range(2):
        got = exchange(sends)
        outs = [node, node, node] + send
        tail = (lists, zone_nodes, mass, mass_tables)
        if section == 0:
            ib, r, d, y, *sends = call(
                functools.partial(start_kernel, first=True), (*got, y, *tail),
                [(ROWS, WIDE)] + outs, scratch, name="mass_start",
            )
        else:
            r, d, y, *sends = call(
                functools.partial(start_kernel, first=False), (*got, y, ib, *tail), outs, scratch,
                name="mass_start_two",
            )
        a = d
        for step in range(SWEEPS - 1):
            got = exchange(sends)
            r, d, a, y, *sends = call(
                functools.partial(sweep_kernel, step=step), (*got, y, r, d, a, ib, *tail),
                [node] + outs, scratch, name="mass_sweep",
            )
        got = exchange(sends)
        if section == 0:
            energy_next, y, *sends = call(
                second_kernel,
                (*got, y, r, d, a, ib, lists, zone_nodes, mass, jac, inv, en, ehalf, vel, force_tables),
                [(LD, WIDE), node] + send, [node, zone, zone, (QP, WIDE), words], limit=24,
                name="force_two",
            )
        else:
            (velocity_next,) = call(
                last_kernel, (*got, y, r, d, a, ib, lists, vel), [velocity.shape], name="finish"
            )
    return velocity_next, energy_next


def solution(mesh):
    both = P(None, AXES)
    rows = P(AXES, None)
    return jax.shard_map(
        per_device,
        mesh=mesh,
        in_specs=(both, both, both, both, both, rows, rows, both, P(AXES, None, None)),
        out_specs=(both, both),
        check_vma=False,
    )
```

```python
import functools
import math

import jax
import jax.numpy as jnp
import numpy as np
from jax import lax
from jax.experimental import pallas as pl
from jax.experimental.pallas import tpu as pltpu
from jax.sharding import PartitionSpec as P

H1D, Q1D, L1D, SWEEPS = 4, 6, 3, 3
NPZ, QP, LD = 64, 216, 27
GAMMA_LESS = 0.4
STEP_SIZE = 0.25
THETA, DELTA = 0.575, 0.425
SIGMA = THETA / DELTA
AXES = ("curve", "split")
CAP = 9
HALF = 128
WIDE = 256
ROWS = 32
AT_JAC, AT_MASS, AT_INV, AT_EN, AT_FLAG, MSG = 0, 2048, 2304, 3072, 3100, 3200
TAIL = 512
BF, F32 = jnp.bfloat16, jnp.float32
NT = (((1,), (1,)), ((), ()))
TN = (((0,), (0,)), ((), ()))


def line_tables():
    on_line = [-0.9324695142031521, -0.6612093864662645, -0.2386191860831909]
    on_line = on_line + [-v for v in reversed(on_line)]
    points = [0.5 * (v + 1.0) for v in on_line]
    lobatto = [0.5 * (v + 1.0) for v in [-1.0, -0.4472135954999579, 0.4472135954999579, 1.0]]
    value, slope, bern = np.zeros((Q1D, H1D)), np.zeros((Q1D, H1D)), np.zeros((Q1D, L1D))
    for i in range(H1D):
        others = [lobatto[j] for j in range(H1D) if j != i]
        scaling = np.prod([lobatto[i] - o for o in others])
        for q, t in enumerate(points):
            value[q, i] = np.prod([t - o for o in others]) / scaling
            slope[q, i] = sum(
                np.prod([t - others[n] for n in range(3) if n != m]) for m in range(3)
            ) / scaling
    for q, t in enumerate(points):
        for j in range(L1D):
            bern[q, j] = math.comb(2, j) * t**j * (1.0 - t) ** (2 - j)
    return [np.float32(t).astype(np.float64) for t in (value, slope, bern)]


def halves(table):
    high = table.astype(np.float32).astype(BF)
    low = (table - high.astype(np.float64)).astype(np.float32).astype(BF)
    return high, low


def beside(table):
    high, low = halves(table)
    return np.concatenate([high, high, low], 1)


def above(table):
    return np.concatenate(halves(table), 0)


def stacked(tables):
    places, blocks, at = {}, [], 0
    for name, table in tables.items():
        rows, columns = table.shape
        places[name] = (at, rows, columns)
        room = -(-rows // 16) * 16
        block = np.zeros((room, WIDE), BF)
        block[:rows, :columns] = table
        blocks.append(block)
        at += room
    return np.concatenate(blocks, 0), places


def constants():
    b, g, p = line_tables()
    kron = lambda x, y, z: np.kron(np.kron(x, y), z)
    bbb, ppp = kron(b, b, b), kron(p, p, p)
    grads = [kron(g, b, b), kron(b, g, b), kron(b, b, g)]
    r = np.abs(b).sum(1, keepdims=True)
    limit = kron(np.abs(b), np.abs(b), np.abs(b)) * kron(r, r, r)
    spread = np.kron(np.ones((LD, 1)), np.eye(LD)).astype(BF)
    collect = np.kron(np.eye(LD), np.ones((1, LD))).astype(BF)
    force = dict(
        bern_up_high=halves(ppp)[0],
        bern_up_low=halves(ppp)[1],
        bern_down_high=halves(ppp.T)[0],
        bern_down_low=halves(ppp.T)[1],
        spread=spread,
        limit=above(limit.T),
    )
    for k, t in enumerate(grads):
        force["up%d" % k] = beside(t)
        force["down%d" % k] = above(t.T)
    for k in range(0, LD * LD, 243):
        force["collect%d" % k] = collect[:, k : k + 243]
    return stacked(force), stacked(dict(up=beside(bbb), down=above(bbb.T)))


(FORCE_TABLES, FORCE_AT), (MASS_TABLES, MASS_AT) = constants()


def entry(ref, places, name):
    at, rows, columns = places[name]
    return ref[at : at + rows, :columns]


def split2(x):
    high = x.astype(BF)
    return high, (x - high.astype(F32)).astype(BF)


def split3(x):
    high = x.astype(BF)
    rest = x - high.astype(F32)
    mid = rest.astype(BF)
    return high, mid, (rest - mid.astype(F32)).astype(BF)


def dot(a, b, dims=None):
    if dims is None:
        return jnp.dot(a, b, preferred_element_type=F32)
    return lax.dot_general(a, b, dims, preferred_element_type=F32)


def up(table, x):
    high, low = split2(x)
    return dot(table, jnp.concatenate([high, low, high], 0))


def down(table, x):
    high, low = split2(x)
    half = table.shape[0] // 2
    both = dot(table, high)
    return both[:half] + both[half:] + dot(table[:half], low)


def pick(tables, chunk_of, lane_of, shape, kind=F32):
    acc = [jnp.zeros(shape, kind) for _ in tables]
    for k in range(62):
        here = chunk_of == k
        for c, row in enumerate(tables):
            got = jnp.take_along_axis(jnp.broadcast_to(row(k), shape), lane_of, axis=1)
            acc[c] = jnp.where(here, got, acc[c])
    return acc


def table_rows(ref, count):
    def row(c, k):
        return ref[c * ROWS + k // 2 : c * ROWS + k // 2 + 1, (k % 2) * HALF : (k % 2 + 1) * HALF]

    return [functools.partial(row, c) for c in range(count)]


def gather_zones(idx_ref, tab_ref, word_ref, out_ref):
    x = tab_ref[...]
    scale = jnp.max(jnp.abs(x), keepdims=True)
    per_unit = 1000000.0 / jnp.maximum(scale, 1e-30)
    step = jnp.maximum(scale, 1e-30) * 1e-6
    q = jnp.round(x * per_unit).astype(jnp.int32) + (1 << 20)
    word_ref[:ROWS] = (q[:ROWS] << 11) | (q[2 * ROWS :] >> 10)
    word_ref[ROWS:] = (q[ROWS : 2 * ROWS] << 11) | (q[2 * ROWS :] & 1023)

    @pl.loop(0, 8)
    def _(t):
        r0 = pl.multiple_of(t * 8, 8)
        for h in range(2):
            lanes = slice(h * HALF, (h + 1) * HALF)
            idx = idx_ref[pl.ds(r0, 8), lanes]
            w0, w1 = pick(table_rows(word_ref, 2), idx >> 7, idx & 127, (8, HALF), jnp.int32)
            back = (
                lax.shift_right_logical(w0, 11),
                lax.shift_right_logical(w1, 11),
                ((w0 & 2047) << 10) | (w1 & 1023),
            )
            for c in range(3):
                out_ref[c, pl.ds(r0, 8), lanes] = (back[c] - (1 << 20)).astype(F32) * step


def spread_rows(idx, rows):
    here = lax.broadcasted_iota(jnp.int32, (ROWS, WIDE), 0) == (idx >> 8)
    parts = []
    for x in rows:
        high = x.astype(BF).astype(F32)
        for part in (high, x - high):
            parts.append(jnp.where(here, part, 0.0).astype(BF))
    return jnp.concatenate(parts, 0)


def scatter_tile(acc, idx, rows):
    lane = jnp.where(
        lax.broadcasted_iota(jnp.int32, (WIDE, WIDE), 0) == (idx & 255), 1.0, 0.0
    ).astype(BF)
    return acc + dot(spread_rows(idx, rows), lane, NT)


def joined(acc):
    acc = acc.reshape(acc.shape[0] // (2 * ROWS), 2, ROWS, WIDE)
    return (acc[:, 0] + acc[:, 1]).reshape(-1, WIDE)


def scatter_zones(idx_ref, lane_ref, term_ref, count):
    def eight(t, acc):
        r0 = pl.multiple_of(t * 8, 8)
        idx = idx_ref[pl.ds(r0, 8), :]
        terms = [term_ref[c, pl.ds(r0, 8), :] for c in range(count)]
        for a in range(8):
            acc = acc + dot(spread_rows(idx[a : a + 1], [x[a : a + 1] for x in terms]), lane_ref[r0 + a])
        return acc

    return joined(lax.fori_loop(0, 8, eight, jnp.zeros((2 * ROWS * count, WIDE), F32)))


def flat_row(ref, first):
    return jnp.concatenate([ref[first : first + 1, :], ref[first + 1 : first + 2, :]], 1)


def received(lists_ref, got_refs, count):
    acc = jnp.zeros((2 * ROWS * count, WIDE), F32)
    for k, got in enumerate(got_refs):
        acc = scatter_tile(acc, flat_row(lists_ref, 2 * k), [flat_row(got, 2 * c) for c in range(count)])
    return joined(acc)


def send_shared(lists_ref, tab_ref, send_refs, count):
    idx = lists_ref[...]
    got = pick(table_rows(tab_ref, count), idx >> 7, idx & 127, (8, HALF))
    for k, send in enumerate(send_refs):
        send[...] = jnp.concatenate(
            [got[min(c, count - 1)][2 * k : 2 * k + 2] for c in range(4)], 0
        )


def force(v_ref, en, jac_ref, mass, t_ref, work_ref, tables):
    get = functools.partial(entry, tables, FORCE_AT)
    eh, el = split2(en)
    e_q = dot(get("bern_up_high"), eh) + dot(get("bern_up_high"), el) + dot(get("bern_up_low"), eh)
    pressure = GAMMA_LESS * e_q * mass
    for c in range(3):
        high, low = split2(v_ref[c])
        vc = jnp.concatenate([high, low, high], 0)
        term = jnp.zeros((NPZ, WIDE), F32)
        for k in range(3):
            w = jac_ref[(3 * k + c) * QP : (3 * k + c + 1) * QP, :] * pressure
            dv = dot(get("up%d" % k), vc)
            if c == 0 and k == 0:
                work_ref[...] = w * dv
            else:
                work_ref[...] += w * dv
            term = term + down(get("down%d" % k), w)
        t_ref[c] = term
    wh, wl = split2(work_ref[...])
    high, low = get("bern_down_high"), get("bern_down_low")
    return -(dot(high, wh) + dot(high, wl) + dot(low, wh))


def energy_change(rhs_e, inv_ref, tables):
    get = functools.partial(entry, tables, FORCE_AT)
    rh, rl = split2(rhs_e)
    prod = inv_ref[...] * (dot(get("spread"), rh) + dot(get("spread"), rl))
    total = jnp.zeros((LD, WIDE), F32)
    for k in range(0, LD * LD, 243):
        for part in split2(prod[k : k + 243]):
            total = total + dot(get("collect%d" % k), part)
    return total


def nodes_in(vel_ref, tab_ref):
    for c in range(3):
        for r in range(31):
            tab_ref[c * ROWS + r : c * ROWS + r + 1, :] = vel_ref[c : c + 1, r * WIDE : (r + 1) * WIDE]
        tab_ref[c * ROWS + 31 : (c + 1) * ROWS, :] = jnp.zeros((1, WIDE), F32)


def fetch(pairs, sems):
    copies = [pltpu.make_async_copy(a, b, sems.at[i]) for i, (a, b) in enumerate(pairs)]
    for copy in copies:
        copy.start()
    return copies


def split_side():
    return lax.axis_index("split")


def sent_block(k):
    s = split_side()
    return (s % 2, 1 - s % 2, 2 + s // 2, 3 - s // 2)[k]


def landing_block(k):
    s = split_side()
    return (1 - s % 2, s % 2, 3 - s // 2, 2 + s // 2)[k]


def pack_kernel(send_ref, shared_ref, jac_hbm, mass_hbm, inv_hbm, en_hbm, *refs):
    msgs, (lists, oh, jac_ref, mass_ref, inv_ref, en_ref, sems) = refs[:4], refs[4:]
    copies = fetch(
        ((mass_hbm, mass_ref), (inv_hbm, inv_ref), (en_hbm, en_ref), (jac_hbm, jac_ref)), sems
    )
    lane = lax.broadcasted_iota(jnp.int32, (1, WIDE), 1)
    for k in range(4):
        first = sent_block(k) * CAP
        for j in range(CAP):
            at = k * 8 + j if j < 8 else 32 + k
            oh[at : at + 1, :] = jnp.where(lane == send_ref[0, first + j], 1.0, 0.0)
    oh[36:40, :] = jnp.zeros((4, WIDE), F32)
    hot = oh[...].astype(BF)
    odds = (lax.axis_index("curve") % 2, split_side() % 2)
    for k in range(4):
        other = k ^ 1
        row = jnp.where(odds[k // 2] == 1, shared_ref[0, other : other + 1, :], shared_ref[0, k : k + 1, :])
        lists[2 * k : 2 * k + 1, :] = row[:, :HALF]
        lists[2 * k + 1 : 2 * k + 2, :] = row[:, HALF:]

    def put(at, n, block):
        for p in range(4):
            msgs[p][:, at : at + n] = block[p * 8 : (p + 1) * 8]
            done = 0
            while done < n:
                piece, off = divmod(at + done, TAIL)
                step = min(n - done, TAIL - off)
                msgs[p][piece : piece + 1, MSG + off : MSG + off + step] = block[
                    32 + p : 33 + p, done : done + step
                ]
                done += step

    places = ((mass_ref, AT_MASS), (inv_ref, AT_INV), (en_ref, AT_EN), (jac_ref, AT_JAC))
    for copy, (ref, at) in zip(copies, places):
        copy.wait()
        total = ref.shape[0]
        for i in range(0, total, WIDE):
            n = min(WIDE, total - i)
            parts = split3(ref[i : i + n, :])
            put(at + i, n, sum(dot(hot, part, NT) for part in parts))
    for p in range(4):
        msgs[p][:, AT_FLAG:MSG] = jnp.ones((8, MSG - AT_FLAG), F32)


def prep_kernel(vel_ref, zn_ref, _lists, _arrive, _en, _tables, vel_out, vz, lane_out, words, column):
    nodes_in(vel_ref, vel_out)
    gather_zones(zn_ref, vel_out, words, vz)
    column[:, :NPZ] = jnp.transpose((zn_ref[...] & 255).astype(F32), (1, 0))
    lane = lax.broadcasted_iota(jnp.int32, (16, WIDE), 1).astype(F32)

    @pl.loop(0, 16)
    def _(t):
        r0 = pl.multiple_of(t * 16, 16)
        rows = column[pl.ds(r0, 16), :]
        for a in range(NPZ):
            lane_out[a, pl.ds(r0, 16), :] = jnp.where(lane == rows[:, a : a + 1], 1.0, 0.0).astype(BF)


def first_kernel(
    arrive_ref, m0, m1, m2, m3, lists_ref, jac_ref, mass_ref, inv_ref, en_ref, zn_ref, tables, vz, lanes,
    jac_out, mass_out, inv_out, en_out, ehalf_out, y_out, s0, s1, s2, s3, oh, arr, terms, work,
):
    msgs = (m0, m1, m2, m3)
    lane = lax.broadcasted_iota(jnp.int32, (1, WIDE), 1)
    oh[...] = jnp.zeros(oh.shape, F32)
    for k in range(4):
        first = landing_block(k) * CAP
        flag = msgs[k][0:1, AT_FLAG : AT_FLAG + 1]
        for j in range(CAP):
            at = k * 8 + j if j < 8 else 32 + k
            oh[at : at + 1, :] = jnp.where(lane == arrive_ref[0, first + j], 1.0, 0.0) * flag
    lands = jnp.sum(oh[...], axis=0, keepdims=True) > 0.5
    hot = oh[...].astype(BF)
    hot3 = jnp.concatenate([hot, hot, hot], 0)
    for p in range(4):
        arr[p * 8 : (p + 1) * 8, :] = msgs[p][:, :MSG]
        for piece in range(7):
            n = min(TAIL, MSG - piece * TAIL)
            arr[32 + p : 33 + p, piece * TAIL : piece * TAIL + n] = msgs[p][
                piece : piece + 1, MSG : MSG + n
            ]
    arr[36:48, :] = jnp.zeros((12, MSG), F32)
    for ref, out, at in (
        (jac_ref, jac_out, AT_JAC), (mass_ref, mass_out, AT_MASS),
        (inv_ref, inv_out, AT_INV), (en_ref, en_out, AT_EN),
    ):
        total = ref.shape[0]
        for i in range(0, total, WIDE):
            n = min(WIDE, total - i)
            wide = min(WIDE, -(-n // HALF) * HALF)
            came = jnp.concatenate(split3(arr[:, at + i : at + i + wide]), 0)
            out[i : i + n, :] = jnp.where(lands, dot(came, hot3, TN)[:n], ref[i : i + n, :])
    mass = mass_out[...]
    rhs_e = force(vz, en_out[...], jac_out, mass, terms, work, tables)
    terms[3] = down(entry(tables, FORCE_AT, "limit"), mass)
    ehalf_out[...] = en_out[...] + 0.5 * STEP_SIZE * energy_change(rhs_e, inv_out, tables)
    y_out[...] = scatter_zones(zn_ref, lanes, terms, 4)
    send_shared(lists_ref, y_out, (s0, s1, s2, s3), 4)


def rhos():
    rho, out = 1.0 / SIGMA, []
    for _ in range(SWEEPS):
        new = 1.0 / (2.0 * SIGMA - rho)
        out.append((new * rho, 2.0 * new / DELTA))
        rho = new
    return out


def three(x):
    return jnp.concatenate([x, x, x], 0)


def update(y, r_ref, d_ref, a_ref, ib_ref, step):
    keep, add = rhos()[step]
    r = r_ref[...] - y
    d = keep * d_ref[...] + add * (r * three(ib_ref[...]))
    return r, d, a_ref[...] + d


def apply_mass(zn_ref, lanes, mass_ref, tables, d_ref, y_out, zone, terms, words):
    gather_zones(zn_ref, d_ref, words, zone)
    mass = mass_ref[...]
    for c in range(3):
        at_points = up(entry(tables, MASS_AT, "up"), zone[c])
        terms[c] = down(entry(tables, MASS_AT, "down"), at_points * mass)
    y_out[...] = scatter_zones(zn_ref, lanes, terms, 3)


def start_kernel(g0, g1, g2, g3, y_ref, *refs, first):
    if first:
        lists, zn, lanes, mass, tables = refs[:5]
        ib, r_out, d_out, y_out, s0, s1, s2, s3, *scratch = refs[5:]
        y = y_ref[...] + received(lists, (g0, g1, g2, g3), 4)
        pad = lax.broadcasted_iota(jnp.int32, (ROWS, WIDE), 0) == 31
        inv_bound = 1.0 / jnp.where(pad, 1.0, y[96:])
        ib[...] = inv_bound
        r = y[:96]
    else:
        ib, lists, zn, lanes, mass, tables = refs[:6]
        r_out, d_out, y_out, s0, s1, s2, s3, *scratch = refs[6:]
        r = y_ref[...] + received(lists, (g0, g1, g2, g3), 3)
        inv_bound = ib[...]
    r_out[...] = r
    d_out[...] = r * three(inv_bound) * (1.0 / THETA)
    apply_mass(zn, lanes, mass, tables, d_out, y_out, *scratch)
    send_shared(lists, y_out, (s0, s1, s2, s3), 3)


def sweep_kernel(
    g0, g1, g2, g3, y_ref, r_ref, d_ref, a_ref, ib_ref, lists, zn, lanes, mass, tables,
    r_out, d_out, a_out, y_out, s0, s1, s2, s3, *scratch, step,
):
    y = y_ref[...] + received(lists, (g0, g1, g2, g3), 3)
    r, d, a = update(y, r_ref, d_ref, a_ref, ib_ref, step)
    r_out[...] = r
    d_out[...] = d
    a_out[...] = a
    apply_mass(zn, lanes, mass, tables, d_out, y_out, *scratch)
    send_shared(lists, y_out, (s0, s1, s2, s3), 3)


def second_kernel(
    g0, g1, g2, g3, y_ref, r_ref, d_ref, a_ref, ib_ref, lists, zn, lanes, mass, jac, inv, en, ehalf, vel, tables,
    en_out, y_out, s0, s1, s2, s3, vhalf, vz, terms, work, words,
):
    y = y_ref[...] + received(lists, (g0, g1, g2, g3), 3)
    _, _, a = update(y, r_ref, d_ref, a_ref, ib_ref, SWEEPS - 1)
    vhalf[...] = vel[...] + 0.5 * STEP_SIZE * a
    gather_zones(zn, vhalf, words, vz)
    rhs_e = force(vz, ehalf[...], jac, mass[...], terms, work, tables)
    y_out[...] = scatter_zones(zn, lanes, terms, 3)
    send_shared(lists, y_out, (s0, s1, s2, s3), 3)
    en_out[...] = en[...] + STEP_SIZE * energy_change(rhs_e, inv, tables)


def last_kernel(g0, g1, g2, g3, y_ref, r_ref, d_ref, a_ref, ib_ref, lists, vel, out):
    y = y_ref[...] + received(lists, (g0, g1, g2, g3), 3)
    _, _, a = update(y, r_ref, d_ref, a_ref, ib_ref, SWEEPS - 1)
    v = vel[...] + STEP_SIZE * a
    for c in range(3):
        for r in range(31):
            out[c : c + 1, r * WIDE : (r + 1) * WIDE] = v[c * ROWS + r : c * ROWS + r + 1]


VM = pl.BlockSpec(memory_space=pltpu.VMEM)
SM = pl.BlockSpec(memory_space=pltpu.SMEM)
HB = pl.BlockSpec(memory_space=pltpu.HBM)


def shape_of(s):
    return s if isinstance(s, jax.ShapeDtypeStruct) else jax.ShapeDtypeStruct(s, F32)


def call(kernel, args, outs, scratch=(), specs=None, limit=16, copies=0, name=None):
    scratch = [pltpu.VMEM(shape_of(s).shape, shape_of(s).dtype) for s in scratch]
    return pl.pallas_call(
        kernel,
        out_shape=[shape_of(s) for s in outs],
        in_specs=specs or [VM] * len(args),
        out_specs=[VM] * len(outs),
        scratch_shapes=scratch + ([pltpu.SemaphoreType.DMA((copies,))] if copies else []),
        compiler_params=pltpu.CompilerParams(vmem_limit_bytes=limit * 1024 * 1024),
        name=name,
    )(*args)


def paired(first, size, hop=1):
    low = [i for i in range(size - hop) if (i // hop) % 2 == first]
    return [p for i in low for p in ((i, i + hop), (i + hop, i))]


def exchange(sends):
    n_curve, n_split = lax.axis_size("curve"), lax.axis_size("split")
    return [
        lax.ppermute(sends[0], "curve", paired(0, n_curve)),
        lax.ppermute(sends[1], "curve", paired(1, n_curve)),
        lax.ppermute(sends[2], "split", paired(0, n_split)),
        lax.ppermute(sends[3], "split", paired(1, n_split)),
    ]


def per_device(velocity, energy, mass, jac, inv, send_rows, arrive_rows, zone_nodes, shared_nodes):
    force_tables, mass_tables = jnp.asarray(FORCE_TABLES), jnp.asarray(MASS_TABLES)
    devices = lax.axis_size("curve") * lax.axis_size("split")
    ints = lambda *s: jax.ShapeDtypeStruct(s, jnp.int32)
    half = lambda *s: jax.ShapeDtypeStruct(s, BF)
    node, msg = (96, WIDE), (8, MSG + TAIL)
    fields = [(9 * QP, WIDE), (QP, WIDE), (LD * LD, WIDE), (LD, WIDE)]
    send = [(8, HALF)] * 4
    zone = (3, NPZ, WIDE)
    words = ints(2 * ROWS, WIDE)
    *msgs, lists = call(
        pack_kernel, (send_rows, shared_nodes, jac, mass, inv, energy), [msg] * 4 + [ints(8, HALF)],
        [(40, WIDE)] + fields, [SM, VM] + [HB] * 4, limit=58, copies=4, name="pack",
    )
    came = []
    for k, m in enumerate(msgs):
        came.append(lax.ppermute(m, AXES, paired(k % 2, devices, 1 + k // 2)))
    vel, vz, lanes = call(
        prep_kernel, (velocity, zone_nodes, lists, arrive_rows, energy, force_tables),
        [node, zone, half(NPZ, WIDE, WIDE)], [words, (WIDE, HALF)], [VM, VM, VM, SM, VM, VM], name="prep",
    )
    jac, mass, inv, en, ehalf, y, *sends = call(
        first_kernel,
        (arrive_rows, *came, lists, jac, mass, inv, energy, zone_nodes, force_tables, vz, lanes),
        fields + [(LD, WIDE), (128, WIDE)] + send,
        [(48, WIDE), (48, MSG), (4, NPZ, WIDE), (QP, WIDE)],
        [SM] + [VM] * 13, name="force_one",
    )
    scratch = [zone, zone, words]
    for section in range(2):
        got = exchange(sends)
        outs = [node, node, node] + send
        tail = (lists, zone_nodes, lanes, mass, mass_tables)
        if section == 0:
            ib, r, d, y, *sends = call(
                functools.partial(start_kernel, first=True), (*got, y, *tail),
                [(ROWS, WIDE)] + outs, scratch, name="mass_start",
            )
        else:
            r, d, y, *sends = call(
                functools.partial(start_kernel, first=False), (*got, y, ib, *tail), outs, scratch,
                name="mass_start_two",
            )
        a = d
        for step in range(SWEEPS - 1):
            got = exchange(sends)
            r, d, a, y, *sends = call(
                functools.partial(sweep_kernel, step=step), (*got, y, r, d, a, ib, *tail),
                [node] + outs, scratch, name="mass_sweep",
            )
        got = exchange(sends)
        if section == 0:
            energy_next, y, *sends = call(
                second_kernel,
                (*got, y, r, d, a, ib, lists, zone_nodes, lanes, mass, jac, inv, en, ehalf, vel, force_tables),
                [(LD, WIDE), node] + send, [node, zone, zone, (QP, WIDE), words], limit=24,
                name="force_two",
            )
        else:
            (velocity_next,) = call(
                last_kernel, (*got, y, r, d, a, ib, lists, vel), [velocity.shape], name="finish"
            )
    return velocity_next, energy_next


def solution(mesh):
    both = P(None, AXES)
    rows = P(AXES, None)
    return jax.shard_map(
        per_device,
        mesh=mesh,
        in_specs=(both, both, both, both, both, rows, rows, both, P(AXES, None, None)),
        out_specs=(both, both),
        check_vma=False,
    )
```

```python
import functools
import math

import jax
import jax.numpy as jnp
import numpy as np
from jax import lax
from jax.experimental import pallas as pl
from jax.experimental.pallas import tpu as pltpu
from jax.sharding import PartitionSpec as P

H1D, Q1D, L1D, SWEEPS = 4, 6, 3, 3
NPZ, QP, LD = 64, 216, 27
GAMMA_LESS = 0.4
STEP_SIZE = 0.25
THETA, DELTA = 0.575, 0.425
SIGMA = THETA / DELTA
AXES = ("curve", "split")
CAP = 9
COMPONENTS = 6
HALF = 128
WIDE = 256
ROWS = 32
AT_JAC, AT_MASS, AT_INV, AT_EN, AT_FLAG, MSG = 0, 2048, 2304, 3072, 3100, 3200
TAIL = 512
BF, F32 = jnp.bfloat16, jnp.float32
NT = (((1,), (1,)), ((), ()))
TN = (((0,), (0,)), ((), ()))


def line_tables():
    on_line = [-0.9324695142031521, -0.6612093864662645, -0.2386191860831909]
    on_line = on_line + [-v for v in reversed(on_line)]
    points = [0.5 * (v + 1.0) for v in on_line]
    lobatto = [0.5 * (v + 1.0) for v in [-1.0, -0.4472135954999579, 0.4472135954999579, 1.0]]
    value, slope, bern = np.zeros((Q1D, H1D)), np.zeros((Q1D, H1D)), np.zeros((Q1D, L1D))
    for i in range(H1D):
        others = [lobatto[j] for j in range(H1D) if j != i]
        scaling = np.prod([lobatto[i] - o for o in others])
        for q, t in enumerate(points):
            value[q, i] = np.prod([t - o for o in others]) / scaling
            slope[q, i] = sum(
                np.prod([t - others[n] for n in range(3) if n != m]) for m in range(3)
            ) / scaling
    for q, t in enumerate(points):
        for j in range(L1D):
            bern[q, j] = math.comb(2, j) * t**j * (1.0 - t) ** (2 - j)
    return [np.float32(t).astype(np.float64) for t in (value, slope, bern)]


def halves(table):
    high = table.astype(np.float32).astype(BF)
    low = (table - high.astype(np.float64)).astype(np.float32).astype(BF)
    return high, low


def beside(table):
    high, low = halves(table)
    return np.concatenate([high, high, low], 1)


def above(table):
    return np.concatenate(halves(table), 0)


def stacked(tables):
    places, blocks, at = {}, [], 0
    for name, table in tables.items():
        rows, columns = table.shape
        places[name] = (at, rows, columns)
        room = -(-rows // 16) * 16
        block = np.zeros((room, WIDE), BF)
        block[:rows, :columns] = table
        blocks.append(block)
        at += room
    return np.concatenate(blocks, 0), places


def constants():
    b, g, p = line_tables()
    kron = lambda x, y, z: np.kron(np.kron(x, y), z)
    bbb, ppp = kron(b, b, b), kron(p, p, p)
    grads = [kron(g, b, b), kron(b, g, b), kron(b, b, g)]
    r = np.abs(b).sum(1, keepdims=True)
    limit = kron(np.abs(b), np.abs(b), np.abs(b)) * kron(r, r, r)
    spread = np.kron(np.ones((LD, 1)), np.eye(LD)).astype(BF)
    collect = np.kron(np.eye(LD), np.ones((1, LD))).astype(BF)
    force = dict(
        bern_up_high=halves(ppp)[0],
        bern_up_low=halves(ppp)[1],
        bern_down_high=halves(ppp.T)[0],
        bern_down_low=halves(ppp.T)[1],
        spread=spread,
        limit=above(limit.T),
    )
    for k, t in enumerate(grads):
        force["up%d" % k] = beside(t)
        force["down%d" % k] = above(t.T)
    for k in range(0, LD * LD, 243):
        force["collect%d" % k] = collect[:, k : k + 243]
    return stacked(force), stacked(dict(up=beside(bbb), down=above(bbb.T)))


(FORCE_TABLES, FORCE_AT), (MASS_TABLES, MASS_AT) = constants()


def entry(ref, places, name):
    at, rows, columns = places[name]
    return ref[at : at + rows, :columns]


def split2(x):
    high = x.astype(BF)
    return high, (x - high.astype(F32)).astype(BF)


def split3(x):
    high = x.astype(BF)
    rest = x - high.astype(F32)
    mid = rest.astype(BF)
    return high, mid, (rest - mid.astype(F32)).astype(BF)


def dot(a, b, dims=None):
    if dims is None:
        return jnp.dot(a, b, preferred_element_type=F32)
    return lax.dot_general(a, b, dims, preferred_element_type=F32)


def up(table, x):
    high, low = split2(x)
    return dot(table, jnp.concatenate([high, low, high], 0))


def down(table, x):
    high, low = split2(x)
    half = table.shape[0] // 2
    both = dot(table, high)
    return both[:half] + both[half:] + dot(table[:half], low)


def pick(tables, chunk_of, lane_of, shape, kind=F32):
    acc = [jnp.zeros(shape, kind) for _ in tables]
    for k in range(62):
        here = chunk_of == k
        for c, row in enumerate(tables):
            got = jnp.take_along_axis(jnp.broadcast_to(row(k), shape), lane_of, axis=1)
            acc[c] = jnp.where(here, got, acc[c])
    return acc


def table_rows(ref, count):
    def row(c, k):
        return ref[c * ROWS + k // 2 : c * ROWS + k // 2 + 1, (k % 2) * HALF : (k % 2 + 1) * HALF]

    return [functools.partial(row, c) for c in range(count)]


def gather_zones(idx_ref, tab_ref, word_ref, out_ref, groups=1):
    steps = []
    for g in range(groups):
        x = tab_ref[3 * g * ROWS : 3 * (g + 1) * ROWS, :]
        scale = jnp.maximum(jnp.max(jnp.abs(x), keepdims=True), 1e-30)
        steps.append(scale * 1e-6)
        q = jnp.round(x * (1000000.0 / scale)).astype(jnp.int32) + (1 << 20)
        at = 2 * g * ROWS
        word_ref[at : at + ROWS] = (q[:ROWS] << 11) | (q[2 * ROWS :] >> 10)
        word_ref[at + ROWS : at + 2 * ROWS] = (q[ROWS : 2 * ROWS] << 11) | (q[2 * ROWS :] & 1023)

    @pl.loop(0, 8)
    def _(t):
        r0 = pl.multiple_of(t * 8, 8)
        for h in range(2):
            lanes = slice(h * HALF, (h + 1) * HALF)
            idx = idx_ref[pl.ds(r0, 8), lanes]
            words = pick(table_rows(word_ref, 2 * groups), idx >> 7, idx & 127, (8, HALF), jnp.int32)
            for g in range(groups):
                w0, w1 = words[2 * g : 2 * g + 2]
                back = (
                    lax.shift_right_logical(w0, 11),
                    lax.shift_right_logical(w1, 11),
                    ((w0 & 2047) << 10) | (w1 & 1023),
                )
                for c in range(3):
                    value = (back[c] - (1 << 20)).astype(F32) * steps[g]
                    out_ref[3 * g + c, pl.ds(r0, 8), lanes] = value


def spread_rows(idx, rows):
    here = lax.broadcasted_iota(jnp.int32, (ROWS, WIDE), 0) == (idx >> 8)
    parts = []
    for x in rows:
        high = x.astype(BF).astype(F32)
        for part in (high, x - high):
            parts.append(jnp.where(here, part, 0.0).astype(BF))
    return jnp.concatenate(parts, 0)


def scatter_tile(acc, idx, rows):
    lane = jnp.where(
        lax.broadcasted_iota(jnp.int32, (WIDE, WIDE), 0) == (idx & 255), 1.0, 0.0
    ).astype(BF)
    return acc + dot(spread_rows(idx, rows), lane, NT)


def joined(acc):
    acc = acc.reshape(acc.shape[0] // (2 * ROWS), 2, ROWS, WIDE)
    return (acc[:, 0] + acc[:, 1]).reshape(-1, WIDE)


def scatter_zones(idx_ref, lane_ref, term_ref, count):
    def eight(t, acc):
        r0 = pl.multiple_of(t * 8, 8)
        idx = idx_ref[pl.ds(r0, 8), :]
        terms = [term_ref[c, pl.ds(r0, 8), :] for c in range(count)]
        for a in range(8):
            acc = acc + dot(spread_rows(idx[a : a + 1], [x[a : a + 1] for x in terms]), lane_ref[r0 + a])
        return acc

    return joined(lax.fori_loop(0, 8, eight, jnp.zeros((2 * ROWS * count, WIDE), F32)))


def flat_row(ref, first):
    return jnp.concatenate([ref[first : first + 1, :], ref[first + 1 : first + 2, :]], 1)


def received(lists_ref, got_refs, count):
    acc = jnp.zeros((2 * ROWS * count, WIDE), F32)
    for k, got in enumerate(got_refs):
        acc = scatter_tile(acc, flat_row(lists_ref, 2 * k), [flat_row(got, 2 * c) for c in range(count)])
    return joined(acc)


def send_shared(lists_ref, tab_ref, send_refs, count):
    idx = lists_ref[...]
    got = pick(table_rows(tab_ref, count), idx >> 7, idx & 127, (8, HALF))
    for k, send in enumerate(send_refs):
        for c in range(count):
            send[2 * c : 2 * c + 2, :] = got[c][2 * k : 2 * k + 2]
        send[2 * count :, :] = jnp.zeros((16 - 2 * count, HALF), F32)


def pressure_at(en, mass, tables):
    get = functools.partial(entry, tables, FORCE_AT)
    eh, el = split2(en)
    e_q = dot(get("bern_up_high"), eh) + dot(get("bern_up_high"), el) + dot(get("bern_up_low"), eh)
    return GAMMA_LESS * e_q * mass


def force(pressure, jac_ref, tables, t_ref=None, at=0, v_ref=None, work_ref=None):
    get = functools.partial(entry, tables, FORCE_AT)
    for c in range(3):
        if v_ref is not None:
            high, low = split2(v_ref[c])
            vc = jnp.concatenate([high, low, high], 0)
        term = jnp.zeros((NPZ, WIDE), F32)
        for k in range(3):
            w = jac_ref[(3 * k + c) * QP : (3 * k + c + 1) * QP, :] * pressure
            if v_ref is not None:
                dv = dot(get("up%d" % k), vc)
                if c == 0 and k == 0:
                    work_ref[...] = w * dv
                else:
                    work_ref[...] += w * dv
            if t_ref is not None:
                term = term + down(get("down%d" % k), w)
        if t_ref is not None:
            t_ref[at + c] = term
    if v_ref is None:
        return None
    wh, wl = split2(work_ref[...])
    high, low = get("bern_down_high"), get("bern_down_low")
    return -(dot(high, wh) + dot(high, wl) + dot(low, wh))


def energy_change(rhs_e, inv_ref, tables):
    get = functools.partial(entry, tables, FORCE_AT)
    rh, rl = split2(rhs_e)
    prod = inv_ref[...] * (dot(get("spread"), rh) + dot(get("spread"), rl))
    total = jnp.zeros((LD, WIDE), F32)
    for k in range(0, LD * LD, 243):
        for part in split2(prod[k : k + 243]):
            total = total + dot(get("collect%d" % k), part)
    return total


def nodes_in(vel_ref, tab_ref):
    for c in range(3):
        for r in range(31):
            tab_ref[c * ROWS + r : c * ROWS + r + 1, :] = vel_ref[c : c + 1, r * WIDE : (r + 1) * WIDE]
        tab_ref[c * ROWS + 31 : (c + 1) * ROWS, :] = jnp.zeros((1, WIDE), F32)


def fetch(pairs, sems):
    copies = [pltpu.make_async_copy(a, b, sems.at[i]) for i, (a, b) in enumerate(pairs)]
    for copy in copies:
        copy.start()
    return copies


def split_side():
    return lax.axis_index("split")


def sent_block(k):
    s = split_side()
    return (s % 2, 1 - s % 2, 2 + s // 2, 3 - s // 2)[k]


def landing_block(k):
    s = split_side()
    return (1 - s % 2, s % 2, 3 - s // 2, 2 + s // 2)[k]


def pack_kernel(send_ref, shared_ref, jac_hbm, mass_hbm, inv_hbm, en_hbm, *refs):
    msgs, (lists, oh, jac_ref, mass_ref, inv_ref, en_ref, sems) = refs[:4], refs[4:]
    copies = fetch(
        ((mass_hbm, mass_ref), (inv_hbm, inv_ref), (en_hbm, en_ref), (jac_hbm, jac_ref)), sems
    )
    lane = lax.broadcasted_iota(jnp.int32, (1, WIDE), 1)
    for k in range(4):
        first = sent_block(k) * CAP
        for j in range(CAP):
            at = k * 8 + j if j < 8 else 32 + k
            oh[at : at + 1, :] = jnp.where(lane == send_ref[0, first + j], 1.0, 0.0)
    oh[36:40, :] = jnp.zeros((4, WIDE), F32)
    hot = oh[...].astype(BF)
    odds = (lax.axis_index("curve") % 2, split_side() % 2)
    for k in range(4):
        other = k ^ 1
        row = jnp.where(odds[k // 2] == 1, shared_ref[0, other : other + 1, :], shared_ref[0, k : k + 1, :])
        lists[2 * k : 2 * k + 1, :] = row[:, :HALF]
        lists[2 * k + 1 : 2 * k + 2, :] = row[:, HALF:]

    def put(at, n, block):
        for p in range(4):
            msgs[p][:, at : at + n] = block[p * 8 : (p + 1) * 8]
            done = 0
            while done < n:
                piece, off = divmod(at + done, TAIL)
                step = min(n - done, TAIL - off)
                msgs[p][piece : piece + 1, MSG + off : MSG + off + step] = block[
                    32 + p : 33 + p, done : done + step
                ]
                done += step

    places = ((mass_ref, AT_MASS), (inv_ref, AT_INV), (en_ref, AT_EN), (jac_ref, AT_JAC))
    for copy, (ref, at) in zip(copies, places):
        copy.wait()
        total = ref.shape[0]
        for i in range(0, total, WIDE):
            n = min(WIDE, total - i)
            parts = split3(ref[i : i + n, :])
            put(at + i, n, sum(dot(hot, part, NT) for part in parts))
    for p in range(4):
        msgs[p][:, AT_FLAG:MSG] = jnp.ones((8, MSG - AT_FLAG), F32)


def prep_kernel(vel_ref, zn_ref, _lists, _arrive, _en, _tables, vel_out, vz, lane_out, words, column):
    nodes_in(vel_ref, vel_out)
    gather_zones(zn_ref, vel_out, words, vz)
    column[:, :NPZ] = jnp.transpose((zn_ref[...] & 255).astype(F32), (1, 0))
    lane = lax.broadcasted_iota(jnp.int32, (16, WIDE), 1).astype(F32)

    @pl.loop(0, 16)
    def _(t):
        r0 = pl.multiple_of(t * 16, 16)
        rows = column[pl.ds(r0, 16), :]
        for a in range(NPZ):
            lane_out[a, pl.ds(r0, 16), :] = jnp.where(lane == rows[:, a : a + 1], 1.0, 0.0).astype(BF)


def first_kernel(
    arrive_ref, m0, m1, m2, m3, lists_ref, jac_ref, mass_ref, inv_ref, en_ref, zn_ref, tables, vz, lanes,
    jac_out, mass_out, inv_out, en_out, ehalf_out, y_out, s0, s1, s2, s3, oh, arr, terms, work,
):
    msgs = (m0, m1, m2, m3)
    lane = lax.broadcasted_iota(jnp.int32, (1, WIDE), 1)
    oh[...] = jnp.zeros(oh.shape, F32)
    for k in range(4):
        first = landing_block(k) * CAP
        flag = msgs[k][0:1, AT_FLAG : AT_FLAG + 1]
        for j in range(CAP):
            at = k * 8 + j if j < 8 else 32 + k
            oh[at : at + 1, :] = jnp.where(lane == arrive_ref[0, first + j], 1.0, 0.0) * flag
    lands = jnp.sum(oh[...], axis=0, keepdims=True) > 0.5
    hot = oh[...].astype(BF)
    hot3 = jnp.concatenate([hot, hot, hot], 0)
    for p in range(4):
        arr[p * 8 : (p + 1) * 8, :] = msgs[p][:, :MSG]
        for piece in range(7):
            n = min(TAIL, MSG - piece * TAIL)
            arr[32 + p : 33 + p, piece * TAIL : piece * TAIL + n] = msgs[p][
                piece : piece + 1, MSG : MSG + n
            ]
    arr[36:48, :] = jnp.zeros((12, MSG), F32)
    for ref, out, at in (
        (jac_ref, jac_out, AT_JAC), (mass_ref, mass_out, AT_MASS),
        (inv_ref, inv_out, AT_INV), (en_ref, en_out, AT_EN),
    ):
        total = ref.shape[0]
        for i in range(0, total, WIDE):
            n = min(WIDE, total - i)
            wide = min(WIDE, -(-n // HALF) * HALF)
            came = jnp.concatenate(split3(arr[:, at + i : at + i + wide]), 0)
            out[i : i + n, :] = jnp.where(lands, dot(came, hot3, TN)[:n], ref[i : i + n, :])
    mass = mass_out[...]
    rhs_e = force(pressure_at(en_out[...], mass, tables), jac_out, tables, terms, 0, vz, work)
    ehalf_out[...] = en_out[...] + 0.5 * STEP_SIZE * energy_change(rhs_e, inv_out, tables)
    force(pressure_at(ehalf_out[...], mass, tables), jac_out, tables, terms, 3)
    terms[6] = down(entry(tables, FORCE_AT, "limit"), mass)
    y_out[...] = scatter_zones(zn_ref, lanes, terms, 7)
    send_shared(lists_ref, y_out, (s0, s1, s2, s3), 7)


def rhos():
    rho, out = 1.0 / SIGMA, []
    for _ in range(SWEEPS):
        new = 1.0 / (2.0 * SIGMA - rho)
        out.append((new * rho, 2.0 * new / DELTA))
        rho = new
    return out


def each(x):
    return jnp.concatenate([x] * COMPONENTS, 0)


def update(y, r_ref, d_ref, a_ref, ib_ref, step):
    keep, add = rhos()[step]
    r = r_ref[...] - y
    d = keep * d_ref[...] + add * (r * each(ib_ref[...]))
    return r, d, a_ref[...] + d


def apply_mass(zn_ref, lanes, mass_ref, tables, d_ref, y_out, zone, terms, words):
    gather_zones(zn_ref, d_ref, words, zone, COMPONENTS // 3)
    for c in range(COMPONENTS):
        at_points = up(entry(tables, MASS_AT, "up"), zone[c])
        terms[c] = down(entry(tables, MASS_AT, "down"), at_points * mass_ref[...])
    y_out[...] = scatter_zones(zn_ref, lanes, terms, COMPONENTS)


def start_kernel(
    g0, g1, g2, g3, y_ref, lists, zn, lanes, mass, tables, ib, r_out, d_out, y_out, s0, s1, s2, s3, *scratch
):
    y = y_ref[...] + received(lists, (g0, g1, g2, g3), COMPONENTS + 1)
    pad = lax.broadcasted_iota(jnp.int32, (ROWS, WIDE), 0) == 31
    inv_bound = 1.0 / jnp.where(pad, 1.0, y[COMPONENTS * ROWS :])
    ib[...] = inv_bound
    r = y[: COMPONENTS * ROWS]
    r_out[...] = r
    d_out[...] = r * each(inv_bound) * (1.0 / THETA)
    apply_mass(zn, lanes, mass, tables, d_out, y_out, *scratch)
    send_shared(lists, y_out, (s0, s1, s2, s3), COMPONENTS)


def sweep_kernel(
    g0, g1, g2, g3, y_ref, r_ref, d_ref, a_ref, ib_ref, lists, zn, lanes, mass, tables,
    r_out, d_out, a_out, y_out, s0, s1, s2, s3, *scratch, step,
):
    y = y_ref[...] + received(lists, (g0, g1, g2, g3), COMPONENTS)
    r, d, a = update(y, r_ref, d_ref, a_ref, ib_ref, step)
    r_out[...] = r
    d_out[...] = d
    a_out[...] = a
    apply_mass(zn, lanes, mass, tables, d_out, y_out, *scratch)
    send_shared(lists, y_out, (s0, s1, s2, s3), COMPONENTS)


def last_kernel(
    g0, g1, g2, g3, y_ref, r_ref, d_ref, a_ref, ib_ref, lists, zn, mass, jac, inv, en, ehalf, vel, tables,
    en_out, vel_out, vhalf, vz, work, words,
):
    y = y_ref[...] + received(lists, (g0, g1, g2, g3), COMPONENTS)
    _, _, a = update(y, r_ref, d_ref, a_ref, ib_ref, SWEEPS - 1)
    vhalf[...] = vel[...] + 0.5 * STEP_SIZE * a[: 3 * ROWS]
    v = vel[...] + STEP_SIZE * a[3 * ROWS :]
    for c in range(3):
        for r in range(31):
            vel_out[c : c + 1, r * WIDE : (r + 1) * WIDE] = v[c * ROWS + r : c * ROWS + r + 1]
    gather_zones(zn, vhalf, words, vz)
    pressure = pressure_at(ehalf[...], mass[...], tables)
    rhs_e = force(pressure, jac, tables, v_ref=vz, work_ref=work)
    en_out[...] = en[...] + STEP_SIZE * energy_change(rhs_e, inv, tables)


VM = pl.BlockSpec(memory_space=pltpu.VMEM)
SM = pl.BlockSpec(memory_space=pltpu.SMEM)
HB = pl.BlockSpec(memory_space=pltpu.HBM)


def shape_of(s):
    return s if isinstance(s, jax.ShapeDtypeStruct) else jax.ShapeDtypeStruct(s, F32)


def call(kernel, args, outs, scratch=(), specs=None, limit=16, copies=0, name=None):
    scratch = [pltpu.VMEM(shape_of(s).shape, shape_of(s).dtype) for s in scratch]
    return pl.pallas_call(
        kernel,
        out_shape=[shape_of(s) for s in outs],
        in_specs=specs or [VM] * len(args),
        out_specs=[VM] * len(outs),
        scratch_shapes=scratch + ([pltpu.SemaphoreType.DMA((copies,))] if copies else []),
        compiler_params=pltpu.CompilerParams(vmem_limit_bytes=limit * 1024 * 1024),
        name=name,
    )(*args)


def paired(first, size, hop=1):
    low = [i for i in range(size - hop) if (i // hop) % 2 == first]
    return [p for i in low for p in ((i, i + hop), (i + hop, i))]


def exchange(sends):
    n_curve, n_split = lax.axis_size("curve"), lax.axis_size("split")
    return [
        lax.ppermute(sends[0], "curve", paired(0, n_curve)),
        lax.ppermute(sends[1], "curve", paired(1, n_curve)),
        lax.ppermute(sends[2], "split", paired(0, n_split)),
        lax.ppermute(sends[3], "split", paired(1, n_split)),
    ]


def per_device(velocity, energy, mass, jac, inv, send_rows, arrive_rows, zone_nodes, shared_nodes):
    force_tables, mass_tables = jnp.asarray(FORCE_TABLES), jnp.asarray(MASS_TABLES)
    devices = lax.axis_size("curve") * lax.axis_size("split")
    ints = lambda *s: jax.ShapeDtypeStruct(s, jnp.int32)
    half = lambda *s: jax.ShapeDtypeStruct(s, BF)
    node, nodes, msg = (3 * ROWS, WIDE), (COMPONENTS * ROWS, WIDE), (8, MSG + TAIL)
    fields = [(9 * QP, WIDE), (QP, WIDE), (LD * LD, WIDE), (LD, WIDE)]
    send = [(16, HALF)] * 4
    zone = lambda count: (count, NPZ, WIDE)
    words = lambda groups: ints(2 * groups * ROWS, WIDE)
    *msgs, lists = call(
        pack_kernel, (send_rows, shared_nodes, jac, mass, inv, energy), [msg] * 4 + [ints(8, HALF)],
        [(40, WIDE)] + fields, [SM, VM] + [HB] * 4, limit=61, copies=4, name="pack",
    )
    came = []
    for k, m in enumerate(msgs):
        came.append(lax.ppermute(m, AXES, paired(k % 2, devices, 1 + k // 2)))
    vel, vz, lanes = call(
        prep_kernel, (velocity, zone_nodes, lists, arrive_rows, energy, force_tables),
        [node, zone(3), half(NPZ, WIDE, WIDE)], [words(1), (WIDE, HALF)], [VM, VM, VM, SM, VM, VM], name="prep",
    )
    jac, mass, inv, en, ehalf, y, *sends = call(
        first_kernel,
        (arrive_rows, *came, lists, jac, mass, inv, energy, zone_nodes, force_tables, vz, lanes),
        fields + [(LD, WIDE), ((COMPONENTS + 1) * ROWS, WIDE)] + send,
        [(48, WIDE), (48, MSG), zone(COMPONENTS + 1), (QP, WIDE)],
        [SM] + [VM] * 13, name="force_one",
    )
    scratch = [zone(COMPONENTS), zone(COMPONENTS), words(COMPONENTS // 3)]
    tail = (lists, zone_nodes, lanes, mass, mass_tables)
    ib, r, d, y, *sends = call(
        start_kernel, (*exchange(sends), y, *tail), [(ROWS, WIDE), nodes, nodes, nodes] + send, scratch,
        name="mass_start",
    )
    a = d
    for step in range(SWEEPS - 1):
        r, d, a, y, *sends = call(
            functools.partial(sweep_kernel, step=step), (*exchange(sends), y, r, d, a, ib, *tail),
            [nodes] * 4 + send, scratch, name="mass_sweep",
        )
    energy_next, velocity_next = call(
        last_kernel,
        (*exchange(sends), y, r, d, a, ib, lists, zone_nodes, mass, jac, inv, en, ehalf, vel, force_tables),
        [(LD, WIDE), velocity.shape], [node, zone(3), (QP, WIDE), words(1)], name="force_two",
    )
    return velocity_next, energy_next


def solution(mesh):
    both = P(None, AXES)
    rows = P(AXES, None)
    return jax.shard_map(
        per_device,
        mesh=mesh,
        in_specs=(both, both, both, both, both, rows, rows, both, P(AXES, None, None)),
        out_specs=(both, both),
        check_vma=False,
    )
```

```python
import functools
import math

import jax
import jax.numpy as jnp
import numpy as np
from jax import lax
from jax.experimental import pallas as pl
from jax.experimental.pallas import tpu as pltpu
from jax.sharding import PartitionSpec as P

H1D, Q1D, L1D, SWEEPS = 4, 6, 3, 3
NPZ, QP, LD = 64, 216, 27
GAMMA_LESS = 0.4
STEP_SIZE = 0.25
THETA, DELTA = 0.575, 0.425
SIGMA = THETA / DELTA
AXES = ("curve", "split")
CAP = 9
COMPONENTS = 6
HALF = 128
WIDE = 256
ROWS = 32
AT_JAC, AT_MASS, AT_INV, AT_EN, AT_FLAG, MSG = 0, 2048, 2304, 3072, 3100, 3200
TAIL = 512
BF, F32 = jnp.bfloat16, jnp.float32
NT = (((1,), (1,)), ((), ()))
TN = (((0,), (0,)), ((), ()))


def line_tables():
    on_line = [-0.9324695142031521, -0.6612093864662645, -0.2386191860831909]
    on_line = on_line + [-v for v in reversed(on_line)]
    points = [0.5 * (v + 1.0) for v in on_line]
    lobatto = [0.5 * (v + 1.0) for v in [-1.0, -0.4472135954999579, 0.4472135954999579, 1.0]]
    value, slope, bern = np.zeros((Q1D, H1D)), np.zeros((Q1D, H1D)), np.zeros((Q1D, L1D))
    for i in range(H1D):
        others = [lobatto[j] for j in range(H1D) if j != i]
        scaling = np.prod([lobatto[i] - o for o in others])
        for q, t in enumerate(points):
            value[q, i] = np.prod([t - o for o in others]) / scaling
            slope[q, i] = sum(
                np.prod([t - others[n] for n in range(3) if n != m]) for m in range(3)
            ) / scaling
    for q, t in enumerate(points):
        for j in range(L1D):
            bern[q, j] = math.comb(2, j) * t**j * (1.0 - t) ** (2 - j)
    return [np.float32(t).astype(np.float64) for t in (value, slope, bern)]


def halves(table):
    high = table.astype(np.float32).astype(BF)
    low = (table - high.astype(np.float64)).astype(np.float32).astype(BF)
    return high, low


def beside(table):
    high, low = halves(table)
    return np.concatenate([high, high, low], 1)


def above(table):
    return np.concatenate(halves(table), 0)


def stacked(tables):
    places, blocks, at = {}, [], 0
    for name, table in tables.items():
        rows, columns = table.shape
        places[name] = (at, rows, columns)
        room = -(-rows // 16) * 16
        block = np.zeros((room, WIDE), BF)
        block[:rows, :columns] = table
        blocks.append(block)
        at += room
    return np.concatenate(blocks, 0), places


def constants():
    b, g, p = line_tables()
    kron = lambda x, y, z: np.kron(np.kron(x, y), z)
    bbb, ppp = kron(b, b, b), kron(p, p, p)
    grads = [kron(g, b, b), kron(b, g, b), kron(b, b, g)]
    r = np.abs(b).sum(1, keepdims=True)
    limit = kron(np.abs(b), np.abs(b), np.abs(b)) * kron(r, r, r)
    spread = np.kron(np.ones((LD, 1)), np.eye(LD)).astype(BF)
    collect = np.kron(np.eye(LD), np.ones((1, LD))).astype(BF)
    force = dict(
        bern_up_high=halves(ppp)[0],
        bern_up_low=halves(ppp)[1],
        bern_down_high=halves(ppp.T)[0],
        bern_down_low=halves(ppp.T)[1],
        spread=spread,
        limit=above(limit.T),
    )
    for k, t in enumerate(grads):
        force["up%d" % k] = beside(t)
        force["down%d" % k] = above(t.T)
    for k in range(0, LD * LD, 243):
        force["collect%d" % k] = collect[:, k : k + 243]
    return stacked(force), stacked(dict(up=beside(bbb), down=above(bbb.T)))


(FORCE_TABLES, FORCE_AT), (MASS_TABLES, MASS_AT) = constants()


def entry(ref, places, name):
    at, rows, columns = places[name]
    return ref[at : at + rows, :columns]


def split2(x):
    high = x.astype(BF)
    return high, (x - high.astype(F32)).astype(BF)


def split3(x):
    high = x.astype(BF)
    rest = x - high.astype(F32)
    mid = rest.astype(BF)
    return high, mid, (rest - mid.astype(F32)).astype(BF)


def dot(a, b, dims=None):
    if dims is None:
        return jnp.dot(a, b, preferred_element_type=F32)
    return lax.dot_general(a, b, dims, preferred_element_type=F32)


def up(table, x):
    high, low = split2(x)
    return dot(table, jnp.concatenate([high, low, high], 0))


def down(table, x):
    high, low = split2(x)
    half = table.shape[0] // 2
    both = dot(table, high)
    return both[:half] + both[half:] + dot(table[:half], low)


def pick(tables, chunk_of, lane_of, shape, kind=F32):
    acc = [jnp.zeros(shape, kind) for _ in tables]
    for k in range(62):
        here = chunk_of == k
        for c, row in enumerate(tables):
            got = jnp.take_along_axis(jnp.broadcast_to(row(k), shape), lane_of, axis=1)
            acc[c] = jnp.where(here, got, acc[c])
    return acc


def table_rows(ref, count):
    def row(c, k):
        return ref[c * ROWS + k // 2 : c * ROWS + k // 2 + 1, (k % 2) * HALF : (k % 2 + 1) * HALF]

    return [functools.partial(row, c) for c in range(count)]


def make_words(tab_ref, word_ref, groups):
    steps = []
    for g in range(groups):
        x = tab_ref[3 * g * ROWS : 3 * (g + 1) * ROWS, :]
        scale = jnp.maximum(jnp.max(jnp.abs(x), keepdims=True), 1e-30)
        steps.append(scale * 1e-6)
        q = jnp.round(x * (1000000.0 / scale)).astype(jnp.int32) + (1 << 20)
        at = 2 * g * ROWS
        word_ref[at : at + ROWS] = (q[:ROWS] << 11) | (q[2 * ROWS :] >> 10)
        word_ref[at + ROWS : at + 2 * ROWS] = (q[ROWS : 2 * ROWS] << 11) | (q[2 * ROWS :] & 1023)
    return steps


def gather_tile(idx_ref, word_ref, out_ref, steps, t, h):
    r0 = pl.multiple_of(t * 8, 8)
    lanes = slice(h * HALF, (h + 1) * HALF)
    idx = idx_ref[pl.ds(r0, 8), lanes]
    words = pick(table_rows(word_ref, 2 * len(steps)), idx >> 7, idx & 127, (8, HALF), jnp.int32)
    for g, step in enumerate(steps):
        w0, w1 = words[2 * g : 2 * g + 2]
        back = (
            lax.shift_right_logical(w0, 11),
            lax.shift_right_logical(w1, 11),
            ((w0 & 2047) << 10) | (w1 & 1023),
        )
        for c in range(3):
            out_ref[3 * g + c, pl.ds(r0, 8), lanes] = (back[c] - (1 << 20)).astype(F32) * step


def gather_zones(idx_ref, tab_ref, word_ref, out_ref, groups=1):
    steps = make_words(tab_ref, word_ref, groups)

    @pl.loop(0, 8)
    def _(t):
        for h in range(2):
            gather_tile(idx_ref, word_ref, out_ref, steps, t, h)


def spread_rows(idx, rows):
    here = lax.broadcasted_iota(jnp.int32, (ROWS, idx.shape[1]), 0) == (idx >> 8)
    parts = []
    for x in rows:
        high = x.astype(BF).astype(F32)
        for part in (high, x - high):
            parts.append(jnp.where(here, part, 0.0).astype(BF))
    return jnp.concatenate(parts, 0)


def scatter_tile(acc, idx, rows):
    lane = jnp.where(
        lax.broadcasted_iota(jnp.int32, (WIDE, WIDE), 0) == (idx & 255), 1.0, 0.0
    ).astype(BF)
    return acc + dot(spread_rows(idx, rows), lane, NT)


def joined(acc):
    acc = acc.reshape(acc.shape[0] // (2 * ROWS), 2, ROWS, WIDE)
    return (acc[:, 0] + acc[:, 1]).reshape(-1, WIDE)


def scatter_zones(idx_ref, lane_ref, term_ref, count):
    def eight(t, acc):
        r0 = pl.multiple_of(t * 8, 8)
        idx = idx_ref[pl.ds(r0, 8), :]
        terms = [term_ref[c, pl.ds(r0, 8), :] for c in range(count)]
        for a in range(8):
            acc = acc + dot(spread_rows(idx[a : a + 1], [x[a : a + 1] for x in terms]), lane_ref[r0 + a])
        return acc

    return joined(lax.fori_loop(0, 8, eight, jnp.zeros((2 * ROWS * count, WIDE), F32)))


def flat_row(ref, first):
    return jnp.concatenate([ref[first : first + 1, :], ref[first + 1 : first + 2, :]], 1)


def received(lists_ref, got_refs, count):
    acc = jnp.zeros((2 * ROWS * count, WIDE), F32)
    for k, got in enumerate(got_refs):
        acc = scatter_tile(acc, flat_row(lists_ref, 2 * k), [flat_row(got, 2 * c) for c in range(count)])
    return joined(acc)


def send_shared(lists_ref, tab_ref, send_refs, count):
    idx = lists_ref[...]
    got = pick(table_rows(tab_ref, count), idx >> 7, idx & 127, (8, HALF))
    for k, send in enumerate(send_refs):
        for c in range(count):
            send[2 * c : 2 * c + 2, :] = got[c][2 * k : 2 * k + 2]
        send[2 * count :, :] = jnp.zeros((16 - 2 * count, HALF), F32)


def pressure_at(en, mass, tables):
    get = functools.partial(entry, tables, FORCE_AT)
    eh, el = split2(en)
    e_q = dot(get("bern_up_high"), eh) + dot(get("bern_up_high"), el) + dot(get("bern_up_low"), eh)
    return GAMMA_LESS * e_q * mass


def force(pressure, jac_ref, tables, t_ref=None, at=0, v_ref=None, work_ref=None):
    get = functools.partial(entry, tables, FORCE_AT)
    for c in range(3):
        if v_ref is not None:
            high, low = split2(v_ref[c])
            vc = jnp.concatenate([high, low, high], 0)
        term = jnp.zeros((NPZ, WIDE), F32)
        for k in range(3):
            w = jac_ref[(3 * k + c) * QP : (3 * k + c + 1) * QP, :] * pressure
            if v_ref is not None:
                dv = dot(get("up%d" % k), vc)
                if c == 0 and k == 0:
                    work_ref[...] = w * dv
                else:
                    work_ref[...] += w * dv
            if t_ref is not None:
                term = term + down(get("down%d" % k), w)
        if t_ref is not None:
            t_ref[at + c] = term
    if v_ref is None:
        return None
    wh, wl = split2(work_ref[...])
    high, low = get("bern_down_high"), get("bern_down_low")
    return -(dot(high, wh) + dot(high, wl) + dot(low, wh))


def energy_change(rhs_e, inv_ref, tables):
    get = functools.partial(entry, tables, FORCE_AT)
    rh, rl = split2(rhs_e)
    prod = inv_ref[...] * (dot(get("spread"), rh) + dot(get("spread"), rl))
    total = jnp.zeros((LD, WIDE), F32)
    for k in range(0, LD * LD, 243):
        for part in split2(prod[k : k + 243]):
            total = total + dot(get("collect%d" % k), part)
    return total


def nodes_in(vel_ref, tab_ref):
    for c in range(3):
        for r in range(31):
            tab_ref[c * ROWS + r : c * ROWS + r + 1, :] = vel_ref[c : c + 1, r * WIDE : (r + 1) * WIDE]
        tab_ref[c * ROWS + 31 : (c + 1) * ROWS, :] = jnp.zeros((1, WIDE), F32)


def fetch(pairs, sems):
    copies = [pltpu.make_async_copy(a, b, sems.at[i]) for i, (a, b) in enumerate(pairs)]
    for copy in copies:
        copy.start()
    return copies


def split_side():
    return lax.axis_index("split")


def sent_block(k):
    s = split_side()
    return (s % 2, 1 - s % 2, 2 + s // 2, 3 - s // 2)[k]


def landing_block(k):
    s = split_side()
    return (1 - s % 2, s % 2, 3 - s // 2, 2 + s // 2)[k]


def pack_kernel(send_ref, shared_ref, jac_hbm, mass_hbm, inv_hbm, en_hbm, *refs):
    msgs, (lists, oh, jac_ref, mass_ref, inv_ref, en_ref, sems) = refs[:4], refs[4:]
    copies = fetch(
        ((mass_hbm, mass_ref), (inv_hbm, inv_ref), (en_hbm, en_ref), (jac_hbm, jac_ref)), sems
    )
    lane = lax.broadcasted_iota(jnp.int32, (1, WIDE), 1)
    for k in range(4):
        first = sent_block(k) * CAP
        for j in range(CAP):
            at = k * 8 + j if j < 8 else 32 + k
            oh[at : at + 1, :] = jnp.where(lane == send_ref[0, first + j], 1.0, 0.0)
    oh[36:40, :] = jnp.zeros((4, WIDE), F32)
    hot = oh[...].astype(BF)
    odds = (lax.axis_index("curve") % 2, split_side() % 2)
    for k in range(4):
        other = k ^ 1
        row = jnp.where(odds[k // 2] == 1, shared_ref[0, other : other + 1, :], shared_ref[0, k : k + 1, :])
        lists[2 * k : 2 * k + 1, :] = row[:, :HALF]
        lists[2 * k + 1 : 2 * k + 2, :] = row[:, HALF:]

    def put(at, n, block):
        for p in range(4):
            msgs[p][:, at : at + n] = block[p * 8 : (p + 1) * 8]
            done = 0
            while done < n:
                piece, off = divmod(at + done, TAIL)
                step = min(n - done, TAIL - off)
                msgs[p][piece : piece + 1, MSG + off : MSG + off + step] = block[
                    32 + p : 33 + p, done : done + step
                ]
                done += step

    places = ((mass_ref, AT_MASS), (inv_ref, AT_INV), (en_ref, AT_EN), (jac_ref, AT_JAC))
    for copy, (ref, at) in zip(copies, places):
        copy.wait()
        total = ref.shape[0]
        for i in range(0, total, WIDE):
            n = min(WIDE, total - i)
            parts = split3(ref[i : i + n, :])
            put(at + i, n, sum(dot(hot, part, NT) for part in parts))
    for p in range(4):
        msgs[p][:, AT_FLAG:MSG] = jnp.ones((8, MSG - AT_FLAG), F32)


def prep_kernel(vel_ref, zn_ref, _lists, _arrive, _en, _tables, vel_out, vz, lane_out, words):
    nodes_in(vel_ref, vel_out)
    gather_zones(zn_ref, vel_out, words, vz)
    down_rows = lax.broadcasted_iota(jnp.int32, (WIDE, WIDE), 0)
    eye = jnp.where(down_rows == lax.broadcasted_iota(jnp.int32, (WIDE, WIDE), 1), 1.0, 0.0).astype(BF)

    @pl.loop(0, 8)
    def _(t):
        r0 = pl.multiple_of(t * 8, 8)
        lane = zn_ref[pl.ds(r0, 8), :] & 255
        for a in range(8):
            hot = jnp.where(down_rows == lane[a : a + 1], 1.0, 0.0).astype(BF)
            lane_out[r0 + a] = dot(eye, hot, NT).astype(BF)


def first_kernel(
    arrive_ref, m0, m1, m2, m3, lists_ref, jac_ref, mass_ref, inv_ref, en_ref, zn_ref, tables, vz, lanes,
    jac_out, mass_out, inv_out, en_out, ehalf_out, y_out, s0, s1, s2, s3, oh, arr, terms, work,
):
    msgs = (m0, m1, m2, m3)
    lane = lax.broadcasted_iota(jnp.int32, (1, WIDE), 1)
    oh[...] = jnp.zeros(oh.shape, F32)
    for k in range(4):
        first = landing_block(k) * CAP
        flag = msgs[k][0:1, AT_FLAG : AT_FLAG + 1]
        for j in range(CAP):
            at = k * 8 + j if j < 8 else 32 + k
            oh[at : at + 1, :] = jnp.where(lane == arrive_ref[0, first + j], 1.0, 0.0) * flag
    lands = jnp.sum(oh[...], axis=0, keepdims=True) > 0.5
    hot = oh[...].astype(BF)
    hot3 = jnp.concatenate([hot, hot, hot], 0)
    for p in range(4):
        arr[p * 8 : (p + 1) * 8, :] = msgs[p][:, :MSG]
        for piece in range(7):
            n = min(TAIL, MSG - piece * TAIL)
            arr[32 + p : 33 + p, piece * TAIL : piece * TAIL + n] = msgs[p][
                piece : piece + 1, MSG : MSG + n
            ]
    arr[36:48, :] = jnp.zeros((12, MSG), F32)
    for ref, out, at in (
        (jac_ref, jac_out, AT_JAC), (mass_ref, mass_out, AT_MASS),
        (inv_ref, inv_out, AT_INV), (en_ref, en_out, AT_EN),
    ):
        total = ref.shape[0]
        for i in range(0, total, WIDE):
            n = min(WIDE, total - i)
            wide = min(WIDE, -(-n // HALF) * HALF)
            came = jnp.concatenate(split3(arr[:, at + i : at + i + wide]), 0)
            out[i : i + n, :] = jnp.where(lands, dot(came, hot3, TN)[:n], ref[i : i + n, :])
    mass = mass_out[...]
    rhs_e = force(pressure_at(en_out[...], mass, tables), jac_out, tables, terms, 0, vz, work)
    ehalf_out[...] = en_out[...] + 0.5 * STEP_SIZE * energy_change(rhs_e, inv_out, tables)
    force(pressure_at(ehalf_out[...], mass, tables), jac_out, tables, terms, 3)
    terms[6] = down(entry(tables, FORCE_AT, "limit"), mass)
    y_out[...] = scatter_zones(zn_ref, lanes, terms, 7)
    send_shared(lists_ref, y_out, (s0, s1, s2, s3), 7)


def rhos():
    rho, out = 1.0 / SIGMA, []
    for _ in range(SWEEPS):
        new = 1.0 / (2.0 * SIGMA - rho)
        out.append((new * rho, 2.0 * new / DELTA))
        rho = new
    return out


def each(x):
    return jnp.concatenate([x] * COMPONENTS, 0)


def update(y, r_ref, d_ref, a_ref, ib_ref, step):
    keep, add = rhos()[step]
    r = r_ref[...] - y
    d = keep * d_ref[...] + add * (r * each(ib_ref[...]))
    return r, d, a_ref[...] + d


def scatter_half(idx_ref, lane_ref, term_ref, acc_ref, t, h):
    r0 = pl.multiple_of(t * 16, 16)
    lanes = slice(h * HALF, (h + 1) * HALF)
    idx = idx_ref[pl.ds(r0, 16), lanes]
    terms = [term_ref[c, pl.ds(r0, 16), lanes] for c in range(COMPONENTS)]
    rows = [spread_rows(idx[a : a + 1], [x[a : a + 1] for x in terms]) for a in range(16)]
    hot = [lane_ref[r0 + a, lanes, :] for a in range(16)]
    acc_ref[...] += dot(jnp.concatenate(rows, 1), jnp.concatenate(hot, 0))


def zone_mass(mass_ref, tables, zone, terms, h):
    lanes = slice(h * HALF, (h + 1) * HALF)
    mass = jnp.concatenate([mass_ref[:, lanes]] * 2, 1)
    for c in range(0, COMPONENTS, 2):
        x = jnp.concatenate([zone[c, :, lanes], zone[c + 1, :, lanes]], 1)
        out = down(entry(tables, MASS_AT, "down"), up(entry(tables, MASS_AT, "up"), x) * mass)
        terms[c, :, lanes] = out[:, :HALF]
        terms[c + 1, :, lanes] = out[:, HALF:]


def apply_mass(zn_ref, lanes, mass_ref, tables, d_ref, y_out, zone, terms, words, acc):
    steps = make_words(d_ref, words, COMPONENTS // 3)
    acc[...] = jnp.zeros(acc.shape, F32)

    @pl.loop(0, 4)
    def _(t):
        gather_tile(zn_ref, words, zone, steps, 2 * t, 0)
        gather_tile(zn_ref, words, zone, steps, 2 * t + 1, 0)

    zone_mass(mass_ref, tables, zone, terms, 0)

    @pl.loop(0, 4)
    def _(t):
        scatter_half(zn_ref, lanes, terms, acc, t, 0)
        gather_tile(zn_ref, words, zone, steps, 2 * t, 1)
        gather_tile(zn_ref, words, zone, steps, 2 * t + 1, 1)

    zone_mass(mass_ref, tables, zone, terms, 1)

    @pl.loop(0, 4)
    def _(t):
        scatter_half(zn_ref, lanes, terms, acc, t, 1)

    y_out[...] = joined(acc[...])


def start_kernel(
    g0, g1, g2, g3, y_ref, lists, zn, lanes, mass, tables, ib, r_out, d_out, y_out, s0, s1, s2, s3, *scratch
):
    y = y_ref[...] + received(lists, (g0, g1, g2, g3), COMPONENTS + 1)
    pad = lax.broadcasted_iota(jnp.int32, (ROWS, WIDE), 0) == 31
    inv_bound = 1.0 / jnp.where(pad, 1.0, y[COMPONENTS * ROWS :])
    ib[...] = inv_bound
    r = y[: COMPONENTS * ROWS]
    r_out[...] = r
    d_out[...] = r * each(inv_bound) * (1.0 / THETA)
    apply_mass(zn, lanes, mass, tables, d_out, y_out, *scratch)
    send_shared(lists, y_out, (s0, s1, s2, s3), COMPONENTS)


def sweep_kernel(
    g0, g1, g2, g3, y_ref, r_ref, d_ref, a_ref, ib_ref, lists, zn, lanes, mass, tables,
    r_out, d_out, a_out, y_out, s0, s1, s2, s3, *scratch, step,
):
    y = y_ref[...] + received(lists, (g0, g1, g2, g3), COMPONENTS)
    r, d, a = update(y, r_ref, d_ref, a_ref, ib_ref, step)
    r_out[...] = r
    d_out[...] = d
    a_out[...] = a
    apply_mass(zn, lanes, mass, tables, d_out, y_out, *scratch)
    send_shared(lists, y_out, (s0, s1, s2, s3), COMPONENTS)


def last_kernel(
    g0, g1, g2, g3, y_ref, r_ref, d_ref, a_ref, ib_ref, lists, zn, mass, jac, inv, en, ehalf, vel, tables,
    en_out, vel_out, vhalf, vz, work, words,
):
    y = y_ref[...] + received(lists, (g0, g1, g2, g3), COMPONENTS)
    _, _, a = update(y, r_ref, d_ref, a_ref, ib_ref, SWEEPS - 1)
    vhalf[...] = vel[...] + 0.5 * STEP_SIZE * a[: 3 * ROWS]
    v = vel[...] + STEP_SIZE * a[3 * ROWS :]
    for c in range(3):
        for r in range(31):
            vel_out[c : c + 1, r * WIDE : (r + 1) * WIDE] = v[c * ROWS + r : c * ROWS + r + 1]
    gather_zones(zn, vhalf, words, vz)
    pressure = pressure_at(ehalf[...], mass[...], tables)
    rhs_e = force(pressure, jac, tables, v_ref=vz, work_ref=work)
    en_out[...] = en[...] + STEP_SIZE * energy_change(rhs_e, inv, tables)


VM = pl.BlockSpec(memory_space=pltpu.VMEM)
SM = pl.BlockSpec(memory_space=pltpu.SMEM)
HB = pl.BlockSpec(memory_space=pltpu.HBM)


def shape_of(s):
    return s if isinstance(s, jax.ShapeDtypeStruct) else jax.ShapeDtypeStruct(s, F32)


def call(kernel, args, outs, scratch=(), specs=None, limit=16, copies=0, name=None):
    scratch = [pltpu.VMEM(shape_of(s).shape, shape_of(s).dtype) for s in scratch]
    return pl.pallas_call(
        kernel,
        out_shape=[shape_of(s) for s in outs],
        in_specs=specs or [VM] * len(args),
        out_specs=[VM] * len(outs),
        scratch_shapes=scratch + ([pltpu.SemaphoreType.DMA((copies,))] if copies else []),
        compiler_params=pltpu.CompilerParams(vmem_limit_bytes=limit * 1024 * 1024),
        name=name,
    )(*args)


def paired(first, size, hop=1):
    low = [i for i in range(size - hop) if (i // hop) % 2 == first]
    return [p for i in low for p in ((i, i + hop), (i + hop, i))]


def exchange(sends):
    n_curve, n_split = lax.axis_size("curve"), lax.axis_size("split")
    return [
        lax.ppermute(sends[0], "curve", paired(0, n_curve)),
        lax.ppermute(sends[1], "curve", paired(1, n_curve)),
        lax.ppermute(sends[2], "split", paired(0, n_split)),
        lax.ppermute(sends[3], "split", paired(1, n_split)),
    ]


def per_device(velocity, energy, mass, jac, inv, send_rows, arrive_rows, zone_nodes, shared_nodes):
    force_tables, mass_tables = jnp.asarray(FORCE_TABLES), jnp.asarray(MASS_TABLES)
    devices = lax.axis_size("curve") * lax.axis_size("split")
    ints = lambda *s: jax.ShapeDtypeStruct(s, jnp.int32)
    half = lambda *s: jax.ShapeDtypeStruct(s, BF)
    node, nodes, msg = (3 * ROWS, WIDE), (COMPONENTS * ROWS, WIDE), (8, MSG + TAIL)
    fields = [(9 * QP, WIDE), (QP, WIDE), (LD * LD, WIDE), (LD, WIDE)]
    send = [(16, HALF)] * 4
    zone = lambda count: (count, NPZ, WIDE)
    words = lambda groups: ints(2 * groups * ROWS, WIDE)
    *msgs, lists = call(
        pack_kernel, (send_rows, shared_nodes, jac, mass, inv, energy), [msg] * 4 + [ints(8, HALF)],
        [(40, WIDE)] + fields, [SM, VM] + [HB] * 4, limit=61, copies=4, name="pack",
    )
    came = [lax.ppermute(msgs[k], AXES, paired(k % 2, devices, 1 + k // 2)) for k in (3, 2, 1, 0)][::-1]
    vel, vz, lanes = call(
        prep_kernel, (velocity, zone_nodes, lists, arrive_rows, energy, force_tables),
        [node, zone(3), half(NPZ, WIDE, WIDE)], [words(1)], [VM, VM, VM, SM, VM, VM], name="prep",
    )
    jac, mass, inv, en, ehalf, y, *sends = call(
        first_kernel,
        (arrive_rows, *came, lists, jac, mass, inv, energy, zone_nodes, force_tables, vz, lanes),
        fields + [(LD, WIDE), ((COMPONENTS + 1) * ROWS, WIDE)] + send,
        [(48, WIDE), (48, MSG), zone(COMPONENTS + 1), (QP, WIDE)],
        [SM] + [VM] * 13, name="force_one",
    )
    scratch = [zone(COMPONENTS), zone(COMPONENTS), words(COMPONENTS // 3), (2 * COMPONENTS * ROWS, WIDE)]
    tail = (lists, zone_nodes, lanes, mass, mass_tables)
    ib, r, d, y, *sends = call(
        start_kernel, (*exchange(sends), y, *tail), [(ROWS, WIDE), nodes, nodes, nodes] + send, scratch,
        name="mass_start",
    )
    a = d
    for step in range(SWEEPS - 1):
        r, d, a, y, *sends = call(
            functools.partial(sweep_kernel, step=step), (*exchange(sends), y, r, d, a, ib, *tail),
            [nodes] * 4 + send, scratch, name="mass_sweep",
        )
    energy_next, velocity_next = call(
        last_kernel,
        (*exchange(sends), y, r, d, a, ib, lists, zone_nodes, mass, jac, inv, en, ehalf, vel, force_tables),
        [(LD, WIDE), velocity.shape], [node, zone(3), (QP, WIDE), words(1)], name="force_two",
    )
    return velocity_next, energy_next


def solution(mesh):
    both = P(None, AXES)
    rows = P(AXES, None)
    return jax.shard_map(
        per_device,
        mesh=mesh,
        in_specs=(both, both, both, both, both, rows, rows, both, P(AXES, None, None)),
        out_specs=(both, both),
        check_vma=False,
    )
```

```python
import functools
import math

import jax
import jax.numpy as jnp
import numpy as np
from jax import lax
from jax.experimental import pallas as pl
from jax.experimental.pallas import tpu as pltpu
from jax.sharding import PartitionSpec as P

H1D, Q1D, L1D, SWEEPS = 4, 6, 3, 3
NPZ, QP, LD = 64, 216, 27
GAMMA_LESS = 0.4
STEP_SIZE = 0.25
THETA, DELTA = 0.575, 0.425
SIGMA = THETA / DELTA
AXES = ("curve", "split")
CAP = 9
COMPONENTS = 6
HALF = 128
WIDE = 256
ROWS = 32
AT_JAC, AT_MASS, AT_INV, AT_EN, AT_FLAG, MSG = 0, 2048, 2304, 3072, 3100, 3200
TAIL = 512
BF, F32 = jnp.bfloat16, jnp.float32
NT = (((1,), (1,)), ((), ()))
TN = (((0,), (0,)), ((), ()))


def line_tables():
    on_line = [-0.9324695142031521, -0.6612093864662645, -0.2386191860831909]
    on_line = on_line + [-v for v in reversed(on_line)]
    points = [0.5 * (v + 1.0) for v in on_line]
    lobatto = [0.5 * (v + 1.0) for v in [-1.0, -0.4472135954999579, 0.4472135954999579, 1.0]]
    value, slope, bern = np.zeros((Q1D, H1D)), np.zeros((Q1D, H1D)), np.zeros((Q1D, L1D))
    for i in range(H1D):
        others = [lobatto[j] for j in range(H1D) if j != i]
        scaling = np.prod([lobatto[i] - o for o in others])
        for q, t in enumerate(points):
            value[q, i] = np.prod([t - o for o in others]) / scaling
            slope[q, i] = sum(
                np.prod([t - others[n] for n in range(3) if n != m]) for m in range(3)
            ) / scaling
    for q, t in enumerate(points):
        for j in range(L1D):
            bern[q, j] = math.comb(2, j) * t**j * (1.0 - t) ** (2 - j)
    return [np.float32(t).astype(np.float64) for t in (value, slope, bern)]


def halves(table):
    high = table.astype(np.float32).astype(BF)
    low = (table - high.astype(np.float64)).astype(np.float32).astype(BF)
    return high, low


def beside(table):
    high, low = halves(table)
    return np.concatenate([high, high, low], 1)


def above(table):
    return np.concatenate(halves(table), 0)


def stacked(tables):
    places, blocks, at = {}, [], 0
    for name, table in tables.items():
        rows, columns = table.shape
        places[name] = (at, rows, columns)
        room = -(-rows // 16) * 16
        block = np.zeros((room, WIDE), BF)
        block[:rows, :columns] = table
        blocks.append(block)
        at += room
    return np.concatenate(blocks, 0), places


def constants():
    b, g, p = line_tables()
    kron = lambda x, y, z: np.kron(np.kron(x, y), z)
    bbb, ppp = kron(b, b, b), kron(p, p, p)
    grads = [kron(g, b, b), kron(b, g, b), kron(b, b, g)]
    r = np.abs(b).sum(1, keepdims=True)
    limit = kron(np.abs(b), np.abs(b), np.abs(b)) * kron(r, r, r)
    spread = np.kron(np.ones((LD, 1)), np.eye(LD)).astype(BF)
    collect = np.kron(np.eye(LD), np.ones((1, LD))).astype(BF)
    force = dict(
        bern_up_high=halves(ppp)[0],
        bern_up_low=halves(ppp)[1],
        bern_down_high=halves(ppp.T)[0],
        bern_down_low=halves(ppp.T)[1],
        spread=spread,
        limit=above(limit.T),
    )
    for k, t in enumerate(grads):
        force["up%d" % k] = beside(t)
        force["down%d" % k] = above(t.T)
    for k in range(0, LD * LD, 243):
        force["collect%d" % k] = collect[:, k : k + 243]
    return stacked(force), stacked(dict(up=beside(bbb), down=above(bbb.T)))


(FORCE_TABLES, FORCE_AT), (MASS_TABLES, MASS_AT) = constants()


def entry(ref, places, name):
    at, rows, columns = places[name]
    return ref[at : at + rows, :columns]


def split2(x):
    high = x.astype(BF)
    return high, (x - high.astype(F32)).astype(BF)


def split3(x):
    high = x.astype(BF)
    rest = x - high.astype(F32)
    mid = rest.astype(BF)
    return high, mid, (rest - mid.astype(F32)).astype(BF)


def dot(a, b, dims=None):
    if dims is None:
        return jnp.dot(a, b, preferred_element_type=F32)
    return lax.dot_general(a, b, dims, preferred_element_type=F32)


def up(table, x):
    high, low = split2(x)
    return dot(table, jnp.concatenate([high, low, high], 0))


def down(table, x):
    high, low = split2(x)
    half = table.shape[0] // 2
    both = dot(table, high)
    return both[:half] + both[half:] + dot(table[:half], low)


def pick(tables, chunk_of, lane_of, shape, kind=F32):
    acc = [jnp.zeros(shape, kind) for _ in tables]
    for k in range(62):
        here = chunk_of == k
        for c, row in enumerate(tables):
            got = jnp.take_along_axis(jnp.broadcast_to(row(k), shape), lane_of, axis=1)
            acc[c] = jnp.where(here, got, acc[c])
    return acc


def table_rows(ref, count):
    def row(c, k):
        return ref[c * ROWS + k // 2 : c * ROWS + k // 2 + 1, (k % 2) * HALF : (k % 2 + 1) * HALF]

    return [functools.partial(row, c) for c in range(count)]


def make_words(tab_ref, word_ref, groups):
    steps = []
    for g in range(groups):
        x = tab_ref[3 * g * ROWS : 3 * (g + 1) * ROWS, :]
        scale = jnp.maximum(jnp.max(jnp.abs(x), keepdims=True), 1e-30)
        steps.append(scale * 1e-6)
        q = jnp.round(x * (1000000.0 / scale)).astype(jnp.int32) + (1 << 20)
        at = 2 * g * ROWS
        word_ref[at : at + ROWS] = (q[:ROWS] << 11) | (q[2 * ROWS :] >> 10)
        word_ref[at + ROWS : at + 2 * ROWS] = (q[ROWS : 2 * ROWS] << 11) | (q[2 * ROWS :] & 1023)
    return steps


def gather_tile(idx_ref, word_ref, out_ref, steps, t, h):
    r0 = pl.multiple_of(t * 8, 8)
    lanes = slice(h * HALF, (h + 1) * HALF)
    idx = idx_ref[pl.ds(r0, 8), lanes]
    words = pick(table_rows(word_ref, 2 * len(steps)), idx >> 7, idx & 127, (8, HALF), jnp.int32)
    for g, step in enumerate(steps):
        w0, w1 = words[2 * g : 2 * g + 2]
        back = (
            lax.shift_right_logical(w0, 11),
            lax.shift_right_logical(w1, 11),
            ((w0 & 2047) << 10) | (w1 & 1023),
        )
        for c in range(3):
            out_ref[3 * g + c, pl.ds(r0, 8), lanes] = (back[c] - (1 << 20)).astype(F32) * step


def gather_zones(idx_ref, tab_ref, word_ref, out_ref, groups=1):
    steps = make_words(tab_ref, word_ref, groups)

    @pl.loop(0, 8)
    def _(t):
        for h in range(2):
            gather_tile(idx_ref, word_ref, out_ref, steps, t, h)


def spread_rows(idx, rows):
    here = lax.broadcasted_iota(jnp.int32, (ROWS, idx.shape[1]), 0) == (idx >> 8)
    parts = []
    for x in rows:
        high = x.astype(BF).astype(F32)
        for part in (high, x - high):
            parts.append(jnp.where(here, part, 0.0).astype(BF))
    return jnp.concatenate(parts, 0)


def scatter_tile(acc, idx, rows):
    lane = jnp.where(
        lax.broadcasted_iota(jnp.int32, (WIDE, WIDE), 0) == (idx & 255), 1.0, 0.0
    ).astype(BF)
    return acc + dot(spread_rows(idx, rows), lane, NT)


def joined(acc):
    acc = acc.reshape(acc.shape[0] // (2 * ROWS), 2, ROWS, WIDE)
    return (acc[:, 0] + acc[:, 1]).reshape(-1, WIDE)


def scatter_zones(idx_ref, lane_ref, term_ref, count):
    def eight(t, acc):
        r0 = pl.multiple_of(t * 8, 8)
        idx = idx_ref[pl.ds(r0, 8), :]
        terms = [term_ref[c, pl.ds(r0, 8), :] for c in range(count)]
        for a in range(8):
            acc = acc + dot(spread_rows(idx[a : a + 1], [x[a : a + 1] for x in terms]), lane_ref[r0 + a])
        return acc

    return joined(lax.fori_loop(0, 8, eight, jnp.zeros((2 * ROWS * count, WIDE), F32)))


def flat_row(ref, first):
    return jnp.concatenate([ref[first : first + 1, :], ref[first + 1 : first + 2, :]], 1)


def received(lists_ref, got_refs, count):
    acc = jnp.zeros((2 * ROWS * count, WIDE), F32)
    for k, got in enumerate(got_refs):
        acc = scatter_tile(acc, flat_row(lists_ref, 2 * k), [flat_row(got, 2 * c) for c in range(count)])
    return joined(acc)


def send_shared(lists_ref, tab_ref, send_refs, count):
    idx = lists_ref[...]
    got = pick(table_rows(tab_ref, count), idx >> 7, idx & 127, (8, HALF))
    for k, send in enumerate(send_refs):
        for c in range(count):
            send[2 * c : 2 * c + 2, :] = got[c][2 * k : 2 * k + 2]
        send[2 * count :, :] = jnp.zeros((16 - 2 * count, HALF), F32)


def pressure_at(en, mass, tables):
    get = functools.partial(entry, tables, FORCE_AT)
    eh, el = split2(en)
    e_q = dot(get("bern_up_high"), eh) + dot(get("bern_up_high"), el) + dot(get("bern_up_low"), eh)
    return GAMMA_LESS * e_q * mass


def force(pressure, jac_ref, tables, t_ref=None, at=0, v_ref=None, work_ref=None):
    get = functools.partial(entry, tables, FORCE_AT)
    for c in range(3):
        if v_ref is not None:
            high, low = split2(v_ref[c])
            vc = jnp.concatenate([high, low, high], 0)
        term = jnp.zeros((NPZ, WIDE), F32)
        for k in range(3):
            w = jac_ref[(3 * k + c) * QP : (3 * k + c + 1) * QP, :] * pressure
            if v_ref is not None:
                dv = dot(get("up%d" % k), vc)
                if c == 0 and k == 0:
                    work_ref[...] = w * dv
                else:
                    work_ref[...] += w * dv
            if t_ref is not None:
                term = term + down(get("down%d" % k), w)
        if t_ref is not None:
            t_ref[at + c] = term
    if v_ref is None:
        return None
    wh, wl = split2(work_ref[...])
    high, low = get("bern_down_high"), get("bern_down_low")
    return -(dot(high, wh) + dot(high, wl) + dot(low, wh))


def energy_change(rhs_e, inv_ref, tables):
    get = functools.partial(entry, tables, FORCE_AT)
    rh, rl = split2(rhs_e)
    prod = inv_ref[...] * (dot(get("spread"), rh) + dot(get("spread"), rl))
    total = jnp.zeros((LD, WIDE), F32)
    for k in range(0, LD * LD, 243):
        for part in split2(prod[k : k + 243]):
            total = total + dot(get("collect%d" % k), part)
    return total


def nodes_in(vel_ref, tab_ref):
    for c in range(3):
        for r in range(31):
            tab_ref[c * ROWS + r : c * ROWS + r + 1, :] = vel_ref[c : c + 1, r * WIDE : (r + 1) * WIDE]
        tab_ref[c * ROWS + 31 : (c + 1) * ROWS, :] = jnp.zeros((1, WIDE), F32)


def fetch(pairs, sems):
    copies = [pltpu.make_async_copy(a, b, sems.at[i]) for i, (a, b) in enumerate(pairs)]
    for copy in copies:
        copy.start()
    return copies


def split_side():
    return lax.axis_index("split")


def sent_block(k):
    s = split_side()
    return (3 - s // 2, 2 + s // 2, 1 - s % 2, s % 2)[k]


def landing_block(k):
    s = split_side()
    return (2 + s // 2, 3 - s // 2, s % 2, 1 - s % 2)[k]


def pack_kernel(send_ref, shared_ref, jac_hbm, mass_hbm, inv_hbm, en_hbm, *refs):
    msgs, (lists, oh, jac_ref, mass_ref, inv_ref, en_ref, sems) = refs[:4], refs[4:]
    chunks = [(i, min(2 * WIDE, 9 * QP - i)) for i in range(0, 9 * QP, 2 * WIDE)]
    copies = fetch(
        ((mass_hbm, mass_ref), (en_hbm, en_ref))
        + tuple((jac_hbm.at[pl.ds(i, n), :], jac_ref.at[pl.ds(i, n), :]) for i, n in chunks)
        + ((inv_hbm, inv_ref),),
        sems,
    )
    lane = lax.broadcasted_iota(jnp.int32, (1, WIDE), 1)
    for k in range(4):
        first = sent_block(k) * CAP
        for j in range(CAP):
            at = k * 8 + j if j < 8 else 32 + k
            oh[at : at + 1, :] = jnp.where(lane == send_ref[0, first + j], 1.0, 0.0)
    oh[36:40, :] = jnp.zeros((4, WIDE), F32)
    hot = oh[...].astype(BF)
    odds = (lax.axis_index("curve") % 2, split_side() % 2)
    for k in range(4):
        other = k ^ 1
        row = jnp.where(odds[k // 2] == 1, shared_ref[0, other : other + 1, :], shared_ref[0, k : k + 1, :])
        lists[2 * k : 2 * k + 1, :] = row[:, :HALF]
        lists[2 * k + 1 : 2 * k + 2, :] = row[:, HALF:]

    def put(at, n, block):
        for p in range(4):
            msgs[p][:, at : at + n] = block[p * 8 : (p + 1) * 8]
            done = 0
            while done < n:
                piece, off = divmod(at + done, TAIL)
                step = min(n - done, TAIL - off)
                msgs[p][piece : piece + 1, MSG + off : MSG + off + step] = block[
                    32 + p : 33 + p, done : done + step
                ]
                done += step

    places = [(mass_ref, AT_MASS, 0, QP), (en_ref, AT_EN, 0, LD)]
    places += [(jac_ref, AT_JAC, i, n) for i, n in chunks] + [(inv_ref, AT_INV, 0, LD * LD)]
    for copy, (ref, at, first, total) in zip(copies, places):
        copy.wait()
        for i in range(first, first + total, WIDE):
            n = min(WIDE, first + total - i)
            parts = split3(ref[i : i + n, :])
            put(at + i, n, sum(dot(hot, part, NT) for part in parts))
    for p in range(4):
        msgs[p][:, AT_FLAG:MSG] = jnp.ones((8, MSG - AT_FLAG), F32)


def prep_kernel(vel_ref, zn_ref, _lists, _arrive, _en, _tables, vel_out, vz, lane_out, words):
    nodes_in(vel_ref, vel_out)
    steps = make_words(vel_out, words, 1)
    down_rows = lax.broadcasted_iota(jnp.int32, (WIDE, WIDE), 0)
    eye = jnp.where(down_rows == lax.broadcasted_iota(jnp.int32, (WIDE, WIDE), 1), 1.0, 0.0).astype(BF)

    @pl.loop(0, 8)
    def _(t):
        r0 = pl.multiple_of(t * 8, 8)
        lane = zn_ref[pl.ds(r0, 8), :] & 255
        for a in range(8):
            hot = jnp.where(down_rows == lane[a : a + 1], 1.0, 0.0).astype(BF)
            lane_out[r0 + a] = dot(eye, hot, NT).astype(BF)
        for h in range(2):
            gather_tile(zn_ref, words, vz, steps, t, h)


def first_kernel(
    arrive_ref, m0, m1, m2, m3, lists_ref, jac_ref, mass_ref, inv_ref, en_ref, zn_ref, tables, vz, lanes,
    jac_out, mass_out, inv_out, en_out, ehalf_out, y_out, s0, s1, s2, s3, oh, arr, terms, work,
):
    msgs = (m0, m1, m2, m3)
    lane = lax.broadcasted_iota(jnp.int32, (1, WIDE), 1)
    oh[...] = jnp.zeros(oh.shape, F32)
    for k in range(4):
        first = landing_block(k) * CAP
        flag = msgs[k][0:1, AT_FLAG : AT_FLAG + 1]
        for j in range(CAP):
            at = k * 8 + j if j < 8 else 32 + k
            oh[at : at + 1, :] = jnp.where(lane == arrive_ref[0, first + j], 1.0, 0.0) * flag
    lands = jnp.sum(oh[...], axis=0, keepdims=True) > 0.5
    hot = oh[...].astype(BF)
    hot3 = jnp.concatenate([hot, hot, hot], 0)
    for p in range(4):
        arr[p * 8 : (p + 1) * 8, :] = msgs[p][:, :MSG]
        for piece in range(7):
            n = min(TAIL, MSG - piece * TAIL)
            arr[32 + p : 33 + p, piece * TAIL : piece * TAIL + n] = msgs[p][
                piece : piece + 1, MSG : MSG + n
            ]
    arr[36:48, :] = jnp.zeros((12, MSG), F32)
    for ref, out, at in (
        (jac_ref, jac_out, AT_JAC), (mass_ref, mass_out, AT_MASS),
        (inv_ref, inv_out, AT_INV), (en_ref, en_out, AT_EN),
    ):
        total = ref.shape[0]
        for i in range(0, total, WIDE):
            n = min(WIDE, total - i)
            wide = min(WIDE, -(-n // HALF) * HALF)
            came = jnp.concatenate(split3(arr[:, at + i : at + i + wide]), 0)
            out[i : i + n, :] = jnp.where(lands, dot(came, hot3, TN)[:n], ref[i : i + n, :])
    mass = mass_out[...]
    rhs_e = force(pressure_at(en_out[...], mass, tables), jac_out, tables, terms, 0, vz, work)
    ehalf_out[...] = en_out[...] + 0.5 * STEP_SIZE * energy_change(rhs_e, inv_out, tables)
    force(pressure_at(ehalf_out[...], mass, tables), jac_out, tables, terms, 3)
    terms[6] = down(entry(tables, FORCE_AT, "limit"), mass)
    y_out[...] = scatter_zones(zn_ref, lanes, terms, 7)
    send_shared(lists_ref, y_out, (s0, s1, s2, s3), 7)


def rhos():
    rho, out = 1.0 / SIGMA, []
    for _ in range(SWEEPS):
        new = 1.0 / (2.0 * SIGMA - rho)
        out.append((new * rho, 2.0 * new / DELTA))
        rho = new
    return out


def each(x):
    return jnp.concatenate([x] * COMPONENTS, 0)


def update(y, r_ref, d_ref, a_ref, ib_ref, step):
    keep, add = rhos()[step]
    r = r_ref[...] - y
    d = keep * d_ref[...] + add * (r * each(ib_ref[...]))
    return r, d, a_ref[...] + d


def scatter_half(idx_ref, lane_ref, term_ref, acc_ref, t, h):
    r0 = pl.multiple_of(t * 16, 16)
    lanes = slice(h * HALF, (h + 1) * HALF)
    idx = idx_ref[pl.ds(r0, 16), lanes]
    terms = [term_ref[c, pl.ds(r0, 16), lanes] for c in range(COMPONENTS)]
    rows = [spread_rows(idx[a : a + 1], [x[a : a + 1] for x in terms]) for a in range(16)]
    hot = [lane_ref[r0 + a, lanes, :] for a in range(16)]
    acc_ref[...] += dot(jnp.concatenate(rows, 1), jnp.concatenate(hot, 0))


def zone_mass(mass_ref, tables, zone, terms, h):
    lanes = slice(h * HALF, (h + 1) * HALF)
    mass = jnp.concatenate([mass_ref[:, lanes]] * 2, 1)
    for c in range(0, COMPONENTS, 2):
        x = jnp.concatenate([zone[c, :, lanes], zone[c + 1, :, lanes]], 1)
        out = down(entry(tables, MASS_AT, "down"), up(entry(tables, MASS_AT, "up"), x) * mass)
        terms[c, :, lanes] = out[:, :HALF]
        terms[c + 1, :, lanes] = out[:, HALF:]


def apply_mass(zn_ref, lanes, mass_ref, tables, d_ref, y_out, zone, terms, words, acc):
    steps = make_words(d_ref, words, COMPONENTS // 3)
    acc[...] = jnp.zeros(acc.shape, F32)

    @pl.loop(0, 4)
    def _(t):
        gather_tile(zn_ref, words, zone, steps, 2 * t, 0)
        gather_tile(zn_ref, words, zone, steps, 2 * t + 1, 0)

    zone_mass(mass_ref, tables, zone, terms, 0)

    @pl.loop(0, 4)
    def _(t):
        scatter_half(zn_ref, lanes, terms, acc, t, 0)
        gather_tile(zn_ref, words, zone, steps, 2 * t, 1)
        gather_tile(zn_ref, words, zone, steps, 2 * t + 1, 1)

    zone_mass(mass_ref, tables, zone, terms, 1)

    @pl.loop(0, 4)
    def _(t):
        scatter_half(zn_ref, lanes, terms, acc, t, 1)

    y_out[...] = joined(acc[...])


def start_kernel(
    g0, g1, g2, g3, y_ref, lists, zn, lanes, mass, tables, ib, r_out, d_out, y_out, s0, s1, s2, s3, *scratch
):
    y = y_ref[...] + received(lists, (g0, g1, g2, g3), COMPONENTS + 1)
    pad = lax.broadcasted_iota(jnp.int32, (ROWS, WIDE), 0) == 31
    inv_bound = 1.0 / jnp.where(pad, 1.0, y[COMPONENTS * ROWS :])
    ib[...] = inv_bound
    r = y[: COMPONENTS * ROWS]
    r_out[...] = r
    d_out[...] = r * each(inv_bound) * (1.0 / THETA)
    apply_mass(zn, lanes, mass, tables, d_out, y_out, *scratch)
    send_shared(lists, y_out, (s0, s1, s2, s3), COMPONENTS)


def sweep_kernel(
    g0, g1, g2, g3, y_ref, r_ref, d_ref, a_ref, ib_ref, lists, zn, lanes, mass, tables,
    r_out, d_out, a_out, y_out, s0, s1, s2, s3, *scratch, step,
):
    y = y_ref[...] + received(lists, (g0, g1, g2, g3), COMPONENTS)
    r, d, a = update(y, r_ref, d_ref, a_ref, ib_ref, step)
    r_out[...] = r
    d_out[...] = d
    a_out[...] = a
    apply_mass(zn, lanes, mass, tables, d_out, y_out, *scratch)
    send_shared(lists, y_out, (s0, s1, s2, s3), COMPONENTS)


def last_kernel(
    g0, g1, g2, g3, y_ref, r_ref, d_ref, a_ref, ib_ref, lists, zn, mass, jac, inv, en, ehalf, vel, tables,
    en_out, vel_out, vhalf, vz, work, words,
):
    y = y_ref[...] + received(lists, (g0, g1, g2, g3), COMPONENTS)
    _, _, a = update(y, r_ref, d_ref, a_ref, ib_ref, SWEEPS - 1)
    vhalf[...] = vel[...] + 0.5 * STEP_SIZE * a[: 3 * ROWS]
    v = vel[...] + STEP_SIZE * a[3 * ROWS :]
    for c in range(3):
        for r in range(31):
            vel_out[c : c + 1, r * WIDE : (r + 1) * WIDE] = v[c * ROWS + r : c * ROWS + r + 1]
    gather_zones(zn, vhalf, words, vz)
    pressure = pressure_at(ehalf[...], mass[...], tables)
    rhs_e = force(pressure, jac, tables, v_ref=vz, work_ref=work)
    en_out[...] = en[...] + STEP_SIZE * energy_change(rhs_e, inv, tables)


VM = pl.BlockSpec(memory_space=pltpu.VMEM)
SM = pl.BlockSpec(memory_space=pltpu.SMEM)
HB = pl.BlockSpec(memory_space=pltpu.HBM)


def shape_of(s):
    return s if isinstance(s, jax.ShapeDtypeStruct) else jax.ShapeDtypeStruct(s, F32)


def call(kernel, args, outs, scratch=(), specs=None, limit=16, copies=0, us=10, name=None):
    scratch = [pltpu.VMEM(shape_of(s).shape, shape_of(s).dtype) for s in scratch]
    return pl.pallas_call(
        kernel,
        out_shape=[shape_of(s) for s in outs],
        in_specs=specs or [VM] * len(args),
        out_specs=[VM] * len(outs),
        scratch_shapes=scratch + ([pltpu.SemaphoreType.DMA((copies,))] if copies else []),
        compiler_params=pltpu.CompilerParams(vmem_limit_bytes=limit * 1024 * 1024),
        cost_estimate=pl.CostEstimate(flops=us * 10**9, bytes_accessed=us * 10**5, transcendentals=0),
        name=name,
    )(*args)


def paired(first, size, hop=1):
    low = [i for i in range(size - hop) if (i // hop) % 2 == first]
    return [p for i in low for p in ((i, i + hop), (i + hop, i))]


def exchange(sends):
    n_curve, n_split = lax.axis_size("curve"), lax.axis_size("split")
    return [
        lax.ppermute(sends[0], "curve", paired(0, n_curve)),
        lax.ppermute(sends[1], "curve", paired(1, n_curve)),
        lax.ppermute(sends[2], "split", paired(0, n_split)),
        lax.ppermute(sends[3], "split", paired(1, n_split)),
    ]


def per_device(velocity, energy, mass, jac, inv, send_rows, arrive_rows, zone_nodes, shared_nodes):
    force_tables, mass_tables = jnp.asarray(FORCE_TABLES), jnp.asarray(MASS_TABLES)
    devices = lax.axis_size("curve") * lax.axis_size("split")
    ints = lambda *s: jax.ShapeDtypeStruct(s, jnp.int32)
    half = lambda *s: jax.ShapeDtypeStruct(s, BF)
    node, nodes, msg = (3 * ROWS, WIDE), (COMPONENTS * ROWS, WIDE), (8, MSG + TAIL)
    fields = [(9 * QP, WIDE), (QP, WIDE), (LD * LD, WIDE), (LD, WIDE)]
    send = [(16, HALF)] * 4
    zone = lambda count: (count, NPZ, WIDE)
    words = lambda groups: ints(2 * groups * ROWS, WIDE)
    *msgs, lists = call(
        pack_kernel, (send_rows, shared_nodes, jac, mass, inv, energy), [msg] * 4 + [ints(8, HALF)],
        [(40, WIDE)] + fields, [SM, VM] + [HB] * 4, limit=61, copies=7, us=4, name="pack",
    )
    rounds = ((1, 2), (0, 2), (1, 1), (0, 1))
    came = [lax.ppermute(m, AXES, paired(first, devices, hop)) for m, (first, hop) in zip(msgs, rounds)]
    vel, vz, lanes = call(
        prep_kernel, (velocity, zone_nodes, lists, arrive_rows, energy, force_tables),
        [node, zone(3), half(NPZ, WIDE, WIDE)], [words(1)], [VM, VM, VM, SM, VM, VM], name="prep",
    )
    jac, mass, inv, en, ehalf, y, *sends = call(
        first_kernel,
        (arrive_rows, *came, lists, jac, mass, inv, energy, zone_nodes, force_tables, vz, lanes),
        fields + [(LD, WIDE), ((COMPONENTS + 1) * ROWS, WIDE)] + send,
        [(48, WIDE), (48, MSG), zone(COMPONENTS + 1), (QP, WIDE)],
        [SM] + [VM] * 13, name="force_one",
    )
    scratch = [zone(COMPONENTS), zone(COMPONENTS), words(COMPONENTS // 3), (2 * COMPONENTS * ROWS, WIDE)]
    tail = (lists, zone_nodes, lanes, mass, mass_tables)
    ib, r, d, y, *sends = call(
        start_kernel, (*exchange(sends), y, *tail), [(ROWS, WIDE), nodes, nodes, nodes] + send, scratch,
        name="mass_start",
    )
    a = d
    for step in range(SWEEPS - 1):
        r, d, a, y, *sends = call(
            functools.partial(sweep_kernel, step=step), (*exchange(sends), y, r, d, a, ib, *tail),
            [nodes] * 4 + send, scratch, name="mass_sweep",
        )
    energy_next, velocity_next = call(
        last_kernel,
        (*exchange(sends), y, r, d, a, ib, lists, zone_nodes, mass, jac, inv, en, ehalf, vel, force_tables),
        [(LD, WIDE), velocity.shape], [node, zone(3), (QP, WIDE), words(1)], name="force_two",
    )
    return velocity_next, energy_next


def solution(mesh):
    both = P(None, AXES)
    rows = P(AXES, None)
    return jax.shard_map(
        per_device,
        mesh=mesh,
        in_specs=(both, both, both, both, both, rows, rows, both, P(AXES, None, None)),
        out_specs=(both, both),
        check_vma=False,
    )
```

```python
import functools
import math

import jax
import jax.numpy as jnp
import numpy as np
from jax import lax
from jax.experimental import pallas as pl
from jax.experimental.pallas import tpu as pltpu
from jax.sharding import PartitionSpec as P

H1D, Q1D, L1D, SWEEPS = 4, 6, 3, 3
NPZ, QP, LD = 64, 216, 27
GAMMA_LESS = 0.4
STEP_SIZE = 0.25
THETA, DELTA = 0.575, 0.425
SIGMA = THETA / DELTA
AXES = ("curve", "split")
CAP = 9
COMPONENTS = 6
HALF = 128
WIDE = 256
ROWS = 32
AT_JAC, AT_MASS, AT_INV, AT_EN, AT_FLAG, MSG = 0, 2048, 2304, 3072, 3100, 3200
TAIL = 512
BF, F32 = jnp.bfloat16, jnp.float32
NT = (((1,), (1,)), ((), ()))
TN = (((0,), (0,)), ((), ()))


def line_tables():
    on_line = [-0.9324695142031521, -0.6612093864662645, -0.2386191860831909]
    on_line = on_line + [-v for v in reversed(on_line)]
    points = [0.5 * (v + 1.0) for v in on_line]
    lobatto = [0.5 * (v + 1.0) for v in [-1.0, -0.4472135954999579, 0.4472135954999579, 1.0]]
    value, slope, bern = np.zeros((Q1D, H1D)), np.zeros((Q1D, H1D)), np.zeros((Q1D, L1D))
    for i in range(H1D):
        others = [lobatto[j] for j in range(H1D) if j != i]
        scaling = np.prod([lobatto[i] - o for o in others])
        for q, t in enumerate(points):
            value[q, i] = np.prod([t - o for o in others]) / scaling
            slope[q, i] = sum(
                np.prod([t - others[n] for n in range(3) if n != m]) for m in range(3)
            ) / scaling
    for q, t in enumerate(points):
        for j in range(L1D):
            bern[q, j] = math.comb(2, j) * t**j * (1.0 - t) ** (2 - j)
    return [np.float32(t).astype(np.float64) for t in (value, slope, bern)]


def halves(table):
    high = table.astype(np.float32).astype(BF)
    low = (table - high.astype(np.float64)).astype(np.float32).astype(BF)
    return high, low


def beside(table):
    high, low = halves(table)
    return np.concatenate([high, high, low], 1)


def above(table):
    return np.concatenate(halves(table), 0)


def stacked(tables):
    places, blocks, at = {}, [], 0
    for name, table in tables.items():
        rows, columns = table.shape
        places[name] = (at, rows, columns)
        room = -(-rows // 16) * 16
        block = np.zeros((room, WIDE), BF)
        block[:rows, :columns] = table
        blocks.append(block)
        at += room
    return np.concatenate(blocks, 0), places


def constants():
    b, g, p = line_tables()
    kron = lambda x, y, z: np.kron(np.kron(x, y), z)
    bbb, ppp = kron(b, b, b), kron(p, p, p)
    grads = [kron(g, b, b), kron(b, g, b), kron(b, b, g)]
    r = np.abs(b).sum(1, keepdims=True)
    limit = kron(np.abs(b), np.abs(b), np.abs(b)) * kron(r, r, r)
    spread = np.kron(np.ones((LD, 1)), np.eye(LD)).astype(BF)
    collect = np.kron(np.eye(LD), np.ones((1, LD))).astype(BF)
    force = dict(
        bern_up_high=halves(ppp)[0],
        bern_up_low=halves(ppp)[1],
        bern_down_high=halves(ppp.T)[0],
        bern_down_low=halves(ppp.T)[1],
        spread=spread,
        limit=above(limit.T),
    )
    for k, t in enumerate(grads):
        force["up%d" % k] = beside(t)
        force["down%d" % k] = above(t.T)
    for k in range(0, LD * LD, 243):
        force["collect%d" % k] = collect[:, k : k + 243]
    return stacked(force), stacked(dict(up=beside(bbb), down=above(bbb.T)))


(FORCE_TABLES, FORCE_AT), (MASS_TABLES, MASS_AT) = constants()


def entry(ref, places, name):
    at, rows, columns = places[name]
    return ref[at : at + rows, :columns]


def split2(x):
    high = x.astype(BF)
    return high, (x - high.astype(F32)).astype(BF)


def dot(a, b, dims=None):
    if dims is None:
        return jnp.dot(a, b, preferred_element_type=F32)
    return lax.dot_general(a, b, dims, preferred_element_type=F32)


def up(table, x):
    high, low = split2(x)
    return dot(table, jnp.concatenate([high, low, high], 0))


def down(table, x):
    high, low = split2(x)
    half = table.shape[0] // 2
    both = dot(table, high)
    return both[:half] + both[half:] + dot(table[:half], low)


def pick(tables, chunk_of, lane_of, shape, kind=F32):
    acc = [jnp.zeros(shape, kind) for _ in tables]
    for k in range(62):
        here = chunk_of == k
        for c, row in enumerate(tables):
            got = jnp.take_along_axis(jnp.broadcast_to(row(k), shape), lane_of, axis=1)
            acc[c] = jnp.where(here, got, acc[c])
    return acc


def table_rows(ref, count):
    def row(c, k):
        return ref[c * ROWS + k // 2 : c * ROWS + k // 2 + 1, (k % 2) * HALF : (k % 2 + 1) * HALF]

    return [functools.partial(row, c) for c in range(count)]


def make_words(tab_ref, word_ref, groups):
    steps = []
    for g in range(groups):
        x = tab_ref[3 * g * ROWS : 3 * (g + 1) * ROWS, :]
        scale = jnp.maximum(jnp.max(jnp.abs(x), keepdims=True), 1e-30)
        steps.append(scale * 1e-6)
        q = jnp.round(x * (1000000.0 / scale)).astype(jnp.int32) + (1 << 20)
        at = 2 * g * ROWS
        word_ref[at : at + ROWS] = (q[:ROWS] << 11) | (q[2 * ROWS :] >> 10)
        word_ref[at + ROWS : at + 2 * ROWS] = (q[ROWS : 2 * ROWS] << 11) | (q[2 * ROWS :] & 1023)
    return steps


def gather_tile(idx_ref, word_ref, out_ref, steps, t, h):
    r0 = pl.multiple_of(t * 8, 8)
    lanes = slice(h * HALF, (h + 1) * HALF)
    idx = idx_ref[pl.ds(r0, 8), lanes]
    words = pick(table_rows(word_ref, 2 * len(steps)), idx >> 7, idx & 127, (8, HALF), jnp.int32)
    for g, step in enumerate(steps):
        w0, w1 = words[2 * g : 2 * g + 2]
        back = (
            lax.shift_right_logical(w0, 11),
            lax.shift_right_logical(w1, 11),
            ((w0 & 2047) << 10) | (w1 & 1023),
        )
        for c in range(3):
            out_ref[3 * g + c, pl.ds(r0, 8), lanes] = (back[c] - (1 << 20)).astype(F32) * step


def gather_zones(idx_ref, tab_ref, word_ref, out_ref, groups=1):
    steps = make_words(tab_ref, word_ref, groups)

    @pl.loop(0, 8)
    def _(t):
        for h in range(2):
            gather_tile(idx_ref, word_ref, out_ref, steps, t, h)


def spread_rows(idx, rows):
    here = lax.broadcasted_iota(jnp.int32, (ROWS, idx.shape[1]), 0) == (idx >> 8)
    parts = []
    for x in rows:
        high = x.astype(BF).astype(F32)
        for part in (high, x - high):
            parts.append(jnp.where(here, part, 0.0).astype(BF))
    return jnp.concatenate(parts, 0)


def scatter_tile(acc, idx, rows):
    lane = jnp.where(
        lax.broadcasted_iota(jnp.int32, (WIDE, WIDE), 0) == (idx & 255), 1.0, 0.0
    ).astype(BF)
    return acc + dot(spread_rows(idx, rows), lane, NT)


def joined(acc):
    acc = acc.reshape(acc.shape[0] // (2 * ROWS), 2, ROWS, WIDE)
    return (acc[:, 0] + acc[:, 1]).reshape(-1, WIDE)


def add_product(acc_ref, rows, hot, step):
    rows, hot = jnp.concatenate(rows, 1), jnp.concatenate(hot, 0)
    for p in range(0, acc_ref.shape[0], step):
        acc_ref[p : p + step, :] += dot(rows[p : p + step], hot)


def scatter_zones(idx_ref, lane_ref, term_ref, acc_ref, count):
    acc_ref[...] = jnp.zeros(acc_ref.shape, F32)

    @pl.loop(0, NPZ // 16)
    def _(t):
        r0 = pl.multiple_of(t * 16, 8)
        idx = idx_ref[pl.ds(r0, 16), :]
        terms = [term_ref[c, pl.ds(r0, 16), :] for c in range(count)]
        rows = [spread_rows(idx[a : a + 1], [x[a : a + 1] for x in terms]) for a in range(16)]
        add_product(acc_ref, rows, [lane_ref[r0 + a] for a in range(16)], 224)

    return joined(acc_ref[...])


def flat_row(ref, first):
    return jnp.concatenate([ref[first : first + 1, :], ref[first + 1 : first + 2, :]], 1)


def received(lists_ref, got_refs, count):
    acc = jnp.zeros((2 * ROWS * count, WIDE), F32)
    for k, got in enumerate(got_refs):
        acc = scatter_tile(acc, flat_row(lists_ref, 2 * k), [flat_row(got, 2 * c) for c in range(count)])
    return joined(acc)


def send_shared(lists_ref, tab_ref, send_refs, count):
    idx = lists_ref[...]
    got = pick(table_rows(tab_ref, count), idx >> 7, idx & 127, (8, HALF))
    for k, send in enumerate(send_refs):
        for c in range(count):
            send[2 * c : 2 * c + 2, :] = got[c][2 * k : 2 * k + 2]
        send[2 * count :, :] = jnp.zeros((16 - 2 * count, HALF), F32)


def pressure_at(en, mass, tables):
    get = functools.partial(entry, tables, FORCE_AT)
    eh, el = split2(en)
    e_q = dot(get("bern_up_high"), eh) + dot(get("bern_up_high"), el) + dot(get("bern_up_low"), eh)
    return GAMMA_LESS * e_q * mass


def force(pressure, jac_ref, tables, t_ref=None, at=0, v_ref=None, work_ref=None):
    get = functools.partial(entry, tables, FORCE_AT)
    for c in range(3):
        if v_ref is not None:
            high, low = split2(v_ref[c])
            vc = jnp.concatenate([high, low, high], 0)
        term = jnp.zeros((NPZ, WIDE), F32)
        for k in range(3):
            w = jac_ref[(3 * k + c) * QP : (3 * k + c + 1) * QP, :] * pressure
            if v_ref is not None:
                dv = dot(get("up%d" % k), vc)
                if c == 0 and k == 0:
                    work_ref[...] = w * dv
                else:
                    work_ref[...] += w * dv
            if t_ref is not None:
                term = term + down(get("down%d" % k), w)
        if t_ref is not None:
            t_ref[at + c] = term
    if v_ref is None:
        return None
    wh, wl = split2(work_ref[...])
    high, low = get("bern_down_high"), get("bern_down_low")
    return -(dot(high, wh) + dot(high, wl) + dot(low, wh))


def energy_change(rhs_e, inv_ref, tables):
    get = functools.partial(entry, tables, FORCE_AT)
    rh, rl = split2(rhs_e)
    prod = inv_ref[...] * (dot(get("spread"), rh) + dot(get("spread"), rl))
    total = jnp.zeros((LD, WIDE), F32)
    for k in range(0, LD * LD, 243):
        for part in split2(prod[k : k + 243]):
            total = total + dot(get("collect%d" % k), part)
    return total


def nodes_in(vel_ref, tab_ref):
    for c in range(3):
        for r in range(31):
            tab_ref[c * ROWS + r : c * ROWS + r + 1, :] = vel_ref[c : c + 1, r * WIDE : (r + 1) * WIDE]
        tab_ref[c * ROWS + 31 : (c + 1) * ROWS, :] = jnp.zeros((1, WIDE), F32)


def fetch(pairs, sems):
    copies = [pltpu.make_async_copy(a, b, sems.at[i]) for i, (a, b) in enumerate(pairs)]
    for copy in copies:
        copy.start()
    return copies


def split_side():
    return lax.axis_index("split")


def sent_block(k):
    s = split_side()
    return (3 - s // 2, 2 + s // 2, 1 - s % 2, s % 2)[k]


def landing_block(k):
    s = split_side()
    return (2 + s // 2, 3 - s // 2, s % 2, 1 - s % 2)[k]


def pack_kernel(send_ref, shared_ref, jac_hbm, mass_hbm, inv_hbm, en_hbm, *refs):
    msgs, (lists, oh, jac_ref, mass_ref, inv_ref, en_ref, sems) = refs[:4], refs[4:]
    chunks = [(i, min(2 * WIDE, 9 * QP - i)) for i in range(0, 9 * QP, 2 * WIDE)]
    copies = fetch(
        ((mass_hbm, mass_ref), (en_hbm, en_ref))
        + tuple((jac_hbm.at[pl.ds(i, n), :], jac_ref.at[pl.ds(i, n), :]) for i, n in chunks)
        + ((inv_hbm, inv_ref),),
        sems,
    )
    lane = lax.broadcasted_iota(jnp.int32, (1, WIDE), 1)
    for k in range(4):
        first = sent_block(k) * CAP
        for j in range(CAP):
            at = k * 8 + j if j < 8 else 32 + k
            oh[at : at + 1, :] = jnp.where(lane == send_ref[0, first + j], 1.0, 0.0)
    oh[36:40, :] = jnp.zeros((4, WIDE), F32)
    hot = oh[...].astype(BF)
    odds = (lax.axis_index("curve") % 2, split_side() % 2)
    for k in range(4):
        other = k ^ 1
        row = jnp.where(odds[k // 2] == 1, shared_ref[0, other : other + 1, :], shared_ref[0, k : k + 1, :])
        lists[2 * k : 2 * k + 1, :] = row[:, :HALF]
        lists[2 * k + 1 : 2 * k + 2, :] = row[:, HALF:]

    def put(at, n, block):
        for p in range(4):
            msgs[p][:, at : at + n] = block[p * 8 : (p + 1) * 8]
            done = 0
            while done < n:
                piece, off = divmod(at + done, TAIL)
                step = min(n - done, TAIL - off)
                msgs[p][piece : piece + 1, MSG + off : MSG + off + step] = block[
                    32 + p : 33 + p, done : done + step
                ]
                done += step

    places = [(mass_ref, AT_MASS, 0, QP), (en_ref, AT_EN, 0, LD)]
    places += [(jac_ref, AT_JAC, i, n) for i, n in chunks] + [(inv_ref, AT_INV, 0, LD * LD)]
    for copy, (ref, at, first, total) in zip(copies, places):
        copy.wait()
        for i in range(first, first + total, WIDE):
            n = min(WIDE, first + total - i)
            parts = split2(ref[i : i + n, :])
            put(at + i, n, sum(dot(hot, part, NT) for part in parts))
    for p in range(4):
        msgs[p][:, AT_FLAG:MSG] = jnp.ones((8, MSG - AT_FLAG), F32)


def prep_kernel(vel_ref, zn_ref, _arrive, _en, _tables, vel_out, vz, lane_out, words):
    nodes_in(vel_ref, vel_out)
    steps = make_words(vel_out, words, 1)
    down_rows = lax.broadcasted_iota(jnp.int32, (WIDE, WIDE), 0)
    eye = jnp.where(down_rows == lax.broadcasted_iota(jnp.int32, (WIDE, WIDE), 1), 1.0, 0.0).astype(BF)

    @pl.loop(0, 8)
    def _(t):
        r0 = pl.multiple_of(t * 8, 8)
        lane = zn_ref[pl.ds(r0, 8), :] & 255
        for a in range(8):
            hot = jnp.where(down_rows == lane[a : a + 1], 1.0, 0.0).astype(BF)
            lane_out[r0 + a] = dot(eye, hot, NT).astype(BF)
        for h in range(2):
            gather_tile(zn_ref, words, vz, steps, t, h)


def first_kernel(
    arrive_ref, m0, m1, m2, m3, lists_ref, jac_ref, mass_ref, inv_ref, en_ref, zn_ref, tables, vz, lanes,
    jac_out, mass_out, inv_out, en_out, ehalf_out, y_out, s0, s1, s2, s3, oh, arr, terms, work, acc,
):
    msgs = (m0, m1, m2, m3)
    lane = lax.broadcasted_iota(jnp.int32, (1, WIDE), 1)
    oh[...] = jnp.zeros(oh.shape, F32)
    for k in range(4):
        first = landing_block(k) * CAP
        flag = msgs[k][0:1, AT_FLAG : AT_FLAG + 1]
        for j in range(CAP):
            at = k * 8 + j if j < 8 else 32 + k
            oh[at : at + 1, :] = jnp.where(lane == arrive_ref[0, first + j], 1.0, 0.0) * flag
    lands = jnp.sum(oh[...], axis=0, keepdims=True) > 0.5
    hot = oh[...].astype(BF)
    hot2 = jnp.concatenate([hot, hot], 0)
    for p in range(4):
        arr[p * 8 : (p + 1) * 8, :] = msgs[p][:, :MSG]
        for piece in range(7):
            n = min(TAIL, MSG - piece * TAIL)
            arr[32 + p : 33 + p, piece * TAIL : piece * TAIL + n] = msgs[p][
                piece : piece + 1, MSG : MSG + n
            ]
    arr[36:48, :] = jnp.zeros((12, MSG), F32)
    for ref, out, at in (
        (jac_ref, jac_out, AT_JAC), (mass_ref, mass_out, AT_MASS),
        (inv_ref, inv_out, AT_INV), (en_ref, en_out, AT_EN),
    ):
        total = ref.shape[0]
        for i in range(0, total, WIDE):
            n = min(WIDE, total - i)
            wide = min(WIDE, -(-n // HALF) * HALF)
            came = jnp.concatenate(split2(arr[:, at + i : at + i + wide]), 0)
            out[i : i + n, :] = jnp.where(lands, dot(came, hot2, TN)[:n], ref[i : i + n, :])
    mass = mass_out[...]
    rhs_e = force(pressure_at(en_out[...], mass, tables), jac_out, tables, terms, 0, vz, work)
    ehalf_out[...] = en_out[...] + 0.5 * STEP_SIZE * energy_change(rhs_e, inv_out, tables)
    force(pressure_at(ehalf_out[...], mass, tables), jac_out, tables, terms, 3)
    terms[6] = down(entry(tables, FORCE_AT, "limit"), mass)
    y_out[...] = scatter_zones(zn_ref, lanes, terms, acc, 7)
    send_shared(lists_ref, y_out, (s0, s1, s2, s3), 7)


def rhos():
    rho, out = 1.0 / SIGMA, []
    for _ in range(SWEEPS):
        new = 1.0 / (2.0 * SIGMA - rho)
        out.append((new * rho, 2.0 * new / DELTA))
        rho = new
    return out


def each(x):
    return jnp.concatenate([x] * COMPONENTS, 0)


def update(y, r_ref, d_ref, a_ref, ib_ref, step):
    keep, add = rhos()[step]
    r = r_ref[...] - y
    d = keep * d_ref[...] + add * (r * each(ib_ref[...]))
    return r, d, a_ref[...] + d


def scatter_half(idx_ref, lane_ref, term_ref, acc_ref, t, h):
    r0 = pl.multiple_of(t * 16, 16)
    lanes = slice(h * HALF, (h + 1) * HALF)
    idx = idx_ref[pl.ds(r0, 16), lanes]
    terms = [term_ref[c, pl.ds(r0, 16), lanes] for c in range(COMPONENTS)]
    rows = [spread_rows(idx[a : a + 1], [x[a : a + 1] for x in terms]) for a in range(16)]
    hot = [lane_ref[r0 + a, lanes, :] for a in range(16)]
    add_product(acc_ref, rows, hot, 192)


def zone_mass(mass_ref, tables, zone, terms, h):
    lanes = slice(h * HALF, (h + 1) * HALF)
    mass = jnp.concatenate([mass_ref[:, lanes]] * 2, 1)
    for c in range(0, COMPONENTS, 2):
        x = jnp.concatenate([zone[c, :, lanes], zone[c + 1, :, lanes]], 1)
        out = down(entry(tables, MASS_AT, "down"), up(entry(tables, MASS_AT, "up"), x) * mass)
        terms[c, :, lanes] = out[:, :HALF]
        terms[c + 1, :, lanes] = out[:, HALF:]


def apply_mass(zn_ref, lanes, mass_ref, tables, d_ref, y_out, zone, terms, words, acc):
    steps = make_words(d_ref, words, COMPONENTS // 3)
    acc[...] = jnp.zeros(acc.shape, F32)

    @pl.loop(0, 4)
    def _(t):
        gather_tile(zn_ref, words, zone, steps, 2 * t, 0)
        gather_tile(zn_ref, words, zone, steps, 2 * t + 1, 0)

    zone_mass(mass_ref, tables, zone, terms, 0)

    @pl.loop(0, 4)
    def _(t):
        scatter_half(zn_ref, lanes, terms, acc, t, 0)
        gather_tile(zn_ref, words, zone, steps, 2 * t, 1)
        gather_tile(zn_ref, words, zone, steps, 2 * t + 1, 1)

    zone_mass(mass_ref, tables, zone, terms, 1)

    @pl.loop(0, 4)
    def _(t):
        scatter_half(zn_ref, lanes, terms, acc, t, 1)

    y_out[...] = joined(acc[...])


def start_kernel(
    g0, g1, g2, g3, y_ref, lists, zn, lanes, mass, tables, ib, r_out, d_out, y_out, s0, s1, s2, s3, *scratch
):
    y = y_ref[...] + received(lists, (g0, g1, g2, g3), COMPONENTS + 1)
    pad = lax.broadcasted_iota(jnp.int32, (ROWS, WIDE), 0) == 31
    inv_bound = 1.0 / jnp.where(pad, 1.0, y[COMPONENTS * ROWS :])
    ib[...] = inv_bound
    r = y[: COMPONENTS * ROWS]
    r_out[...] = r
    d_out[...] = r * each(inv_bound) * (1.0 / THETA)
    apply_mass(zn, lanes, mass, tables, d_out, y_out, *scratch)
    send_shared(lists, y_out, (s0, s1, s2, s3), COMPONENTS)


def sweep_kernel(
    g0, g1, g2, g3, y_ref, r_ref, d_ref, a_ref, ib_ref, lists, zn, lanes, mass, tables,
    r_out, d_out, a_out, y_out, s0, s1, s2, s3, *scratch, step,
):
    y = y_ref[...] + received(lists, (g0, g1, g2, g3), COMPONENTS)
    r, d, a = update(y, r_ref, d_ref, a_ref, ib_ref, step)
    r_out[...] = r
    d_out[...] = d
    a_out[...] = a
    apply_mass(zn, lanes, mass, tables, d_out, y_out, *scratch)
    send_shared(lists, y_out, (s0, s1, s2, s3), COMPONENTS)


def last_kernel(
    g0, g1, g2, g3, y_ref, r_ref, d_ref, a_ref, ib_ref, lists, zn, mass, jac, inv, en, ehalf, vel, tables,
    en_out, vel_out, vhalf, vz, work, words,
):
    y = y_ref[...] + received(lists, (g0, g1, g2, g3), COMPONENTS)
    _, _, a = update(y, r_ref, d_ref, a_ref, ib_ref, SWEEPS - 1)
    vhalf[...] = vel[...] + 0.5 * STEP_SIZE * a[: 3 * ROWS]
    v = vel[...] + STEP_SIZE * a[3 * ROWS :]
    for c in range(3):
        for r in range(31):
            vel_out[c : c + 1, r * WIDE : (r + 1) * WIDE] = v[c * ROWS + r : c * ROWS + r + 1]
    gather_zones(zn, vhalf, words, vz)
    pressure = pressure_at(ehalf[...], mass[...], tables)
    rhs_e = force(pressure, jac, tables, v_ref=vz, work_ref=work)
    en_out[...] = en[...] + STEP_SIZE * energy_change(rhs_e, inv, tables)


VM = pl.BlockSpec(memory_space=pltpu.VMEM)
SM = pl.BlockSpec(memory_space=pltpu.SMEM)
HB = pl.BlockSpec(memory_space=pltpu.HBM)


def shape_of(s):
    return s if isinstance(s, jax.ShapeDtypeStruct) else jax.ShapeDtypeStruct(s, F32)


def call(kernel, args, outs, scratch=(), specs=None, limit=16, copies=0, us=10, name=None):
    scratch = [pltpu.VMEM(shape_of(s).shape, shape_of(s).dtype) for s in scratch]
    return pl.pallas_call(
        kernel,
        out_shape=[shape_of(s) for s in outs],
        in_specs=specs or [VM] * len(args),
        out_specs=[VM] * len(outs),
        scratch_shapes=scratch + ([pltpu.SemaphoreType.DMA((copies,))] if copies else []),
        compiler_params=pltpu.CompilerParams(vmem_limit_bytes=limit * 1024 * 1024),
        cost_estimate=pl.CostEstimate(flops=us * 10**9, bytes_accessed=us * 10**5, transcendentals=0),
        name=name,
    )(*args)


def paired(first, size, hop=1):
    low = [i for i in range(size - hop) if (i // hop) % 2 == first]
    return [p for i in low for p in ((i, i + hop), (i + hop, i))]


def exchange(sends):
    n_curve, n_split = lax.axis_size("curve"), lax.axis_size("split")
    return [
        lax.ppermute(sends[0], "curve", paired(0, n_curve)),
        lax.ppermute(sends[1], "curve", paired(1, n_curve)),
        lax.ppermute(sends[2], "split", paired(0, n_split)),
        lax.ppermute(sends[3], "split", paired(1, n_split)),
    ]


def per_device(velocity, energy, mass, jac, inv, send_rows, arrive_rows, zone_nodes, shared_nodes):
    force_tables, mass_tables = jnp.asarray(FORCE_TABLES), jnp.asarray(MASS_TABLES)
    devices = lax.axis_size("curve") * lax.axis_size("split")
    ints = lambda *s: jax.ShapeDtypeStruct(s, jnp.int32)
    half = lambda *s: jax.ShapeDtypeStruct(s, BF)
    node, nodes, msg = (3 * ROWS, WIDE), (COMPONENTS * ROWS, WIDE), (8, MSG + TAIL)
    fields = [(9 * QP, WIDE), (QP, WIDE), (LD * LD, WIDE), (LD, WIDE)]
    send = [(16, HALF)] * 4
    zone = lambda count: (count, NPZ, WIDE)
    words = lambda groups: ints(2 * groups * ROWS, WIDE)
    *msgs, lists = call(
        pack_kernel, (send_rows, shared_nodes, jac, mass, inv, energy), [msg] * 4 + [ints(8, HALF)],
        [(40, WIDE)] + fields, [SM, VM] + [HB] * 4, limit=61, copies=7, us=4, name="pack",
    )
    rounds = ((1, 2), (0, 2), (1, 1), (0, 1))
    came = [lax.ppermute(m, AXES, paired(first, devices, hop)) for m, (first, hop) in zip(msgs, rounds)]
    vel, vz, lanes = call(
        prep_kernel, (velocity, zone_nodes, arrive_rows, energy, force_tables),
        [node, zone(3), half(NPZ, WIDE, WIDE)], [words(1)], [VM, VM, SM, VM, VM], name="prep",
    )
    jac, mass, inv, en, ehalf, y, *sends = call(
        first_kernel,
        (arrive_rows, *came, lists, jac, mass, inv, energy, zone_nodes, force_tables, vz, lanes),
        fields + [(LD, WIDE), ((COMPONENTS + 1) * ROWS, WIDE)] + send,
        [(48, WIDE), (48, MSG), zone(COMPONENTS + 1), (QP, WIDE), (2 * (COMPONENTS + 1) * ROWS, WIDE)],
        [SM] + [VM] * 13, name="force_one",
    )
    scratch = [zone(COMPONENTS), zone(COMPONENTS), words(COMPONENTS // 3), (2 * COMPONENTS * ROWS, WIDE)]
    tail = (lists, zone_nodes, lanes, mass, mass_tables)
    ib, r, d, y, *sends = call(
        start_kernel, (*exchange(sends), y, *tail), [(ROWS, WIDE), nodes, nodes, nodes] + send, scratch,
        name="mass_start",
    )
    a = d
    for step in range(SWEEPS - 1):
        r, d, a, y, *sends = call(
            functools.partial(sweep_kernel, step=step), (*exchange(sends), y, r, d, a, ib, *tail),
            [nodes] * 4 + send, scratch, name="mass_sweep",
        )
    energy_next, velocity_next = call(
        last_kernel,
        (*exchange(sends), y, r, d, a, ib, lists, zone_nodes, mass, jac, inv, en, ehalf, vel, force_tables),
        [(LD, WIDE), velocity.shape], [node, zone(3), (QP, WIDE), words(1)], name="force_two",
    )
    return velocity_next, energy_next


def solution(mesh):
    both = P(None, AXES)
    rows = P(AXES, None)
    return jax.shard_map(
        per_device,
        mesh=mesh,
        in_specs=(both, both, both, both, both, rows, rows, both, P(AXES, None, None)),
        out_specs=(both, both),
        check_vma=False,
    )
```

```python
import functools
import math

import jax
import jax.numpy as jnp
import numpy as np
from jax import lax
from jax.experimental import pallas as pl
from jax.experimental.pallas import tpu as pltpu
from jax.sharding import PartitionSpec as P

H1D, Q1D, L1D, SWEEPS = 4, 6, 3, 3
NPZ, QP, LD = 64, 216, 27
GAMMA_LESS = 0.4
STEP_SIZE = 0.25
THETA, DELTA = 0.575, 0.425
SIGMA = THETA / DELTA
AXES = ("curve", "split")
CAP = 9
COMPONENTS = 6
HALF = 128
WIDE = 256
ROWS = 32
AT_JAC, AT_MASS, AT_INV, AT_EN, AT_FLAG, MSG = 0, 2048, 2304, 3072, 3100, 3200
TAIL = 512
BF, F32 = jnp.bfloat16, jnp.float32
NT = (((1,), (1,)), ((), ()))
TN = (((0,), (0,)), ((), ()))


def line_tables():
    on_line = [-0.9324695142031521, -0.6612093864662645, -0.2386191860831909]
    on_line = on_line + [-v for v in reversed(on_line)]
    points = [0.5 * (v + 1.0) for v in on_line]
    lobatto = [0.5 * (v + 1.0) for v in [-1.0, -0.4472135954999579, 0.4472135954999579, 1.0]]
    value, slope, bern = np.zeros((Q1D, H1D)), np.zeros((Q1D, H1D)), np.zeros((Q1D, L1D))
    for i in range(H1D):
        others = [lobatto[j] for j in range(H1D) if j != i]
        scaling = np.prod([lobatto[i] - o for o in others])
        for q, t in enumerate(points):
            value[q, i] = np.prod([t - o for o in others]) / scaling
            slope[q, i] = sum(
                np.prod([t - others[n] for n in range(3) if n != m]) for m in range(3)
            ) / scaling
    for q, t in enumerate(points):
        for j in range(L1D):
            bern[q, j] = math.comb(2, j) * t**j * (1.0 - t) ** (2 - j)
    return [np.float32(t).astype(np.float64) for t in (value, slope, bern)]


def halves(table):
    high = table.astype(np.float32).astype(BF)
    low = (table - high.astype(np.float64)).astype(np.float32).astype(BF)
    return high, low


def beside(table):
    high, low = halves(table)
    return np.concatenate([high, high, low], 1)


def above(table):
    return np.concatenate(halves(table), 0)


def stacked(tables):
    places, blocks, at = {}, [], 0
    for name, table in tables.items():
        rows, columns = table.shape
        places[name] = (at, rows, columns)
        room = -(-rows // 16) * 16
        block = np.zeros((room, WIDE), BF)
        block[:rows, :columns] = table
        blocks.append(block)
        at += room
    return np.concatenate(blocks, 0), places


def constants():
    b, g, p = line_tables()
    kron = lambda x, y, z: np.kron(np.kron(x, y), z)
    bbb, ppp = kron(b, b, b), kron(p, p, p)
    grads = [kron(g, b, b), kron(b, g, b), kron(b, b, g)]
    r = np.abs(b).sum(1, keepdims=True)
    limit = kron(np.abs(b), np.abs(b), np.abs(b)) * kron(r, r, r)
    spread = np.kron(np.ones((LD, 1)), np.eye(LD)).astype(BF)
    collect = np.kron(np.eye(LD), np.ones((1, LD))).astype(BF)
    force = dict(
        bern_up_high=halves(ppp)[0],
        bern_up_low=halves(ppp)[1],
        bern_down_high=halves(ppp.T)[0],
        bern_down_low=halves(ppp.T)[1],
        spread=spread,
        limit=above(limit.T),
    )
    for k, t in enumerate(grads):
        force["up%d" % k] = beside(t)
        force["down%d" % k] = above(t.T)
    for k in range(0, LD * LD, 243):
        force["collect%d" % k] = collect[:, k : k + 243]
    return stacked(force), stacked(dict(up=beside(bbb), down=above(bbb.T)))


(FORCE_TABLES, FORCE_AT), (MASS_TABLES, MASS_AT) = constants()


def entry(ref, places, name):
    at, rows, columns = places[name]
    return ref[at : at + rows, :columns]


def split2(x):
    high = x.astype(BF)
    return high, (x - high.astype(F32)).astype(BF)


def dot(a, b, dims=None):
    if dims is None:
        return jnp.dot(a, b, preferred_element_type=F32)
    return lax.dot_general(a, b, dims, preferred_element_type=F32)


def up(table, x):
    high, low = split2(x)
    return dot(table, jnp.concatenate([high, low, high], 0))


def down(table, x):
    high, low = split2(x)
    half = table.shape[0] // 2
    both = dot(table, high)
    return both[:half] + both[half:] + dot(table[:half], low)


def pick(tables, chunk_of, lane_of, shape, kind=F32):
    acc = [jnp.zeros(shape, kind) for _ in tables]
    for k in range(62):
        here = chunk_of == k
        for c, row in enumerate(tables):
            got = jnp.take_along_axis(jnp.broadcast_to(row(k), shape), lane_of, axis=1)
            acc[c] = jnp.where(here, got, acc[c])
    return acc


def table_rows(ref, count):
    def row(c, k):
        return ref[c * ROWS + k // 2 : c * ROWS + k // 2 + 1, (k % 2) * HALF : (k % 2 + 1) * HALF]

    return [functools.partial(row, c) for c in range(count)]


def make_words(tab_ref, word_ref, groups):
    steps = []
    for g in range(groups):
        x = tab_ref[3 * g * ROWS : 3 * (g + 1) * ROWS, :]
        scale = jnp.maximum(jnp.max(jnp.abs(x), keepdims=True), 1e-30)
        steps.append(scale * 1e-6)
        q = jnp.round(x * (1000000.0 / scale)).astype(jnp.int32) + (1 << 20)
        at = 2 * g * ROWS
        word_ref[at : at + ROWS] = (q[:ROWS] << 11) | (q[2 * ROWS :] >> 10)
        word_ref[at + ROWS : at + 2 * ROWS] = (q[ROWS : 2 * ROWS] << 11) | (q[2 * ROWS :] & 1023)
    return steps


def gather_tile(idx_ref, word_ref, out_ref, steps, t, h):
    r0 = pl.multiple_of(t * 8, 8)
    lanes = slice(h * HALF, (h + 1) * HALF)
    idx = idx_ref[pl.ds(r0, 8), lanes]
    words = pick(table_rows(word_ref, 2 * len(steps)), idx >> 7, idx & 127, (8, HALF), jnp.int32)
    for g, step in enumerate(steps):
        w0, w1 = words[2 * g : 2 * g + 2]
        back = (
            lax.shift_right_logical(w0, 11),
            lax.shift_right_logical(w1, 11),
            ((w0 & 2047) << 10) | (w1 & 1023),
        )
        for c in range(3):
            out_ref[3 * g + c, pl.ds(r0, 8), lanes] = (back[c] - (1 << 20)).astype(F32) * step


def gather_zones(idx_ref, tab_ref, word_ref, out_ref, groups=1):
    steps = make_words(tab_ref, word_ref, groups)

    @pl.loop(0, 8)
    def _(t):
        for h in range(2):
            gather_tile(idx_ref, word_ref, out_ref, steps, t, h)


def spread_rows(idx, rows):
    here = lax.broadcasted_iota(jnp.int32, (ROWS, idx.shape[1]), 0) == (idx >> 8)
    parts = []
    for x in rows:
        high = x.astype(BF).astype(F32)
        for part in (high, x - high):
            parts.append(jnp.where(here, part, 0.0).astype(BF))
    return jnp.concatenate(parts, 0)


def scatter_tile(acc, idx, rows):
    lane = jnp.where(
        lax.broadcasted_iota(jnp.int32, (WIDE, WIDE), 0) == (idx & 255), 1.0, 0.0
    ).astype(BF)
    return acc + dot(spread_rows(idx, rows), lane, NT)


def joined(acc):
    acc = acc.reshape(acc.shape[0] // (2 * ROWS), 2, ROWS, WIDE)
    return (acc[:, 0] + acc[:, 1]).reshape(-1, WIDE)


def add_product(acc_ref, rows, hot, step):
    rows, hot = jnp.concatenate(rows, 1), jnp.concatenate(hot, 0)
    for p in range(0, acc_ref.shape[0], step):
        acc_ref[p : p + step, :] += dot(rows[p : p + step], hot)


def scatter_zones(idx_ref, lane_ref, term_ref, acc_ref, count):
    acc_ref[...] = jnp.zeros(acc_ref.shape, F32)

    @pl.loop(0, NPZ // 16)
    def _(t):
        r0 = pl.multiple_of(t * 16, 8)
        idx = idx_ref[pl.ds(r0, 16), :]
        terms = [term_ref[c, pl.ds(r0, 16), :] for c in range(count)]
        rows = [spread_rows(idx[a : a + 1], [x[a : a + 1] for x in terms]) for a in range(16)]
        add_product(acc_ref, rows, [lane_ref[r0 + a] for a in range(16)], 224)

    return joined(acc_ref[...])


def flat_row(ref, first):
    return jnp.concatenate([ref[first : first + 1, :], ref[first + 1 : first + 2, :]], 1)


def received(lists_ref, got_refs, count):
    acc = jnp.zeros((2 * ROWS * count, WIDE), F32)
    for k, got in enumerate(got_refs):
        acc = scatter_tile(acc, flat_row(lists_ref, 2 * k), [flat_row(got, 2 * c) for c in range(count)])
    return joined(acc)


def send_shared(lists_ref, tab_ref, send_refs, count):
    idx = lists_ref[...]
    got = pick(table_rows(tab_ref, count), idx >> 7, idx & 127, (8, HALF))
    for k, send in enumerate(send_refs):
        for c in range(count):
            send[2 * c : 2 * c + 2, :] = got[c][2 * k : 2 * k + 2]
        send[2 * count :, :] = jnp.zeros((16 - 2 * count, HALF), F32)


def pressure_at(en, mass, tables):
    get = functools.partial(entry, tables, FORCE_AT)
    eh, el = split2(en)
    e_q = dot(get("bern_up_high"), eh) + dot(get("bern_up_high"), el) + dot(get("bern_up_low"), eh)
    return GAMMA_LESS * e_q * mass


def force(pressure, jac_ref, tables, t_ref=None, at=0, v_ref=None, work_ref=None):
    get = functools.partial(entry, tables, FORCE_AT)
    for c in range(3):
        if v_ref is not None:
            high, low = split2(v_ref[c])
            vc = jnp.concatenate([high, low, high], 0)
        term = jnp.zeros((NPZ, WIDE), F32)
        for k in range(3):
            w = jac_ref[(3 * k + c) * QP : (3 * k + c + 1) * QP, :] * pressure
            if v_ref is not None:
                dv = dot(get("up%d" % k), vc)
                if c == 0 and k == 0:
                    work_ref[...] = w * dv
                else:
                    work_ref[...] += w * dv
            if t_ref is not None:
                term = term + down(get("down%d" % k), w)
        if t_ref is not None:
            t_ref[at + c] = term
    if v_ref is None:
        return None
    wh, wl = split2(work_ref[...])
    high, low = get("bern_down_high"), get("bern_down_low")
    return -(dot(high, wh) + dot(high, wl) + dot(low, wh))


def energy_change(rhs_e, inv_ref, tables):
    get = functools.partial(entry, tables, FORCE_AT)
    rh, rl = split2(rhs_e)
    prod = inv_ref[...] * (dot(get("spread"), rh) + dot(get("spread"), rl))
    total = jnp.zeros((LD, WIDE), F32)
    for k in range(0, LD * LD, 243):
        for part in split2(prod[k : k + 243]):
            total = total + dot(get("collect%d" % k), part)
    return total


def nodes_in(vel_ref, tab_ref):
    for c in range(3):
        for r in range(31):
            tab_ref[c * ROWS + r : c * ROWS + r + 1, :] = vel_ref[c : c + 1, r * WIDE : (r + 1) * WIDE]
        tab_ref[c * ROWS + 31 : (c + 1) * ROWS, :] = jnp.zeros((1, WIDE), F32)


def fetch(pairs, sems):
    copies = [pltpu.make_async_copy(a, b, sems.at[i]) for i, (a, b) in enumerate(pairs)]
    for copy in copies:
        copy.start()
    return copies


def split_side():
    return lax.axis_index("split")


def sent_block(k):
    s = split_side()
    return (3 - s // 2, 2 + s // 2, 1 - s % 2, s % 2)[k]


def landing_block(k):
    s = split_side()
    return (2 + s // 2, 3 - s // 2, s % 2, 1 - s % 2)[k]


def pack_kernel(send_ref, shared_ref, jac_hbm, mass_hbm, inv_hbm, en_hbm, *refs):
    msgs, (lists, oh, jac_ref, mass_ref, inv_ref, en_ref, sems) = refs[:4], refs[4:]
    chunks = [(i, min(2 * WIDE, 9 * QP - i)) for i in range(0, 9 * QP, 2 * WIDE)]
    copies = fetch(
        ((mass_hbm, mass_ref), (en_hbm, en_ref))
        + tuple((jac_hbm.at[pl.ds(i, n), :], jac_ref.at[pl.ds(i, n), :]) for i, n in chunks)
        + ((inv_hbm, inv_ref),),
        sems,
    )
    lane = lax.broadcasted_iota(jnp.int32, (1, WIDE), 1)
    for k in range(4):
        first = sent_block(k) * CAP
        for j in range(CAP):
            at = k * 8 + j if j < 8 else 32 + k
            oh[at : at + 1, :] = jnp.where(lane == send_ref[0, first + j], 1.0, 0.0)
    oh[36:40, :] = jnp.zeros((4, WIDE), F32)
    hot = oh[...].astype(BF)
    odds = (lax.axis_index("curve") % 2, split_side() % 2)
    for k in range(4):
        other = k ^ 1
        row = jnp.where(odds[k // 2] == 1, shared_ref[0, other : other + 1, :], shared_ref[0, k : k + 1, :])
        lists[2 * k : 2 * k + 1, :] = row[:, :HALF]
        lists[2 * k + 1 : 2 * k + 2, :] = row[:, HALF:]

    def put(at, n, block):
        for p in range(4):
            msgs[p][:, at : at + n] = block[p * 8 : (p + 1) * 8]
            done = 0
            while done < n:
                piece, off = divmod(at + done, TAIL)
                step = min(n - done, TAIL - off)
                msgs[p][piece : piece + 1, MSG + off : MSG + off + step] = block[
                    32 + p : 33 + p, done : done + step
                ]
                done += step

    places = [(mass_ref, AT_MASS, 0, QP), (en_ref, AT_EN, 0, LD)]
    places += [(jac_ref, AT_JAC, i, n) for i, n in chunks] + [(inv_ref, AT_INV, 0, LD * LD)]
    for copy, (ref, at, first, total) in zip(copies, places):
        copy.wait()
        for i in range(first, first + total, WIDE):
            n = min(WIDE, first + total - i)
            parts = split2(ref[i : i + n, :])
            put(at + i, n, sum(dot(hot, part, NT) for part in parts))
    for p in range(4):
        msgs[p][:, AT_FLAG:MSG] = jnp.ones((8, MSG - AT_FLAG), F32)


def prep_kernel(vel_ref, zn_ref, _arrive, _en, _tables, vel_out, vz, lane_out, words):
    nodes_in(vel_ref, vel_out)
    steps = make_words(vel_out, words, 1)
    down_rows = lax.broadcasted_iota(jnp.int32, (WIDE, WIDE), 0)
    eye = jnp.where(down_rows == lax.broadcasted_iota(jnp.int32, (WIDE, WIDE), 1), 1.0, 0.0).astype(BF)

    @pl.loop(0, 8)
    def _(t):
        r0 = pl.multiple_of(t * 8, 8)
        lane = zn_ref[pl.ds(r0, 8), :] & 255
        for a in range(8):
            hot = jnp.where(down_rows == lane[a : a + 1], 1.0, 0.0).astype(BF)
            lane_out[r0 + a] = dot(eye, hot, NT).astype(BF)
        for h in range(2):
            gather_tile(zn_ref, words, vz, steps, t, h)


def first_kernel(
    arrive_ref, m0, m1, m2, m3, lists_ref, jac_ref, mass_ref, inv_ref, en_ref, zn_ref, tables, vz, lanes,
    jac_out, mass_out, inv_out, en_out, ehalf_out, y_out, s0, s1, s2, s3, oh, arr, terms, work, acc,
):
    msgs = (m0, m1, m2, m3)
    lane = lax.broadcasted_iota(jnp.int32, (1, WIDE), 1)
    oh[...] = jnp.zeros(oh.shape, F32)
    for k in range(4):
        first = landing_block(k) * CAP
        flag = msgs[k][0:1, AT_FLAG : AT_FLAG + 1]
        for j in range(CAP):
            at = k * 8 + j if j < 8 else 32 + k
            oh[at : at + 1, :] = jnp.where(lane == arrive_ref[0, first + j], 1.0, 0.0) * flag
    lands = jnp.sum(oh[...], axis=0, keepdims=True) > 0.5
    hot = oh[...].astype(BF)
    hot2 = jnp.concatenate([hot, hot], 0)
    for p in range(4):
        arr[p * 8 : (p + 1) * 8, :] = msgs[p][:, :MSG]
        for piece in range(7):
            n = min(TAIL, MSG - piece * TAIL)
            arr[32 + p : 33 + p, piece * TAIL : piece * TAIL + n] = msgs[p][
                piece : piece + 1, MSG : MSG + n
            ]
    arr[36:48, :] = jnp.zeros((12, MSG), F32)
    for ref, out, at in (
        (jac_ref, jac_out, AT_JAC), (mass_ref, mass_out, AT_MASS),
        (inv_ref, inv_out, AT_INV), (en_ref, en_out, AT_EN),
    ):
        total = ref.shape[0]
        for i in range(0, total, WIDE):
            n = min(WIDE, total - i)
            wide = min(WIDE, -(-n // HALF) * HALF)
            came = jnp.concatenate(split2(arr[:, at + i : at + i + wide]), 0)
            out[i : i + n, :] = jnp.where(lands, dot(came, hot2, TN)[:n], ref[i : i + n, :])
    mass = mass_out[...]
    rhs_e = force(pressure_at(en_out[...], mass, tables), jac_out, tables, terms, 0, vz, work)
    ehalf_out[...] = en_out[...] + 0.5 * STEP_SIZE * energy_change(rhs_e, inv_out, tables)
    force(pressure_at(ehalf_out[...], mass, tables), jac_out, tables, terms, 3)
    terms[6] = down(entry(tables, FORCE_AT, "limit"), mass)
    y_out[...] = scatter_zones(zn_ref, lanes, terms, acc, 7)
    send_shared(lists_ref, y_out, (s0, s1, s2, s3), 7)


def rhos():
    rho, out = 1.0 / SIGMA, []
    for _ in range(SWEEPS):
        new = 1.0 / (2.0 * SIGMA - rho)
        out.append((new * rho, 2.0 * new / DELTA))
        rho = new
    return out


def each(x):
    return jnp.concatenate([x] * COMPONENTS, 0)


def update(y, r_ref, d_ref, a_ref, ib_ref, step):
    keep, add = rhos()[step]
    r = r_ref[...] - y
    d = keep * d_ref[...] + add * (r * each(ib_ref[...]))
    return r, d, a_ref[...] + d


def scatter_half(idx_ref, lane_ref, term_ref, acc_ref, t, h):
    r0 = pl.multiple_of(t * 16, 16)
    lanes = slice(h * HALF, (h + 1) * HALF)
    idx = idx_ref[pl.ds(r0, 16), lanes]
    terms = [term_ref[c, pl.ds(r0, 16), lanes] for c in range(COMPONENTS)]
    rows = [spread_rows(idx[a : a + 1], [x[a : a + 1] for x in terms]) for a in range(16)]
    hot = [lane_ref[r0 + a, lanes, :] for a in range(16)]
    add_product(acc_ref, rows, hot, 192)


def zone_mass(mass_ref, tables, zone, terms, h):
    lanes = slice(h * HALF, (h + 1) * HALF)
    mass = jnp.concatenate([mass_ref[:, lanes]] * 2, 1)
    pairs = range(0, COMPONENTS, 2)
    xs = [jnp.concatenate([zone[c, :, lanes], zone[c + 1, :, lanes]], 1) for c in pairs]
    at_points = [up(entry(tables, MASS_AT, "up"), x) * mass for x in xs]
    outs = [down(entry(tables, MASS_AT, "down"), x) for x in at_points]
    for c, out in zip(pairs, outs):
        terms[c, :, lanes] = out[:, :HALF]
        terms[c + 1, :, lanes] = out[:, HALF:]


def apply_mass(zn_ref, lanes, mass_ref, tables, d_ref, y_out, zone, terms, words, acc):
    steps = make_words(d_ref, words, COMPONENTS // 3)
    acc[...] = jnp.zeros(acc.shape, F32)

    @pl.loop(0, 4)
    def _(t):
        gather_tile(zn_ref, words, zone, steps, 2 * t, 0)
        gather_tile(zn_ref, words, zone, steps, 2 * t + 1, 0)

    zone_mass(mass_ref, tables, zone, terms, 0)

    @pl.loop(0, 4)
    def _(t):
        scatter_half(zn_ref, lanes, terms, acc, t, 0)
        gather_tile(zn_ref, words, zone, steps, 2 * t, 1)
        gather_tile(zn_ref, words, zone, steps, 2 * t + 1, 1)

    zone_mass(mass_ref, tables, zone, terms, 1)

    @pl.loop(0, 4)
    def _(t):
        scatter_half(zn_ref, lanes, terms, acc, t, 1)

    y_out[...] = joined(acc[...])


def start_kernel(
    g0, g1, g2, g3, y_ref, lists, zn, lanes, mass, tables, ib, r_out, d_out, y_out, s0, s1, s2, s3, *scratch
):
    y = y_ref[...] + received(lists, (g0, g1, g2, g3), COMPONENTS + 1)
    pad = lax.broadcasted_iota(jnp.int32, (ROWS, WIDE), 0) == 31
    inv_bound = 1.0 / jnp.where(pad, 1.0, y[COMPONENTS * ROWS :])
    ib[...] = inv_bound
    r = y[: COMPONENTS * ROWS]
    r_out[...] = r
    d_out[...] = r * each(inv_bound) * (1.0 / THETA)
    apply_mass(zn, lanes, mass, tables, d_out, y_out, *scratch)
    send_shared(lists, y_out, (s0, s1, s2, s3), COMPONENTS)


def sweep_kernel(
    g0, g1, g2, g3, y_ref, r_ref, d_ref, a_ref, ib_ref, lists, zn, lanes, mass, tables,
    r_out, d_out, a_out, y_out, s0, s1, s2, s3, *scratch, step,
):
    y = y_ref[...] + received(lists, (g0, g1, g2, g3), COMPONENTS)
    r, d, a = update(y, r_ref, d_ref, a_ref, ib_ref, step)
    r_out[...] = r
    d_out[...] = d
    a_out[...] = a
    apply_mass(zn, lanes, mass, tables, d_out, y_out, *scratch)
    send_shared(lists, y_out, (s0, s1, s2, s3), COMPONENTS)


def last_kernel(
    g0, g1, g2, g3, y_ref, r_ref, d_ref, a_ref, ib_ref, lists, zn, mass, jac, inv, en, ehalf, vel, tables,
    en_out, vel_out, vhalf, vz, work, words,
):
    y = y_ref[...] + received(lists, (g0, g1, g2, g3), COMPONENTS)
    _, _, a = update(y, r_ref, d_ref, a_ref, ib_ref, SWEEPS - 1)
    vhalf[...] = vel[...] + 0.5 * STEP_SIZE * a[: 3 * ROWS]
    v = vel[...] + STEP_SIZE * a[3 * ROWS :]
    for c in range(3):
        for r in range(31):
            vel_out[c : c + 1, r * WIDE : (r + 1) * WIDE] = v[c * ROWS + r : c * ROWS + r + 1]
    gather_zones(zn, vhalf, words, vz)
    pressure = pressure_at(ehalf[...], mass[...], tables)
    rhs_e = force(pressure, jac, tables, v_ref=vz, work_ref=work)
    en_out[...] = en[...] + STEP_SIZE * energy_change(rhs_e, inv, tables)


VM = pl.BlockSpec(memory_space=pltpu.VMEM)
SM = pl.BlockSpec(memory_space=pltpu.SMEM)
HB = pl.BlockSpec(memory_space=pltpu.HBM)


def shape_of(s):
    return s if isinstance(s, jax.ShapeDtypeStruct) else jax.ShapeDtypeStruct(s, F32)


def call(kernel, args, outs, scratch=(), specs=None, limit=16, copies=0, us=10, name=None):
    scratch = [pltpu.VMEM(shape_of(s).shape, shape_of(s).dtype) for s in scratch]
    return pl.pallas_call(
        kernel,
        out_shape=[shape_of(s) for s in outs],
        in_specs=specs or [VM] * len(args),
        out_specs=[VM] * len(outs),
        scratch_shapes=scratch + ([pltpu.SemaphoreType.DMA((copies,))] if copies else []),
        compiler_params=pltpu.CompilerParams(vmem_limit_bytes=limit * 1024 * 1024),
        cost_estimate=pl.CostEstimate(flops=us * 10**9, bytes_accessed=us * 10**5, transcendentals=0),
        name=name,
    )(*args)


def paired(first, size, hop=1):
    low = [i for i in range(size - hop) if (i // hop) % 2 == first]
    return [p for i in low for p in ((i, i + hop), (i + hop, i))]


def exchange(sends):
    n_curve, n_split = lax.axis_size("curve"), lax.axis_size("split")
    return [
        lax.ppermute(sends[0], "curve", paired(0, n_curve)),
        lax.ppermute(sends[1], "curve", paired(1, n_curve)),
        lax.ppermute(sends[2], "split", paired(0, n_split)),
        lax.ppermute(sends[3], "split", paired(1, n_split)),
    ]


def per_device(velocity, energy, mass, jac, inv, send_rows, arrive_rows, zone_nodes, shared_nodes):
    force_tables, mass_tables = jnp.asarray(FORCE_TABLES), jnp.asarray(MASS_TABLES)
    devices = lax.axis_size("curve") * lax.axis_size("split")
    ints = lambda *s: jax.ShapeDtypeStruct(s, jnp.int32)
    half = lambda *s: jax.ShapeDtypeStruct(s, BF)
    node, nodes, msg = (3 * ROWS, WIDE), (COMPONENTS * ROWS, WIDE), (8, MSG + TAIL)
    fields = [(9 * QP, WIDE), (QP, WIDE), (LD * LD, WIDE), (LD, WIDE)]
    send = [(16, HALF)] * 4
    zone = lambda count: (count, NPZ, WIDE)
    words = lambda groups: ints(2 * groups * ROWS, WIDE)
    *msgs, lists = call(
        pack_kernel, (send_rows, shared_nodes, jac, mass, inv, energy), [msg] * 4 + [ints(8, HALF)],
        [(40, WIDE)] + fields, [SM, VM] + [HB] * 4, limit=61, copies=7, us=4, name="pack",
    )
    rounds = ((1, 2), (0, 2), (1, 1), (0, 1))
    came = [lax.ppermute(m, AXES, paired(first, devices, hop)) for m, (first, hop) in zip(msgs, rounds)]
    vel, vz, lanes = call(
        prep_kernel, (velocity, zone_nodes, arrive_rows, energy, force_tables),
        [node, zone(3), half(NPZ, WIDE, WIDE)], [words(1)], [VM, VM, SM, VM, VM], name="prep",
    )
    jac, mass, inv, en, ehalf, y, *sends = call(
        first_kernel,
        (arrive_rows, *came, lists, jac, mass, inv, energy, zone_nodes, force_tables, vz, lanes),
        fields + [(LD, WIDE), ((COMPONENTS + 1) * ROWS, WIDE)] + send,
        [(48, WIDE), (48, MSG), zone(COMPONENTS + 1), (QP, WIDE), (2 * (COMPONENTS + 1) * ROWS, WIDE)],
        [SM] + [VM] * 13, name="force_one",
    )
    scratch = [zone(COMPONENTS), zone(COMPONENTS), words(COMPONENTS // 3), (2 * COMPONENTS * ROWS, WIDE)]
    tail = (lists, zone_nodes, lanes, mass, mass_tables)
    ib, r, d, y, *sends = call(
        start_kernel, (*exchange(sends), y, *tail), [(ROWS, WIDE), nodes, nodes, nodes] + send, scratch,
        name="mass_start",
    )
    a = d
    for step in range(SWEEPS - 1):
        r, d, a, y, *sends = call(
            functools.partial(sweep_kernel, step=step), (*exchange(sends), y, r, d, a, ib, *tail),
            [nodes] * 4 + send, scratch, name="mass_sweep",
        )
    energy_next, velocity_next = call(
        last_kernel,
        (*exchange(sends), y, r, d, a, ib, lists, zone_nodes, mass, jac, inv, en, ehalf, vel, force_tables),
        [(LD, WIDE), velocity.shape], [node, zone(3), (QP, WIDE), words(1)], name="force_two",
    )
    return velocity_next, energy_next


def solution(mesh):
    both = P(None, AXES)
    rows = P(AXES, None)
    return jax.shard_map(
        per_device,
        mesh=mesh,
        in_specs=(both, both, both, both, both, rows, rows, both, P(AXES, None, None)),
        out_specs=(both, both),
        check_vma=False,
    )
```

```python
import functools
import math

import jax
import jax.numpy as jnp
import numpy as np
from jax import lax
from jax.experimental import pallas as pl
from jax.experimental.pallas import tpu as pltpu
from jax.sharding import PartitionSpec as P

H1D, Q1D, L1D, SWEEPS = 4, 6, 3, 3
NPZ, QP, LD = 64, 216, 27
GAMMA_LESS = 0.4
STEP_SIZE = 0.25
THETA, DELTA = 0.575, 0.425
SIGMA = THETA / DELTA
AXES = ("curve", "split")
CAP = 9
COMPONENTS = 6
HALF = 128
WIDE = 256
ROWS = 32
AT_JAC, AT_MASS, AT_INV, AT_EN, AT_FLAG, MSG = 0, 2048, 2304, 3072, 3100, 3200
TAIL = 512
BF, F32 = jnp.bfloat16, jnp.float32
NT = (((1,), (1,)), ((), ()))
TN = (((0,), (0,)), ((), ()))


def line_tables():
    on_line = [-0.9324695142031521, -0.6612093864662645, -0.2386191860831909]
    on_line = on_line + [-v for v in reversed(on_line)]
    points = [0.5 * (v + 1.0) for v in on_line]
    lobatto = [0.5 * (v + 1.0) for v in [-1.0, -0.4472135954999579, 0.4472135954999579, 1.0]]
    value, slope, bern = np.zeros((Q1D, H1D)), np.zeros((Q1D, H1D)), np.zeros((Q1D, L1D))
    for i in range(H1D):
        others = [lobatto[j] for j in range(H1D) if j != i]
        scaling = np.prod([lobatto[i] - o for o in others])
        for q, t in enumerate(points):
            value[q, i] = np.prod([t - o for o in others]) / scaling
            slope[q, i] = sum(
                np.prod([t - others[n] for n in range(3) if n != m]) for m in range(3)
            ) / scaling
    for q, t in enumerate(points):
        for j in range(L1D):
            bern[q, j] = math.comb(2, j) * t**j * (1.0 - t) ** (2 - j)
    return [np.float32(t).astype(np.float64) for t in (value, slope, bern)]


def halves(table):
    high = table.astype(np.float32).astype(BF)
    low = (table - high.astype(np.float64)).astype(np.float32).astype(BF)
    return high, low


def beside(table):
    high, low = halves(table)
    return np.concatenate([high, high, low], 1)


def above(table):
    return np.concatenate(halves(table), 0)


def stacked(tables):
    places, blocks, at = {}, [], 0
    for name, table in tables.items():
        rows, columns = table.shape
        places[name] = (at, rows, columns)
        room = -(-rows // 16) * 16
        block = np.zeros((room, WIDE), BF)
        block[:rows, :columns] = table
        blocks.append(block)
        at += room
    return np.concatenate(blocks, 0), places


def constants():
    b, g, p = line_tables()
    kron = lambda x, y, z: np.kron(np.kron(x, y), z)
    bbb, ppp = kron(b, b, b), kron(p, p, p)
    grads = [kron(g, b, b), kron(b, g, b), kron(b, b, g)]
    r = np.abs(b).sum(1, keepdims=True)
    limit = kron(np.abs(b), np.abs(b), np.abs(b)) * kron(r, r, r)
    spread = np.kron(np.ones((LD, 1)), np.eye(LD)).astype(BF)
    collect = np.kron(np.eye(LD), np.ones((1, LD))).astype(BF)
    force = dict(
        bern_up_high=halves(ppp)[0],
        bern_up_low=halves(ppp)[1],
        bern_down_high=halves(ppp.T)[0],
        bern_down_low=halves(ppp.T)[1],
        spread=spread,
        limit=above(limit.T),
    )
    for k, t in enumerate(grads):
        force["up%d" % k] = beside(t)
        force["down%d" % k] = above(t.T)
    for k in range(0, LD * LD, 243):
        force["collect%d" % k] = collect[:, k : k + 243]
    return stacked(force), stacked(dict(up=beside(bbb), down=above(bbb.T)))


(FORCE_TABLES, FORCE_AT), (MASS_TABLES, MASS_AT) = constants()


def entry(ref, places, name):
    at, rows, columns = places[name]
    return ref[at : at + rows, :columns]


def split2(x):
    high = x.astype(BF)
    return high, (x - high.astype(F32)).astype(BF)


def dot(a, b, dims=None):
    if dims is None:
        return jnp.dot(a, b, preferred_element_type=F32)
    return lax.dot_general(a, b, dims, preferred_element_type=F32)


def up(table, x):
    high, low = split2(x)
    return dot(table, jnp.concatenate([high, low, high], 0))


def down(table, x):
    high, low = split2(x)
    half = table.shape[0] // 2
    both = dot(table, high)
    return both[:half] + both[half:] + dot(table[:half], low)


def pick(tables, chunk_of, lane_of, shape, kind=F32):
    acc = [jnp.zeros(shape, kind) for _ in tables]
    for k in range(62):
        here = chunk_of == k
        for c, row in enumerate(tables):
            got = jnp.take_along_axis(jnp.broadcast_to(row(k), shape), lane_of, axis=1)
            acc[c] = jnp.where(here, got, acc[c])
    return acc


def table_rows(ref, count):
    def row(c, k):
        return ref[c * ROWS + k // 2 : c * ROWS + k // 2 + 1, (k % 2) * HALF : (k % 2 + 1) * HALF]

    return [functools.partial(row, c) for c in range(count)]


def make_words(tab_ref, word_ref, groups):
    steps = []
    for g in range(groups):
        x = tab_ref[3 * g * ROWS : 3 * (g + 1) * ROWS, :]
        scale = jnp.maximum(jnp.max(jnp.abs(x), keepdims=True), 1e-30)
        steps.append(scale * 1e-6)
        q = jnp.round(x * (1000000.0 / scale)).astype(jnp.int32) + (1 << 20)
        at = 2 * g * ROWS
        word_ref[at : at + ROWS] = (q[:ROWS] << 11) | (q[2 * ROWS :] >> 10)
        word_ref[at + ROWS : at + 2 * ROWS] = (q[ROWS : 2 * ROWS] << 11) | (q[2 * ROWS :] & 1023)
    return steps


def gather_tile(idx_ref, word_ref, out_ref, steps, t, h):
    r0 = pl.multiple_of(t * 8, 8)
    lanes = slice(h * HALF, (h + 1) * HALF)
    idx = idx_ref[pl.ds(r0, 8), lanes]
    words = pick(table_rows(word_ref, 2 * len(steps)), idx >> 7, idx & 127, (8, HALF), jnp.int32)
    for g, step in enumerate(steps):
        w0, w1 = words[2 * g : 2 * g + 2]
        back = (
            lax.shift_right_logical(w0, 11),
            lax.shift_right_logical(w1, 11),
            ((w0 & 2047) << 10) | (w1 & 1023),
        )
        for c in range(3):
            out_ref[3 * g + c, pl.ds(r0, 8), lanes] = (back[c] - (1 << 20)).astype(F32) * step


def gather_zones(idx_ref, tab_ref, word_ref, out_ref, groups=1):
    steps = make_words(tab_ref, word_ref, groups)

    @pl.loop(0, 8)
    def _(t):
        for h in range(2):
            gather_tile(idx_ref, word_ref, out_ref, steps, t, h)


def spread_rows(idx, rows):
    here = lax.broadcasted_iota(jnp.int32, (ROWS, idx.shape[1]), 0) == (idx >> 8)
    parts = []
    for x in rows:
        high = x.astype(BF).astype(F32)
        for part in (high, x - high):
            parts.append(jnp.where(here, part, 0.0).astype(BF))
    return jnp.concatenate(parts, 0)


def scatter_tile(acc, idx, rows):
    lane = jnp.where(
        lax.broadcasted_iota(jnp.int32, (WIDE, WIDE), 0) == (idx & 255), 1.0, 0.0
    ).astype(BF)
    return acc + dot(spread_rows(idx, rows), lane, NT)


def joined(acc):
    acc = acc.reshape(acc.shape[0] // (2 * ROWS), 2, ROWS, WIDE)
    return (acc[:, 0] + acc[:, 1]).reshape(-1, WIDE)


def add_product(acc_ref, rows, hot, step):
    rows, hot = jnp.concatenate(rows, 1), jnp.concatenate(hot, 0)
    for p in range(0, acc_ref.shape[0], step):
        acc_ref[p : p + step, :] += dot(rows[p : p + step], hot)


def scatter_zones(idx_ref, lane_ref, term_ref, acc_ref, count):
    acc_ref[...] = jnp.zeros(acc_ref.shape, F32)

    @pl.loop(0, NPZ // 16)
    def _(t):
        r0 = pl.multiple_of(t * 16, 8)
        idx = idx_ref[pl.ds(r0, 16), :]
        terms = [term_ref[c, pl.ds(r0, 16), :] for c in range(count)]
        rows = [spread_rows(idx[a : a + 1], [x[a : a + 1] for x in terms]) for a in range(16)]
        add_product(acc_ref, rows, [lane_ref[r0 + a] for a in range(16)], 224)

    return joined(acc_ref[...])


def flat_row(ref, first):
    return jnp.concatenate([ref[first : first + 1, :], ref[first + 1 : first + 2, :]], 1)


def received(lists_ref, got_refs, count):
    acc = jnp.zeros((2 * ROWS * count, WIDE), F32)
    for k, got in enumerate(got_refs):
        acc = scatter_tile(acc, flat_row(lists_ref, 2 * k), [flat_row(got, 2 * c) for c in range(count)])
    return joined(acc)


def send_shared(lists_ref, tab_ref, send_refs, count):
    idx = lists_ref[...]
    got = pick(table_rows(tab_ref, count), idx >> 7, idx & 127, (8, HALF))
    for k, send in enumerate(send_refs):
        for c in range(count):
            send[2 * c : 2 * c + 2, :] = got[c][2 * k : 2 * k + 2]
        send[2 * count :, :] = jnp.zeros((16 - 2 * count, HALF), F32)


def pressure_at(en, mass, tables):
    get = functools.partial(entry, tables, FORCE_AT)
    eh, el = split2(en)
    e_q = dot(get("bern_up_high"), eh) + dot(get("bern_up_high"), el) + dot(get("bern_up_low"), eh)
    return GAMMA_LESS * e_q * mass


def force(pressure, jac_ref, tables, t_ref=None, at=0, v_ref=None, work_ref=None):
    get = functools.partial(entry, tables, FORCE_AT)
    for c in range(3):
        if v_ref is not None:
            high, low = split2(v_ref[c])
            vc = jnp.concatenate([high, low, high], 0)
        ws = [jac_ref[(3 * k + c) * QP : (3 * k + c + 1) * QP, :] * pressure for k in range(3)]
        if v_ref is not None:
            for k in range(3):
                work = ws[k] * dot(get("up%d" % k), vc)
                work_ref[...] = work if c == 0 and k == 0 else work_ref[...] + work
        if t_ref is not None:
            t_ref[at + c] = sum(down(get("down%d" % k), ws[k]) for k in range(3))
    if v_ref is None:
        return None
    wh, wl = split2(work_ref[...])
    high, low = get("bern_down_high"), get("bern_down_low")
    return -(dot(high, wh) + dot(high, wl) + dot(low, wh))


def energy_change(rhs_e, inv_ref, tables):
    get = functools.partial(entry, tables, FORCE_AT)
    rh, rl = split2(rhs_e)
    prod = inv_ref[...] * (dot(get("spread"), rh) + dot(get("spread"), rl))
    total = jnp.zeros((LD, WIDE), F32)
    for k in range(0, LD * LD, 243):
        for part in split2(prod[k : k + 243]):
            total = total + dot(get("collect%d" % k), part)
    return total


def nodes_in(vel_ref, tab_ref):
    for c in range(3):
        for r in range(31):
            tab_ref[c * ROWS + r : c * ROWS + r + 1, :] = vel_ref[c : c + 1, r * WIDE : (r + 1) * WIDE]
        tab_ref[c * ROWS + 31 : (c + 1) * ROWS, :] = jnp.zeros((1, WIDE), F32)


def fetch(pairs, sems):
    copies = [pltpu.make_async_copy(a, b, sems.at[i]) for i, (a, b) in enumerate(pairs)]
    for copy in copies:
        copy.start()
    return copies


def split_side():
    return lax.axis_index("split")


def sent_block(k):
    s = split_side()
    return (3 - s // 2, 2 + s // 2, 1 - s % 2, s % 2)[k]


def landing_block(k):
    s = split_side()
    return (2 + s // 2, 3 - s // 2, s % 2, 1 - s % 2)[k]


def pack_kernel(send_ref, shared_ref, jac_hbm, mass_hbm, inv_hbm, en_hbm, *refs):
    msgs, (lists, oh, jac_ref, mass_ref, inv_ref, en_ref, sems) = refs[:4], refs[4:]
    chunks = [(i, min(2 * WIDE, 9 * QP - i)) for i in range(0, 9 * QP, 2 * WIDE)]
    copies = fetch(
        ((mass_hbm, mass_ref), (en_hbm, en_ref))
        + tuple((jac_hbm.at[pl.ds(i, n), :], jac_ref.at[pl.ds(i, n), :]) for i, n in chunks)
        + ((inv_hbm, inv_ref),),
        sems,
    )
    lane = lax.broadcasted_iota(jnp.int32, (1, WIDE), 1)
    for k in range(4):
        first = sent_block(k) * CAP
        for j in range(CAP):
            at = k * 8 + j if j < 8 else 32 + k
            oh[at : at + 1, :] = jnp.where(lane == send_ref[0, first + j], 1.0, 0.0)
    oh[36:40, :] = jnp.zeros((4, WIDE), F32)
    hot = oh[...].astype(BF)
    odds = (lax.axis_index("curve") % 2, split_side() % 2)
    for k in range(4):
        other = k ^ 1
        row = jnp.where(odds[k // 2] == 1, shared_ref[0, other : other + 1, :], shared_ref[0, k : k + 1, :])
        lists[2 * k : 2 * k + 1, :] = row[:, :HALF]
        lists[2 * k + 1 : 2 * k + 2, :] = row[:, HALF:]

    def put(at, n, block):
        for p in range(4):
            msgs[p][:, at : at + n] = block[p * 8 : (p + 1) * 8]
            done = 0
            while done < n:
                piece, off = divmod(at + done, TAIL)
                step = min(n - done, TAIL - off)
                msgs[p][piece : piece + 1, MSG + off : MSG + off + step] = block[
                    32 + p : 33 + p, done : done + step
                ]
                done += step

    places = [(mass_ref, AT_MASS, 0, QP), (en_ref, AT_EN, 0, LD)]
    places += [(jac_ref, AT_JAC, i, n) for i, n in chunks] + [(inv_ref, AT_INV, 0, LD * LD)]
    for copy, (ref, at, first, total) in zip(copies, places):
        copy.wait()
        for i in range(first, first + total, WIDE):
            n = min(WIDE, first + total - i)
            parts = split2(ref[i : i + n, :])
            put(at + i, n, sum(dot(hot, part, NT) for part in parts))
    for p in range(4):
        msgs[p][:, AT_FLAG:MSG] = jnp.ones((8, MSG - AT_FLAG), F32)


def prep_kernel(vel_ref, zn_ref, _arrive, _en, _tables, vel_out, vz, lane_out, words):
    nodes_in(vel_ref, vel_out)
    steps = make_words(vel_out, words, 1)
    down_rows = lax.broadcasted_iota(jnp.int32, (WIDE, WIDE), 0)
    eye = jnp.where(down_rows == lax.broadcasted_iota(jnp.int32, (WIDE, WIDE), 1), 1.0, 0.0).astype(BF)

    @pl.loop(0, 8)
    def _(t):
        r0 = pl.multiple_of(t * 8, 8)
        lane = zn_ref[pl.ds(r0, 8), :] & 255
        for a in range(8):
            hot = jnp.where(down_rows == lane[a : a + 1], 1.0, 0.0).astype(BF)
            lane_out[r0 + a] = dot(eye, hot, NT).astype(BF)
        for h in range(2):
            gather_tile(zn_ref, words, vz, steps, t, h)


def first_kernel(
    arrive_ref, m0, m1, m2, m3, lists_ref, jac_ref, mass_ref, inv_ref, en_ref, zn_ref, tables, vz, lanes,
    jac_out, mass_out, inv_out, en_out, ehalf_out, y_out, s0, s1, s2, s3, oh, arr, terms, work, acc,
):
    msgs = (m0, m1, m2, m3)
    lane = lax.broadcasted_iota(jnp.int32, (1, WIDE), 1)
    oh[...] = jnp.zeros(oh.shape, F32)
    for k in range(4):
        first = landing_block(k) * CAP
        flag = msgs[k][0:1, AT_FLAG : AT_FLAG + 1]
        for j in range(CAP):
            at = k * 8 + j if j < 8 else 32 + k
            oh[at : at + 1, :] = jnp.where(lane == arrive_ref[0, first + j], 1.0, 0.0) * flag
    lands = jnp.sum(oh[...], axis=0, keepdims=True) > 0.5
    hot = oh[...].astype(BF)
    hot2 = jnp.concatenate([hot, hot], 0)
    for p in range(4):
        arr[p * 8 : (p + 1) * 8, :] = msgs[p][:, :MSG]
        for piece in range(7):
            n = min(TAIL, MSG - piece * TAIL)
            arr[32 + p : 33 + p, piece * TAIL : piece * TAIL + n] = msgs[p][
                piece : piece + 1, MSG : MSG + n
            ]
    arr[36:48, :] = jnp.zeros((12, MSG), F32)
    for ref, out, at in (
        (jac_ref, jac_out, AT_JAC), (mass_ref, mass_out, AT_MASS),
        (inv_ref, inv_out, AT_INV), (en_ref, en_out, AT_EN),
    ):
        total = ref.shape[0]
        for i in range(0, total, WIDE):
            n = min(WIDE, total - i)
            wide = min(WIDE, -(-n // HALF) * HALF)
            came = jnp.concatenate(split2(arr[:, at + i : at + i + wide]), 0)
            out[i : i + n, :] = jnp.where(lands, dot(came, hot2, TN)[:n], ref[i : i + n, :])
    mass = mass_out[...]
    rhs_e = force(pressure_at(en_out[...], mass, tables), jac_out, tables, terms, 0, vz, work)
    ehalf_out[...] = en_out[...] + 0.5 * STEP_SIZE * energy_change(rhs_e, inv_out, tables)
    force(pressure_at(ehalf_out[...], mass, tables), jac_out, tables, terms, 3)
    terms[6] = down(entry(tables, FORCE_AT, "limit"), mass)
    y_out[...] = scatter_zones(zn_ref, lanes, terms, acc, 7)
    send_shared(lists_ref, y_out, (s0, s1, s2, s3), 7)


def rhos():
    rho, out = 1.0 / SIGMA, []
    for _ in range(SWEEPS):
        new = 1.0 / (2.0 * SIGMA - rho)
        out.append((new * rho, 2.0 * new / DELTA))
        rho = new
    return out


def each(x):
    return jnp.concatenate([x] * COMPONENTS, 0)


def update(y, r_ref, d_ref, a_ref, ib_ref, step):
    keep, add = rhos()[step]
    r = r_ref[...] - y
    d = keep * d_ref[...] + add * (r * each(ib_ref[...]))
    return r, d, a_ref[...] + d


def scatter_half(idx_ref, lane_ref, term_ref, acc_ref, t, h):
    r0 = pl.multiple_of(t * 16, 16)
    lanes = slice(h * HALF, (h + 1) * HALF)
    idx = idx_ref[pl.ds(r0, 16), lanes]
    terms = [term_ref[c, pl.ds(r0, 16), lanes] for c in range(COMPONENTS)]
    rows = [spread_rows(idx[a : a + 1], [x[a : a + 1] for x in terms]) for a in range(16)]
    hot = [lane_ref[r0 + a, lanes, :] for a in range(16)]
    add_product(acc_ref, rows, hot, 192)


def zone_mass(mass_ref, tables, zone, terms, h):
    lanes = slice(h * HALF, (h + 1) * HALF)
    mass = jnp.concatenate([mass_ref[:, lanes]] * 2, 1)
    pairs = range(0, COMPONENTS, 2)
    xs = [jnp.concatenate([zone[c, :, lanes], zone[c + 1, :, lanes]], 1) for c in pairs]
    at_points = [up(entry(tables, MASS_AT, "up"), x) * mass for x in xs]
    outs = [down(entry(tables, MASS_AT, "down"), x) for x in at_points]
    for c, out in zip(pairs, outs):
        terms[c, :, lanes] = out[:, :HALF]
        terms[c + 1, :, lanes] = out[:, HALF:]


def apply_mass(zn_ref, lanes, mass_ref, tables, d_ref, y_out, zone, terms, words, acc):
    steps = make_words(d_ref, words, COMPONENTS // 3)
    acc[...] = jnp.zeros(acc.shape, F32)

    @pl.loop(0, 4)
    def _(t):
        gather_tile(zn_ref, words, zone, steps, 2 * t, 0)
        gather_tile(zn_ref, words, zone, steps, 2 * t + 1, 0)

    zone_mass(mass_ref, tables, zone, terms, 0)

    @pl.loop(0, 4)
    def _(t):
        scatter_half(zn_ref, lanes, terms, acc, t, 0)
        gather_tile(zn_ref, words, zone, steps, 2 * t, 1)
        gather_tile(zn_ref, words, zone, steps, 2 * t + 1, 1)

    zone_mass(mass_ref, tables, zone, terms, 1)

    @pl.loop(0, 4)
    def _(t):
        scatter_half(zn_ref, lanes, terms, acc, t, 1)

    y_out[...] = joined(acc[...])


def start_kernel(
    g0, g1, g2, g3, y_ref, lists, zn, lanes, mass, tables, ib, r_out, d_out, y_out, s0, s1, s2, s3, *scratch
):
    y = y_ref[...] + received(lists, (g0, g1, g2, g3), COMPONENTS + 1)
    pad = lax.broadcasted_iota(jnp.int32, (ROWS, WIDE), 0) == 31
    inv_bound = 1.0 / jnp.where(pad, 1.0, y[COMPONENTS * ROWS :])
    ib[...] = inv_bound
    r = y[: COMPONENTS * ROWS]
    r_out[...] = r
    d_out[...] = r * each(inv_bound) * (1.0 / THETA)
    apply_mass(zn, lanes, mass, tables, d_out, y_out, *scratch)
    send_shared(lists, y_out, (s0, s1, s2, s3), COMPONENTS)


def sweep_kernel(
    g0, g1, g2, g3, y_ref, r_ref, d_ref, a_ref, ib_ref, lists, zn, lanes, mass, tables,
    r_out, d_out, a_out, y_out, s0, s1, s2, s3, *scratch, step,
):
    y = y_ref[...] + received(lists, (g0, g1, g2, g3), COMPONENTS)
    r, d, a = update(y, r_ref, d_ref, a_ref, ib_ref, step)
    r_out[...] = r
    d_out[...] = d
    a_out[...] = a
    apply_mass(zn, lanes, mass, tables, d_out, y_out, *scratch)
    send_shared(lists, y_out, (s0, s1, s2, s3), COMPONENTS)


def last_kernel(
    g0, g1, g2, g3, y_ref, r_ref, d_ref, a_ref, ib_ref, lists, zn, mass, jac, inv, en, ehalf, vel, tables,
    en_out, vel_out, vhalf, vz, work, words,
):
    y = y_ref[...] + received(lists, (g0, g1, g2, g3), COMPONENTS)
    _, _, a = update(y, r_ref, d_ref, a_ref, ib_ref, SWEEPS - 1)
    vhalf[...] = vel[...] + 0.5 * STEP_SIZE * a[: 3 * ROWS]
    v = vel[...] + STEP_SIZE * a[3 * ROWS :]
    for c in range(3):
        for r in range(31):
            vel_out[c : c + 1, r * WIDE : (r + 1) * WIDE] = v[c * ROWS + r : c * ROWS + r + 1]
    gather_zones(zn, vhalf, words, vz)
    pressure = pressure_at(ehalf[...], mass[...], tables)
    rhs_e = force(pressure, jac, tables, v_ref=vz, work_ref=work)
    en_out[...] = en[...] + STEP_SIZE * energy_change(rhs_e, inv, tables)


VM = pl.BlockSpec(memory_space=pltpu.VMEM)
SM = pl.BlockSpec(memory_space=pltpu.SMEM)
HB = pl.BlockSpec(memory_space=pltpu.HBM)


def shape_of(s):
    return s if isinstance(s, jax.ShapeDtypeStruct) else jax.ShapeDtypeStruct(s, F32)


def call(kernel, args, outs, scratch=(), specs=None, limit=16, copies=0, us=10, name=None):
    scratch = [pltpu.VMEM(shape_of(s).shape, shape_of(s).dtype) for s in scratch]
    return pl.pallas_call(
        kernel,
        out_shape=[shape_of(s) for s in outs],
        in_specs=specs or [VM] * len(args),
        out_specs=[VM] * len(outs),
        scratch_shapes=scratch + ([pltpu.SemaphoreType.DMA((copies,))] if copies else []),
        compiler_params=pltpu.CompilerParams(vmem_limit_bytes=limit * 1024 * 1024),
        cost_estimate=pl.CostEstimate(flops=us * 10**9, bytes_accessed=us * 10**5, transcendentals=0),
        name=name,
    )(*args)


def paired(first, size, hop=1):
    low = [i for i in range(size - hop) if (i // hop) % 2 == first]
    return [p for i in low for p in ((i, i + hop), (i + hop, i))]


def exchange(sends):
    n_curve, n_split = lax.axis_size("curve"), lax.axis_size("split")
    return [
        lax.ppermute(sends[0], "curve", paired(0, n_curve)),
        lax.ppermute(sends[1], "curve", paired(1, n_curve)),
        lax.ppermute(sends[2], "split", paired(0, n_split)),
        lax.ppermute(sends[3], "split", paired(1, n_split)),
    ]


def per_device(velocity, energy, mass, jac, inv, send_rows, arrive_rows, zone_nodes, shared_nodes):
    force_tables, mass_tables = jnp.asarray(FORCE_TABLES), jnp.asarray(MASS_TABLES)
    devices = lax.axis_size("curve") * lax.axis_size("split")
    ints = lambda *s: jax.ShapeDtypeStruct(s, jnp.int32)
    half = lambda *s: jax.ShapeDtypeStruct(s, BF)
    node, nodes, msg = (3 * ROWS, WIDE), (COMPONENTS * ROWS, WIDE), (8, MSG + TAIL)
    fields = [(9 * QP, WIDE), (QP, WIDE), (LD * LD, WIDE), (LD, WIDE)]
    send = [(16, HALF)] * 4
    zone = lambda count: (count, NPZ, WIDE)
    words = lambda groups: ints(2 * groups * ROWS, WIDE)
    *msgs, lists = call(
        pack_kernel, (send_rows, shared_nodes, jac, mass, inv, energy), [msg] * 4 + [ints(8, HALF)],
        [(40, WIDE)] + fields, [SM, VM] + [HB] * 4, limit=61, copies=7, us=4, name="pack",
    )
    rounds = ((1, 2), (0, 2), (1, 1), (0, 1))
    came = [lax.ppermute(m, AXES, paired(first, devices, hop)) for m, (first, hop) in zip(msgs, rounds)]
    vel, vz, lanes = call(
        prep_kernel, (velocity, zone_nodes, arrive_rows, energy, force_tables),
        [node, zone(3), half(NPZ, WIDE, WIDE)], [words(1)], [VM, VM, SM, VM, VM], name="prep",
    )
    jac, mass, inv, en, ehalf, y, *sends = call(
        first_kernel,
        (arrive_rows, *came, lists, jac, mass, inv, energy, zone_nodes, force_tables, vz, lanes),
        fields + [(LD, WIDE), ((COMPONENTS + 1) * ROWS, WIDE)] + send,
        [(48, WIDE), (48, MSG), zone(COMPONENTS + 1), (QP, WIDE), (2 * (COMPONENTS + 1) * ROWS, WIDE)],
        [SM] + [VM] * 13, name="force_one",
    )
    scratch = [zone(COMPONENTS), zone(COMPONENTS), words(COMPONENTS // 3), (2 * COMPONENTS * ROWS, WIDE)]
    tail = (lists, zone_nodes, lanes, mass, mass_tables)
    ib, r, d, y, *sends = call(
        start_kernel, (*exchange(sends), y, *tail), [(ROWS, WIDE), nodes, nodes, nodes] + send, scratch,
        name="mass_start",
    )
    a = d
    for step in range(SWEEPS - 1):
        r, d, a, y, *sends = call(
            functools.partial(sweep_kernel, step=step), (*exchange(sends), y, r, d, a, ib, *tail),
            [nodes] * 4 + send, scratch, name="mass_sweep",
        )
    energy_next, velocity_next = call(
        last_kernel,
        (*exchange(sends), y, r, d, a, ib, lists, zone_nodes, mass, jac, inv, en, ehalf, vel, force_tables),
        [(LD, WIDE), velocity.shape], [node, zone(3), (QP, WIDE), words(1)], name="force_two",
    )
    return velocity_next, energy_next


def solution(mesh):
    both = P(None, AXES)
    rows = P(AXES, None)
    return jax.shard_map(
        per_device,
        mesh=mesh,
        in_specs=(both, both, both, both, both, rows, rows, both, P(AXES, None, None)),
        out_specs=(both, both),
        check_vma=False,
    )
```
